128 devices in a mesh: pop: 32 (over y, x_lo, z), mp: 4 (over x_hi, core).
Axes of the slice: x: 4 (x_hi: 2, x_lo: 2; x = x_hi * 2 + x_lo), y: 4, z: 4, core: 2. Of those that a mesh axis runs over, the one named last changes fastest.
Arguments:
- token_ids: int32 [384, 4, 16], P('pop'), may hold values from 0 to 255
- fitness_ranks: int32 [384], P('pop'), may hold values from 0 to 575, as said below
- embedding: bfloat16 [256, 4096], P(None, 'mp'), may hold values from -6 to 6
- mix_weights: bfloat16 [2, 4096, 4096], P(None, 'mp'), may hold values from -0.09375 to 0.09375
- factors_in: bfloat16 [2, 384, 4, 4096], P(None, 'pop', None, 'mp'), may hold values from -6 to 6
- factors_out: bfloat16 [2, 384, 4, 4096], P(None, 'pop'), may hold values from -6 to 6
- decay_rates: float32 [2, 4096], P(None, 'mp'), may hold values from 0.2 to 0.98
- norm_gain: float32 [2, 4096], P(None, 'mp'), may hold values from 0.1 to 1.9
- reward_dir: float32 [4096], P('mp'), may hold values from -6 to 6
Outputs:
- final_features: bfloat16 [384, 4, 4096], P('pop', None, 'mp')
- scores: float32 [384, 4], P('pop')
- weight_step: float32 [2, 4096, 4096], P(None, 'mp', 'pop')
The draws below stay inside these ranges and needn't reach their ends.
Inputs may be any that keep to these rules, and one draw needn't show every extreme that they name: `fitness_ranks`: ranks may repeat.
All inputs are finite; a program needn't handle non-finite values.
Results may differ from the reference program's by a relative error of at most 0.023.
Values may be sent and summed in bfloat16 or wider, within the bound.
No kernel may reach another device: no remote copies, remote signals or barrier semaphores. Data moves between devices by JAX's collectives and lax.ppermute only.
A program may use at most 128 MiB of HBM per device.

```python
import jax
import jax.numpy as jnp
from jax import lax

D = 4096
VOCAB = 256
RANK = 4
LAYERS = 2
STEPS = 16
SEQS = 4
MEMBERS = 384
N_MP = 4


def draw_fitness_ranks(key, part):
    member_idx = jnp.arange(MEMBERS, dtype=jnp.int32)
    upper = MEMBERS // 2 + member_idx + 1
    drawn = jax.random.randint(jax.random.fold_in(key, 11), (MEMBERS,), 0, upper, dtype=jnp.int32)
    drawn = drawn.at[MEMBERS - 1].set(MEMBERS + MEMBERS // 2 - 1)
    drawn = drawn.at[0].set(0)
    return drawn


def place_ends(array, rng, smallest, high):
    dims = array.shape
    index_at = [jax.random.randint(jax.random.fold_in(rng, axis), (), 0, dims[axis]) for axis in range(len(dims))]
    array = array.at[tuple(index_at)].set(smallest)
    longest = dims.index(max(dims))
    index_at[longest] = (index_at[longest] + 1) % dims[longest]
    return array.at[tuple(index_at)].set(high)


def block_levels(stream_key, dims, pieces, smallest, top_value):
    gain, own = 1.0, jax.random.fold_in(stream_key, 6)
    for axis_at, blocks in pieces:
        heights = jnp.exp(jax.random.uniform(jax.random.fold_in(own, axis_at), (blocks,), jnp.float32, smallest / len(pieces), top_value / len(pieces)))
        gain = gain * jnp.repeat(heights, dims[axis_at] // blocks).reshape([-1 if axis == axis_at else 1 for axis in range(len(dims))])
    return gain


def centred(own_key, extent, spread, reach, shards=(), kind=jnp.bfloat16):
    level = block_levels(own_key, extent, shards, -0.22, 0.18) if shards else 1.0
    entries = jax.random.normal(own_key, extent, jnp.float32) * spread * level
    return jnp.minimum(jnp.maximum(entries, -reach), reach).astype(kind)


def setup_inputs(seed: int = 0) -> dict:
    seeds = jax.random.split(jax.random.key(seed), 10)
    token_ids = place_ends(jax.random.randint(seeds[0], (MEMBERS, SEQS, STEPS), 0, VOCAB), jax.random.fold_in(seeds[0], 1), 0, VOCAB - 1).astype(jnp.int32)
    fitness_ranks = draw_fitness_ranks(jax.random.fold_in(seeds[9], 71), 0)
    embedding = centred(seeds[2], (VOCAB, D), 1.0, 6.0, ((1, 4),))
    mix_weights = centred(seeds[3], (LAYERS, D, D), D ** -0.5, 0.09375, ((1, 4),))
    factors_in = centred(seeds[4], (LAYERS, MEMBERS, RANK, D), 1.0, 6.0, ((1, 32), (3, 4)))
    factors_out = centred(seeds[5], (LAYERS, MEMBERS, RANK, D), 1.0, 6.0, ((1, 32),))
    decay_rates = jnp.clip(0.2 + 0.78000002 * jax.random.uniform(seeds[6], (LAYERS, D), jnp.float32) ** block_levels(seeds[6], (LAYERS, D), ((1, 4),), -0.2, 0.2), 0.2, 0.98)
    norm_gain = jnp.clip(1.0 + 0.18 * jax.random.normal(seeds[7], (LAYERS, D), jnp.float32), 0.1, 1.9)
    reward_dir = centred(seeds[8], (D,), 1.0, 6.0, ((0, 4),), jnp.float32)
    return dict(token_ids=token_ids, fitness_ranks=fitness_ranks, embedding=embedding, mix_weights=mix_weights, factors_in=factors_in, factors_out=factors_out, decay_rates=decay_rates, norm_gain=norm_gain, reward_dir=reward_dir)


noise_scale = 0.25
norm_eps = 1e-06
spread_eps = 1e-05

def recurrence(inputs, decay):
    time_major = jnp.moveaxis(inputs, 2, 0)

    def advance(carried, column):
        carried = decay * carried + (1.0 - decay) * column
        return (carried, carried)
    initial = jnp.zeros(time_major.shape[1:], jnp.float32)
    _, states = lax.scan(advance, initial, time_major)
    return jnp.moveaxis(states, 0, 2)

def reference(token_ids, fitness_ranks, embedding, mix_weights, factors_in, factors_out, decay_rates, norm_gain, reward_dir):
    block_width = D // N_MP
    coef = noise_scale * (D * RANK) ** (-0.5)
    hidden = jnp.take(embedding, token_ids, axis=0)
    shape_full = hidden.shape
    for layer_idx in range(LAYERS):
        base_mix = jnp.zeros((MEMBERS * SEQS * STEPS, D), jnp.float32)
        for shard_idx in range(N_MP):
            portion = hidden[..., shard_idx * block_width:(shard_idx + 1) * block_width].reshape(-1, block_width)
            rows_w = mix_weights[layer_idx, shard_idx * block_width:(shard_idx + 1) * block_width, :]
            partial_value = jnp.dot(portion, rows_w, preferred_element_type=jnp.float32).astype(jnp.bfloat16)
            partial_value = lax.optimization_barrier(partial_value)
            base_mix = base_mix + partial_value.astype(jnp.float32)
        base_mix = base_mix.reshape(shape_full)
        low_rank = jnp.einsum('mstd,mrd->mstr', hidden.astype(jnp.float32), factors_in[layer_idx].astype(jnp.float32))
        correction = jnp.einsum('mstr,mrd->mstd', low_rank, factors_out[layer_idx].astype(jnp.float32), precision=lax.Precision.HIGHEST)
        mixed = base_mix + coef * correction
        states = recurrence(mixed, decay_rates[layer_idx])
        mean_sq = lax.optimization_barrier(jnp.mean(states * states, axis=3, keepdims=True))
        norm_scale = lax.rsqrt(mean_sq + norm_eps)
        hidden = (hidden.astype(jnp.float32) + states * norm_scale * norm_gain[layer_idx]).astype(jnp.bfloat16)
    final_features = hidden[:, :, STEPS - 1, :]
    dots = jnp.einsum('mstd,d->mst', hidden.astype(jnp.float32), reward_dir, precision=lax.Precision.HIGHEST)
    scores = lax.optimization_barrier(jnp.mean(dots, axis=2)) * D ** (-0.5)
    shares = fitness_ranks.astype(jnp.float32) / MEMBERS
    rank_mean = jnp.mean(shares)
    rank_spread = jnp.mean((shares - rank_mean) * (shares - rank_mean)) + spread_eps
    shaped = (shares - rank_mean) * lax.rsqrt(rank_spread)
    deltas = []
    for layer_idx in range(LAYERS):
        weighted = (factors_in[layer_idx].astype(jnp.float32) * shaped[:, None, None]).astype(jnp.bfloat16)
        outer = factors_out[layer_idx]
        delta = jnp.dot(weighted.reshape(-1, D).T, outer.reshape(-1, D), preferred_element_type=jnp.float32)
        deltas.append(delta * (MEMBERS * RANK) ** (-0.5))
    weight_step = jnp.stack(deltas, axis=0)
    return (final_features, scores, weight_step)
```

```python
import jax
import jax.numpy as jnp
from jax import lax
from jax.experimental import pallas as pl
from jax.experimental.pallas import tpu as pltpu
from jax.sharding import Mesh
from jax.sharding import PartitionSpec as P

noise_scale = 0.25
norm_eps = 1e-06
spread_eps = 1e-05

POP = ("y", "xl", "z")
MP = ("xh", "c")
CHUNKS = 3
f32 = jnp.float32
bf16 = jnp.bfloat16
SMEM = pl.BlockSpec(memory_space=pltpu.SMEM)
VMEM = pl.BlockSpec(memory_space=pltpu.VMEM)


def params(mib=48):
    return pltpu.CompilerParams(vmem_limit_bytes=mib * 1024 * 1024)


def swap(value, axis):
    return lax.ppermute(value, axis, [(0, 1), (1, 0)])


def shift(value, axis, by):
    n = lax.axis_size(axis)
    return lax.ppermute(value, axis, [(i, (i + by) % n) for i in range(n)])


def mp_parts(value):
    both = lax.ppermute(value, MP, [(i, 3 - i) for i in range(4)])
    return value, swap(value, "c"), swap(value, "xh"), both


def dot(a, b, ca, cb, precision=None):
    return lax.dot_general(
        a, b, (((ca,), (cb,)), ((), ())), preferred_element_type=f32, precision=precision
    )


def regroup(factors, first, second):
    layers, members, ranks, width = factors.shape
    blocks = width // 128

    def kernel(in_ref, out_ref):
        for m in range(members):
            rows = jnp.concatenate(
                [in_ref[l, m].astype(f32) for l in range(layers)], axis=0
            ).astype(bf16)
            lo = m * layers * ranks
            for b in range(blocks):
                out_ref[b, lo : lo + layers * ranks, :] = rows[:, b * 128 : (b + 1) * 128]

    return pl.pallas_call(
        kernel,
        out_shape=jax.ShapeDtypeStruct((blocks, members * layers * ranks, 128), bf16),
        in_specs=[VMEM],
        out_specs=VMEM,
        compiler_params=params(),
        name=first,
    )(factors)


def table_partial(layer, where, embedding, weights):
    vocab, width = embedding.shape
    full = weights.shape[2]
    piece = full // 16

    def kernel(where_ref, e_ref, wp_ref, wo_ref, peer_ref, own_ref):
        peer_ref[0] = jnp.dot(e_ref[...], wp_ref[0], preferred_element_type=f32).astype(bf16)
        own_ref[0] = jnp.dot(e_ref[...], wo_ref[0], preferred_element_type=f32).astype(bf16)

    def block(rel, where_ref, flip):
        z, xh, c = where_ref[0], where_ref[1], where_ref[2]
        owner = (xh ^ rel) * 2 + (c ^ flip)
        return owner * 4 + z

    return pl.pallas_call(
        kernel,
        grid_spec=pltpu.PrefetchScalarGridSpec(
            num_scalar_prefetch=1,
            grid=(2,),
            in_specs=[
                pl.BlockSpec((vocab, width), lambda r, s: (0, 0)),
                pl.BlockSpec((1, width, piece), lambda r, s: (layer, 0, block(r, s, 1))),
                pl.BlockSpec((1, width, piece), lambda r, s: (layer, 0, block(r, s, 0))),
            ],
            out_specs=[pl.BlockSpec((1, vocab, piece), lambda r, s: (r, 0, 0))] * 2,
        ),
        out_shape=[jax.ShapeDtypeStruct((2, vocab, piece), bf16)] * 2,
        compiler_params=params(),
        name="table",
        cost_estimate=pl.CostEstimate(
            flops=2 * vocab * width * piece * 4, bytes_accessed=width * piece * 8, transcendentals=0
        ),
    )(where, embedding, weights, weights)


def member_of(shape, per, dim):
    return lax.broadcasted_iota(jnp.int32, shape, dim) // per


def low_kernel(onehot, embedding, factors):
    rows = onehot.shape[0]
    per_chunk = rows // CHUNKS
    group = factors.shape[1] // CHUNKS

    def kernel(o_ref, e_ref, a_ref, out_ref):
        for k in range(CHUNKS):
            x = jnp.dot(
                o_ref[k * per_chunk : (k + 1) * per_chunk, :], e_ref[...], preferred_element_type=f32
            ).astype(bf16)
            total = jnp.zeros((group, per_chunk), f32)
            for b in range(factors.shape[0]):
                total += dot(
                    a_ref[b, k * group : (k + 1) * group, :], x[:, b * 128 : (b + 1) * 128], 1, 1
                )
            out_ref[:, k * per_chunk : (k + 1) * per_chunk] = diagonal(total)

    return pl.pallas_call(
        kernel,
        out_shape=jax.ShapeDtypeStruct((8, rows), f32),
        in_specs=[VMEM] * 3,
        out_specs=VMEM,
        compiler_params=params(),
        name="low",
    )(onehot, embedding, factors)


def diagonal(total):
    group, cols = total.shape
    row_member = member_of((group, cols), 8, 0)
    col_member = (lax.broadcasted_iota(jnp.int32, (group, cols), 1) % 16) // 4
    kept = jnp.where(row_member == col_member, total, 0.0)
    out = kept[0:8]
    for m in range(1, group // 8):
        out = out + kept[m * 8 : (m + 1) * 8]
    return out


def spread(low, layer, group):
    cols = low.shape[1]
    row = lax.broadcasted_iota(jnp.int32, (group, cols), 0)
    col_member = (lax.broadcasted_iota(jnp.int32, (group, cols), 1) % 16) // 4
    keep = (row // 8 == col_member) & ((row % 8) // 4 == layer)
    tiled = jnp.concatenate([low] * (group // 8), axis=0)
    return jnp.where(keep, tiled, 0.0).astype(bf16)


def first_layer(chunk, where, coef, onehot, tables, lows, out_factors, in_factors, decay, gain):
    rows = onehot.shape[0] // CHUNKS
    group = out_factors.shape[1] // CHUNKS
    width = decay.shape[1]
    steps = 16
    per = rows // steps

    def kernel(where_ref, o_ref, t0, t1, t2, t3, l0, l1, l2, l3, b_ref, a_ref, d_ref, g_ref,
               lifted_ref, stats_ref, square):
        z = where_ref[0]
        low = (l0[...] + l1[...] + l2[...] + l3[...]) * coef
        spread_low = spread(low, 0, group)
        square[...] = jnp.zeros_like(square)
        total = jnp.zeros((group, rows), f32)
        for k, table in enumerate((t0, t1, t2, t3)):
            blk = (z - k + 4) % 4
            cols = pl.ds(pl.multiple_of(blk * 256, 256), 256)
            factor = jnp.concatenate([b_ref[2 * blk], b_ref[2 * blk + 1]], axis=1)
            u = jnp.dot(o_ref[...], table[...], preferred_element_type=f32) + dot(
                spread_low, factor, 0, 0
            )
            d = d_ref[:, cols]
            g = g_ref[:, cols]
            rest = 1.0 - d
            h = jnp.zeros((per, 256), f32)
            for t in range(steps):
                span = slice(t * per, (t + 1) * per)
                h = d * h + rest * u[span]
                lifted_ref[span, cols] = (h * g).astype(bf16)
                hh = h * h
                square[span] += hh[:, :128] + hh[:, 128:]
            factor_in = jnp.concatenate([a_ref[2 * blk], a_ref[2 * blk + 1]], axis=1)
            total += dot(factor_in, lifted_ref[:, cols], 1, 1)
        sums = dot(jnp.ones((8, 128), f32), square[...], 1, 1, lax.Precision.HIGHEST)
        low_next = diagonal(total)
        row = lax.broadcasted_iota(jnp.int32, (8, rows), 0)
        stats_ref[...] = jnp.where(row < 4, sums, low_next)

    sl = lambda a, n: lax.slice_in_dim(a, chunk * n, (chunk + 1) * n, axis=0)
    lc = [lax.slice_in_dim(a, chunk * rows, (chunk + 1) * rows, axis=1) for a in lows]
    mid = lambda a: lax.slice_in_dim(a, chunk * group, (chunk + 1) * group, axis=1)
    return pl.pallas_call(
        kernel,
        out_shape=[
            jax.ShapeDtypeStruct((rows, width), bf16),
            jax.ShapeDtypeStruct((8, rows), f32),
        ],
        in_specs=[SMEM] + [VMEM] * 13,
        out_specs=[VMEM, VMEM],
        scratch_shapes=[pltpu.VMEM((rows, 128), f32)],
        compiler_params=params(),
        name="first_layer",
        cost_estimate=pl.CostEstimate(flops=2000000000, bytes_accessed=4000000, transcendentals=0),
    )(where, sl(onehot, rows), *tables, *lc, mid(out_factors), mid(in_factors), decay, gain)


def product(where, rel, lifted, lifted_peer, weights, weights_peer, out_dtype):
    rows, width = lifted.shape
    blocks = 4
    piece = width // blocks

    def kernel(where_ref, a_ref, b_ref, wa_ref, wb_ref, out_ref):
        out_ref[...] = (
            jnp.dot(a_ref[...], wa_ref[0], preferred_element_type=f32)
            + jnp.dot(b_ref[...], wb_ref[0], preferred_element_type=f32)
        ).astype(out_dtype)

    return pl.pallas_call(
        kernel,
        grid_spec=pltpu.PrefetchScalarGridSpec(
            num_scalar_prefetch=1,
            grid=(blocks,),
            in_specs=[
                pl.BlockSpec((rows, width), lambda n, s: (0, 0)),
                pl.BlockSpec((rows, width), lambda n, s: (0, 0)),
                pl.BlockSpec(
                    (1, width, piece),
                    lambda n, s: (1, 0, ((s[1] ^ rel) * 2 + s[2]) * blocks + n),
                ),
                pl.BlockSpec((1, width, piece), lambda n, s: (rel, 0, n)),
            ],
            out_specs=pl.BlockSpec((rows, piece), lambda n, s: (0, n)),
        ),
        out_shape=jax.ShapeDtypeStruct((rows, width), out_dtype),
        compiler_params=params(),
        name="product",
        cost_estimate=pl.CostEstimate(
            flops=4 * rows * width * width, bytes_accessed=6 * width * width, transcendentals=0
        ),
    )(where, lifted, lifted_peer, weights, weights_peer)


def second_layer(chunk, where, coef, full_width, onehot, embedding, tables, lows, stats, lifted,
                 own, other, out_factors, decay, gain, reward):
    rows = lifted.shape[0]
    group = out_factors.shape[1] // CHUNKS
    width = decay.shape[1]
    steps = 16
    per = rows // steps

    def kernel(where_ref, o_ref, e_ref, t0, t1, t2, t3, l0, l1, l2, l3, s0, s1, s2, s3, lifted_ref,
               own_ref, other_ref, b_ref, d_ref, g_ref, r_ref,
               stats_ref, hidden_ref, last_ref, square, lr, xr):
        z = where_ref[0]
        from_hidden = l0[...] + l1[...] + l2[...] + l3[...]
        so_far = s0[...] + s1[...] + s2[...] + s3[...]
        norm = lax.rsqrt(so_far[0:1] / full_width + norm_eps)
        low = (from_hidden + norm * so_far) * coef
        spread_low = spread(low, 1, group)
        norm_col = jnp.transpose(jnp.broadcast_to(norm, (8, rows)))[:, 0:1]
        square[...] = jnp.zeros_like(square)
        lr[...] = jnp.zeros_like(lr)
        xr[...] = jnp.zeros_like(xr)
        for k, table in enumerate((t0, t1, t2, t3)):
            blk = (z - k + 4) % 4
            cols = pl.ds(pl.multiple_of(blk * 256, 256), 256)
            factor = jnp.concatenate([b_ref[2 * blk], b_ref[2 * blk + 1]], axis=1)
            both = own_ref[:, cols] + other_ref[:, cols].astype(f32)
            u = (
                jnp.dot(o_ref[...], table[...], preferred_element_type=f32)
                + dot(spread_low, factor, 0, 0)
                + norm_col * both
            )
            x = jnp.dot(o_ref[...], e_ref[:, cols], preferred_element_type=f32)
            x = (x + norm_col * lifted_ref[:, cols].astype(f32)).astype(bf16)
            d = d_ref[:, cols]
            g = g_ref[:, cols]
            r = r_ref[:, cols]
            rest = 1.0 - d
            h = jnp.zeros((per, 256), f32)
            xrr = x.astype(f32) * r
            xr[...] += xrr[:, :128] + xrr[:, 128:]
            gr = g * r
            for t in range(steps):
                span = slice(t * per, (t + 1) * per)
                h = d * h + rest * u[span]
                hr = h * gr
                hh = h * h
                square[span] += hh[:, :128] + hh[:, 128:]
                lr[span] += hr[:, :128] + hr[:, 128:]
            hidden_ref[:, cols] = x[(steps - 1) * per :].astype(f32)
            last_ref[:, cols] = h * g
        ones = jnp.ones((8, 128), f32)
        sums = [dot(ones, a[...], 1, 1, lax.Precision.HIGHEST) for a in (square, lr, xr)]
        row = lax.broadcasted_iota(jnp.int32, (8, rows), 0)
        stats_ref[...] = jnp.where(row == 0, sums[0], jnp.where(row == 1, sums[1], sums[2]))

    sl = lambda a, n: lax.slice_in_dim(a, chunk * n, (chunk + 1) * n, axis=0)
    lc = [lax.slice_in_dim(a, chunk * rows, (chunk + 1) * rows, axis=1) for a in lows]
    mid = lambda a: lax.slice_in_dim(a, chunk * group, (chunk + 1) * group, axis=1)
    return pl.pallas_call(
        kernel,
        out_shape=[
            jax.ShapeDtypeStruct((8, rows), f32),
            jax.ShapeDtypeStruct((per, width), f32),
            jax.ShapeDtypeStruct((per, width), f32),
        ],
        in_specs=[SMEM] + [VMEM] * 21,
        out_specs=[VMEM] * 3,
        scratch_shapes=[pltpu.VMEM((rows, 128), f32)] * 3,
        compiler_params=params(),
        name="second_layer",
        cost_estimate=pl.CostEstimate(flops=2000000000, bytes_accessed=4000000, transcendentals=0),
    )(where, sl(onehot, rows), embedding, *tables, *lc, *stats, lifted, own, other,
      mid(out_factors), decay, gain, reward)


def step_kernel(where, ins, outs, width):
    pops, k, cols = outs.shape
    halves = len(ins)
    per_half = width // halves

    def kernel(where_ref, outs_ref, *refs):
        in_refs = refs[:8]
        out_ref, paired = refs[8], refs[9]
        z, y, xl = where_ref[0], where_ref[3], where_ref[4]
        half = (lax.broadcasted_iota(jnp.int32, (k, cols), 0) % 8) // 4
        for half_idx in range(2):
            total = [jnp.zeros((2 * cols, 128), f32) for _ in range(4)]
            for dy in range(4):
                for dz in range(4):
                    for dx in range(2):
                        at = (dz * 2 + dx) * k
                        pop = ((y - dy + 4) % 4) * 8 + (xl ^ dx) * 4 + (z - dz + 4) % 4
                        o = outs_ref[pop]
                        zero = jnp.zeros_like(o)
                        paired[at : at + k, 0:cols] = jnp.where(half == 0, o, zero)
                        paired[at : at + k, cols : 2 * cols] = jnp.where(half == 1, o, zero)
                flipped = paired[...]
                for b in range(4):
                    parts = [
                        in_refs[dy][dz, dx, b] if half_idx == 0 else in_refs[4 + dz][dy, dx, b]
                        for dz in range(4)
                        for dx in range(2)
                    ]
                    a = jnp.concatenate(parts, axis=0)
                    total[b] += dot(flipped, a, 0, 0)
            for b in range(4):
                lo = half_idx * per_half + b * 128
                out = jnp.transpose(total[b])
                out_ref[0, lo : lo + 128, :] = out[:, :cols]
                out_ref[1, lo : lo + 128, :] = out[:, cols:]

    return pl.pallas_call(
        kernel,
        out_shape=jax.ShapeDtypeStruct((2, width, cols), f32),
        in_specs=[SMEM] + [VMEM] * 9,
        out_specs=VMEM,
        scratch_shapes=[pltpu.VMEM((8 * k, 2 * cols), bf16)],
        compiler_params=params(56),
        name="weight_step",
        cost_estimate=pl.CostEstimate(flops=2000000000, bytes_accessed=8000000, transcendentals=0),
    )(where, outs, *ins[0], *ins[1])


def ring_copies(value, axis):
    return [value] + [shift(value, axis, j) for j in range(1, lax.axis_size(axis))]


def shards(
    token_ids,
    fitness_ranks,
    embedding,
    mix_weights,
    factors_in,
    factors_out,
    decay_rates,
    norm_gain,
    reward_dir,
):
    members, seq_count, step_count = token_ids.shape
    vocab, width = embedding.shape
    full_width = mix_weights.shape[2]
    rank_count = factors_in.shape[2]
    pop_count = lax.axis_size(POP)
    members_all = members * pop_count
    coef = noise_scale * (full_width * rank_count) ** (-0.5)
    y, xl, z = (lax.axis_index(a) for a in POP)
    xh, c = (lax.axis_index(a) for a in MP)
    where = jnp.stack([z, xh, c, y, xl]).astype(jnp.int32)
    rows_all = members * seq_count * step_count
    rows = rows_all // CHUNKS

    tables = []
    for layer in range(2):
        peer, own = table_partial(layer, where, embedding, mix_weights)
        pair = own.astype(f32) + swap(peer, "c").astype(f32)
        crossing = swap(pair[1].astype(bf16), "xh")
        table = (pair[0] + crossing.astype(f32)).astype(bf16)
        tables.append(ring_copies(table, "z"))

    order = token_ids.reshape(CHUNKS, -1, step_count).transpose(0, 2, 1).reshape(-1)
    onehot = (order[:, None] == jnp.arange(vocab, dtype=jnp.int32)[None, :]).astype(bf16)
    a_blocks = regroup(factors_in, "regroup_in", 0)
    b_blocks = regroup(factors_out, "regroup_out", 0)
    b_own = lax.dynamic_slice_in_dim(b_blocks, (xh * 2 + c) * 8, 8, 0)
    lows = mp_parts(low_kernel(onehot, embedding, a_blocks))

    peer_cols = [
        lax.dynamic_slice(mix_weights, (1, 0, ((xh ^ rel) * 2 + (1 - c)) * width), (1, width, width))
        for rel in range(2)
    ]
    weights_peer = swap(jnp.concatenate(peer_cols, axis=0), "c")

    decay = [decay_rates[l : l + 1] for l in range(2)]
    gain = [norm_gain[l : l + 1] for l in range(2)]
    lifted, stats, sent, own_half, peers = [], [], [], [], []
    for k in range(CHUNKS):
        up, st = first_layer(
            k, where, coef, onehot, tables_of(tables, 0), lows, b_own, a_blocks, decay[0], gain[0]
        )
        lifted.append(up)
        peers.append(swap(up, "c"))
        stats.append(mp_parts(st))
    for k in range(CHUNKS):
        half = product(where, 1, lifted[k], peers[k], mix_weights, weights_peer, bf16)
        sent.append(swap(half, "xh"))
    for k in range(CHUNKS):
        own_half.append(product(where, 0, lifted[k], peers[k], mix_weights, weights_peer, f32))

    pair_in = jnp.stack([a_blocks, swap(a_blocks, "xl")])
    first, second = pair_in[:, :4], pair_in[:, 4:]
    first_z = jnp.stack(ring_copies(first, "z"))
    second_y = jnp.stack(ring_copies(second, "y"))
    first_zy = ring_copies(first_z, "y")
    second_yz = ring_copies(second_y, "z")
    half_rows = b_blocks.shape[1] // 2
    my_rows = lax.dynamic_slice_in_dim(b_blocks, c * half_rows, half_rows, 1)
    mine = lax.all_to_all(my_rows, POP, 0, 0, tiled=True)
    theirs = swap(mine, "c")
    outs = jnp.where(
        c == 0, jnp.concatenate([mine, theirs], axis=1), jnp.concatenate([theirs, mine], axis=1)
    )
    ranks_every = lax.all_gather(fitness_ranks, POP, tiled=True)
    shares_all = ranks_every.astype(f32) / members_all
    rank_mean = jnp.mean(shares_all)
    rank_spread = jnp.mean((shares_all - rank_mean) * (shares_all - rank_mean)) + spread_eps
    shaped = (shares_all - rank_mean) * lax.rsqrt(rank_spread)
    shaped = shaped * (members_all * rank_count) ** (-0.5)
    shaped_rows = jnp.repeat(shaped.reshape(pop_count, members), 2 * rank_count, axis=1)
    outs = (outs.astype(f32) * shaped_rows[:, :, None]).astype(bf16)
    weight_step = step_kernel(where, [first_zy, second_yz], outs, width)

    finals, terms = [], []
    for k in range(CHUNKS):
        st, hidden, last = second_layer(
            k, where, coef, full_width, onehot, embedding, tables_of(tables, 1), lows, stats[k],
            lifted[k], own_half[k], sent[k], b_own, decay[1], gain[1], reward_dir[None],
        )
        so_far = sum(mp_parts(st))
        norm = lax.rsqrt(so_far[0] / full_width + norm_eps)
        terms.append(so_far[2] + norm * so_far[1])
        tail = norm[-last.shape[0] :]
        finals.append((hidden + last * tail[:, None]).astype(bf16))
    final_features = jnp.concatenate(finals, axis=0).reshape(members, seq_count, width)
    scores = jnp.mean(jnp.stack(terms).reshape(CHUNKS, step_count, -1), axis=1)
    scores = scores.reshape(members, seq_count) * full_width ** (-0.5)
    return (final_features, scores, weight_step)


def tables_of(tables, layer):
    return tables[layer]


def solution(mesh):
    fine = Mesh(mesh.devices.reshape(4, 2, 4, 2, 2), POP + MP)
    return jax.shard_map(
        shards,
        mesh=fine,
        in_specs=(
            P(POP, None, None),
            P(POP),
            P(None, MP),
            P(None, MP, None),
            P(None, POP, None, MP),
            P(None, POP, None, None),
            P(None, MP),
            P(None, MP),
            P(MP),
        ),
        out_specs=(P(POP, None, MP), P(POP, None), P(None, MP, POP)),
        check_vma=False,
    )
```

```python
import jax
import jax.numpy as jnp
from jax import lax
from jax.experimental import pallas as pl
from jax.experimental.pallas import tpu as pltpu
from jax.sharding import Mesh
from jax.sharding import PartitionSpec as P

noise_scale = 0.25
norm_eps = 1e-06
spread_eps = 1e-05

POP = ("y", "xl", "z")
MP = ("xh", "c")
CHUNKS = 3
f32 = jnp.float32
bf16 = jnp.bfloat16
SMEM = pl.BlockSpec(memory_space=pltpu.SMEM)
VMEM = pl.BlockSpec(memory_space=pltpu.VMEM)


def params(mib=48):
    return pltpu.CompilerParams(vmem_limit_bytes=mib * 1024 * 1024)


def swap(value, axis):
    return lax.ppermute(value, axis, [(0, 1), (1, 0)])


def shift(value, axis, by):
    n = lax.axis_size(axis)
    return lax.ppermute(value, axis, [(i, (i + by) % n) for i in range(n)])


def after(value, *earlier):
    return lax.optimization_barrier((value, *earlier))[0]


def mp_parts(value):
    pair = value + swap(value, "c")
    return pair, swap(pair, "xh")


def dot(a, b, ca, cb, precision=None):
    return lax.dot_general(
        a, b, (((ca,), (cb,)), ((), ())), preferred_element_type=f32, precision=precision
    )


def regroup(factors, first, second):
    layers, members, ranks, width = factors.shape
    blocks = width // 128

    def kernel(in_ref, out_ref):
        for m in range(members):
            rows = jnp.concatenate(
                [in_ref[l, m].astype(f32) for l in range(layers)], axis=0
            ).astype(bf16)
            lo = m * layers * ranks
            for b in range(blocks):
                out_ref[b, lo : lo + layers * ranks, :] = rows[:, b * 128 : (b + 1) * 128]

    return pl.pallas_call(
        kernel,
        out_shape=jax.ShapeDtypeStruct((blocks, members * layers * ranks, 128), bf16),
        in_specs=[VMEM],
        out_specs=VMEM,
        compiler_params=params(),
        name=first,
    )(factors)


def table_partial(layer, part_at, where, embedding, weights):
    vocab, width = embedding.shape
    full = weights.shape[2]
    piece = full // 16

    def kernel(where_ref, e_ref, wp_ref, wo_ref, peer_ref, own_ref):
        peer_ref[0] = jnp.dot(e_ref[...], wp_ref[0], preferred_element_type=f32).astype(bf16)
        own_ref[0] = jnp.dot(e_ref[...], wo_ref[0], preferred_element_type=f32).astype(bf16)

    def block(rel, s, flip):
        owner = (s[1] ^ rel) * 2 + (s[2] ^ flip)
        return owner * 4 + s[part_at]

    return pl.pallas_call(
        kernel,
        grid_spec=pltpu.PrefetchScalarGridSpec(
            num_scalar_prefetch=1,
            grid=(2,),
            in_specs=[
                pl.BlockSpec((vocab, width), lambda r, s: (0, 0)),
                pl.BlockSpec((1, width, piece), lambda r, s: (layer, 0, block(r, s, 1))),
                pl.BlockSpec((1, width, piece), lambda r, s: (layer, 0, block(r, s, 0))),
            ],
            out_specs=[pl.BlockSpec((1, vocab, piece), lambda r, s: (r, 0, 0))] * 2,
        ),
        out_shape=[jax.ShapeDtypeStruct((2, vocab, piece), bf16)] * 2,
        compiler_params=params(),
        name="table",
        cost_estimate=pl.CostEstimate(
            flops=2 * vocab * width * piece * 4, bytes_accessed=width * piece * 8, transcendentals=0
        ),
    )(where, embedding, weights, weights)


def member_of(shape, per, dim):
    return lax.broadcasted_iota(jnp.int32, shape, dim) // per


def low_kernel(onehot, embedding, factors):
    rows = onehot.shape[0]
    per_chunk = rows // CHUNKS
    group = factors.shape[1] // CHUNKS

    def kernel(o_ref, e_ref, a_ref, out_ref):
        for k in range(CHUNKS):
            x = jnp.dot(
                o_ref[k * per_chunk : (k + 1) * per_chunk, :], e_ref[...], preferred_element_type=f32
            ).astype(bf16)
            total = jnp.zeros((group, per_chunk), f32)
            for b in range(factors.shape[0]):
                total += dot(
                    a_ref[b, k * group : (k + 1) * group, :], x[:, b * 128 : (b + 1) * 128], 1, 1
                )
            out_ref[:, k * per_chunk : (k + 1) * per_chunk] = diagonal(total)

    return pl.pallas_call(
        kernel,
        out_shape=jax.ShapeDtypeStruct((8, rows), f32),
        in_specs=[VMEM] * 3,
        out_specs=VMEM,
        compiler_params=params(),
        name="low",
    )(onehot, embedding, factors)


def diagonal(total):
    group, cols = total.shape
    row_member = member_of((group, cols), 8, 0)
    col_member = (lax.broadcasted_iota(jnp.int32, (group, cols), 1) % 16) // 4
    kept = jnp.where(row_member == col_member, total, 0.0)
    out = kept[0:8]
    for m in range(1, group // 8):
        out = out + kept[m * 8 : (m + 1) * 8]
    return out


def spread(low, layer, group):
    cols = low.shape[1]
    row = lax.broadcasted_iota(jnp.int32, (group, cols), 0)
    col_member = (lax.broadcasted_iota(jnp.int32, (group, cols), 1) % 16) // 4
    keep = (row // 8 == col_member) & ((row % 8) // 4 == layer)
    tiled = jnp.concatenate([low] * (group // 8), axis=0)
    return jnp.where(keep, tiled, 0.0).astype(bf16)


def first_layer(chunk, where, coef, onehot, tables, lows, out_factors, in_factors, decay, gain):
    rows = onehot.shape[0] // CHUNKS
    group = out_factors.shape[1] // CHUNKS
    width = decay.shape[1]
    steps = 16
    per = rows // steps

    def kernel(where_ref, o_ref, t0, t1, t2, t3, l0, l1, b_ref, a_ref, d_ref, g_ref,
               lifted_ref, stats_ref, square):
        z = where_ref[0]
        low = (l0[...] + l1[...]) * coef
        spread_low = spread(low, 0, group)
        square[...] = jnp.zeros_like(square)
        total = jnp.zeros((group, rows), f32)
        for k, table in enumerate((t0, t1, t2, t3)):
            blk = (z - k + 4) % 4
            cols = pl.ds(pl.multiple_of(blk * 256, 256), 256)
            factor = jnp.concatenate([b_ref[2 * blk], b_ref[2 * blk + 1]], axis=1)
            u = jnp.dot(o_ref[...], table[...], preferred_element_type=f32) + dot(
                spread_low, factor, 0, 0
            )
            d = d_ref[:, cols]
            g = g_ref[:, cols]
            rest = 1.0 - d
            h = jnp.zeros((per, 256), f32)
            for t in range(steps):
                span = slice(t * per, (t + 1) * per)
                h = d * h + rest * u[span]
                lifted_ref[span, cols] = (h * g).astype(bf16)
                hh = h * h
                square[span] += hh[:, :128] + hh[:, 128:]
            factor_in = jnp.concatenate([a_ref[2 * blk], a_ref[2 * blk + 1]], axis=1)
            total += dot(factor_in, lifted_ref[:, cols], 1, 1)
        sums = dot(jnp.ones((8, 128), f32), square[...], 1, 1, lax.Precision.HIGHEST)
        low_next = diagonal(total)
        row = lax.broadcasted_iota(jnp.int32, (8, rows), 0)
        stats_ref[...] = jnp.where(row < 4, sums, low_next)

    whole = lambda a: pl.BlockSpec(a.shape, lambda i, n=a.ndim: (0,) * n)
    at_col = pl.BlockSpec((8, rows), lambda i: (0, chunk))
    mid = pl.BlockSpec((8, group, 128), lambda i: (0, chunk, 0))
    return pl.pallas_call(
        kernel,
        grid=(1,),
        out_shape=[
            jax.ShapeDtypeStruct((rows, width), bf16),
            jax.ShapeDtypeStruct((8, rows), f32),
        ],
        in_specs=[SMEM, pl.BlockSpec((rows, onehot.shape[1]), lambda i: (chunk, 0))]
        + [whole(t) for t in tables]
        + [at_col, at_col, mid, mid, whole(decay), whole(gain)],
        out_specs=[
            pl.BlockSpec((rows, width), lambda i: (0, 0)),
            pl.BlockSpec((8, rows), lambda i: (0, 0)),
        ],
        scratch_shapes=[pltpu.VMEM((rows, 128), f32)],
        compiler_params=params(),
        name="first_layer",
        cost_estimate=pl.CostEstimate(flops=2000000000, bytes_accessed=4000000, transcendentals=0),
    )(where, onehot, *tables, *lows, out_factors, in_factors, decay, gain)


def product(where, rel, first, count, lifted, weights, weights_peer, out_dtype):
    rows, width = lifted[0].shape
    piece = width // 4
    chunks = len(lifted)

    def kernel(where_ref, *refs):
        wa_ref, wb_ref, out_ref = refs[chunks:]
        for k in range(chunks // 2):
            out_ref[k * rows : (k + 1) * rows, :] = (
                jnp.dot(refs[k][...], wa_ref[0], preferred_element_type=f32)
                + jnp.dot(refs[chunks // 2 + k][...], wb_ref[...], preferred_element_type=f32)
            ).astype(out_dtype)

    total = rows * chunks // 2
    return pl.pallas_call(
        kernel,
        grid_spec=pltpu.PrefetchScalarGridSpec(
            num_scalar_prefetch=1,
            grid=(count,),
            in_specs=[pl.BlockSpec((rows, width), lambda n, s: (0, 0))] * chunks
            + [
                pl.BlockSpec(
                    (1, width, piece),
                    lambda n, s: (1, 0, ((s[1] ^ rel) * 2 + s[2]) * 4 + first + n),
                ),
                pl.BlockSpec((width, piece), lambda n, s: (0, first + n)),
            ],
            out_specs=pl.BlockSpec((total, piece), lambda n, s: (0, n)),
        ),
        out_shape=jax.ShapeDtypeStruct((total, piece * count), out_dtype),
        compiler_params=params(),
        name="product",
        cost_estimate=pl.CostEstimate(
            flops=4 * total * width * piece * count,
            bytes_accessed=6 * width * piece * count,
            transcendentals=0,
        ),
    )(where, *lifted, weights, weights_peer)


def second_layer(n, where, coef, full_width, onehot, embedding, table, lows, stats, lifted,
                 own, other, out_factors, decay, gain, reward, before):
    rows = onehot.shape[0] // CHUNKS
    group = out_factors.shape[1] // CHUNKS
    steps = 16
    per = rows // steps

    def kernel(where_ref, o_ref, e_ref, t_ref, l0, l1, s0, s1, up0, up1, up2,
               own_ref, other_ref, b_ref, d_ref, g_ref, r_ref, before_ref,
               stats_ref, hidden_ref, last_ref, square, lr, xr):
        y = where_ref[3]
        table = t_ref[(y - n + 4) % 4]
        factor = jnp.concatenate([b_ref[0], b_ref[1]], axis=1)
        e = e_ref[...]
        d = d_ref[...]
        g = g_ref[...]
        r = r_ref[...]
        rest = 1.0 - d
        gr = g * r
        for k, up in enumerate((up0, up1, up2)):
            span_k = slice(k * rows, (k + 1) * rows)
            so_far = s0[:, span_k] + s1[:, span_k]
            norm = lax.rsqrt(so_far[0:1] / full_width + norm_eps)
            low = (l0[:, span_k] + l1[:, span_k] + norm * so_far) * coef
            spread_low = spread(low, 1, group)
            norm_col = jnp.transpose(jnp.broadcast_to(norm, (8, rows)))[:, 0:1]
            both = own_ref[span_k] + other_ref[span_k].astype(f32)
            o = o_ref[span_k]
            u = (
                jnp.dot(o, table, preferred_element_type=f32)
                + dot(spread_low, factor[k * group : (k + 1) * group], 0, 0)
                + norm_col * both
            )
            x = jnp.dot(o, e, preferred_element_type=f32)
            x = (x + norm_col * up[...].astype(f32)).astype(bf16)
            h = jnp.zeros((per, 256), f32)
            xrr = x.astype(f32) * r
            xr[...] = xrr[:, :128] + xrr[:, 128:]
            for t in range(steps):
                span = slice(t * per, (t + 1) * per)
                h = d * h + rest * u[span]
                hr = h * gr
                hh = h * h
                square[span] = hh[:, :128] + hh[:, 128:]
                lr[span] = hr[:, :128] + hr[:, 128:]
            tail = slice(k * per, (k + 1) * per)
            hidden_ref[tail] = x[(steps - 1) * per :].astype(f32)
            last_ref[tail] = h * g
            ones = jnp.ones((8, 128), f32)
            sums = [dot(ones, a[...], 1, 1, lax.Precision.HIGHEST) for a in (square, lr, xr)]
            row = lax.broadcasted_iota(jnp.int32, (8, rows), 0)
            stats_ref[:, span_k] = before_ref[:, span_k] + jnp.where(
                row == 0, sums[0], jnp.where(row == 1, sums[1], sums[2])
            )

    whole = lambda a: pl.BlockSpec(a.shape, lambda i, m=a.ndim: (0,) * m)
    col = lambda a: pl.BlockSpec((a.shape[0], 256), lambda i: (0, n))
    total = rows * CHUNKS
    return pl.pallas_call(
        kernel,
        grid=(1,),
        out_shape=[
            jax.ShapeDtypeStruct((8, total), f32),
            jax.ShapeDtypeStruct((per * CHUNKS, 256), f32),
            jax.ShapeDtypeStruct((per * CHUNKS, 256), f32),
        ],
        in_specs=[SMEM, whole(onehot), col(embedding), whole(table)]
        + [whole(a) for a in (*lows, *stats)]
        + [col(a) for a in lifted]
        + [col(own), whole(other)]
        + [pl.BlockSpec((2, group * CHUNKS, 128), lambda i: (n, 0, 0))]
        + [col(a) for a in (decay, gain, reward)]
        + [whole(before)],
        out_specs=[
            pl.BlockSpec((8, total), lambda i: (0, 0)),
            pl.BlockSpec((per * CHUNKS, 256), lambda i: (0, 0)),
            pl.BlockSpec((per * CHUNKS, 256), lambda i: (0, 0)),
        ],
        scratch_shapes=[pltpu.VMEM((rows, 128), f32)] * 3,
        compiler_params=params(),
        name="second_layer",
        cost_estimate=pl.CostEstimate(flops=2000000000, bytes_accessed=4000000, transcendentals=0),
    )(where, onehot, embedding, table, *lows, *stats, *lifted, own, other,
      out_factors, decay, gain, reward, before)


def step_kernel(where, ins, outs, width):
    pops, k, cols = outs.shape
    halves = len(ins)
    per_half = width // halves

    def kernel(where_ref, outs_ref, *refs):
        in_refs = refs[:8]
        out_ref, paired = refs[8], refs[9]
        z, y, xl = where_ref[0], where_ref[3], where_ref[4]
        half = (lax.broadcasted_iota(jnp.int32, (k, cols), 0) % 8) // 4
        for half_idx in range(2):
            total = [jnp.zeros((2 * cols, 128), f32) for _ in range(4)]
            for dy in range(4):
                for dz in range(4):
                    for dx in range(2):
                        at = (dz * 2 + dx) * k
                        pop = ((y - dy + 4) % 4) * 8 + (xl ^ dx) * 4 + (z - dz + 4) % 4
                        o = outs_ref[pop]
                        zero = jnp.zeros_like(o)
                        paired[at : at + k, 0:cols] = jnp.where(half == 0, o, zero)
                        paired[at : at + k, cols : 2 * cols] = jnp.where(half == 1, o, zero)
                flipped = paired[...]
                for b in range(4):
                    parts = [
                        in_refs[dy][dz, dx, b] if half_idx == 0 else in_refs[4 + dz][dy, dx, b]
                        for dz in range(4)
                        for dx in range(2)
                    ]
                    a = jnp.concatenate(parts, axis=0)
                    total[b] += dot(flipped, a, 0, 0)
            for b in range(4):
                lo = half_idx * per_half + b * 128
                out = jnp.transpose(total[b])
                out_ref[0, lo : lo + 128, :] = out[:, :cols]
                out_ref[1, lo : lo + 128, :] = out[:, cols:]

    return pl.pallas_call(
        kernel,
        out_shape=jax.ShapeDtypeStruct((2, width, cols), f32),
        in_specs=[SMEM] + [VMEM] * 9,
        out_specs=VMEM,
        scratch_shapes=[pltpu.VMEM((8 * k, 2 * cols), bf16)],
        compiler_params=params(56),
        name="weight_step",
        cost_estimate=pl.CostEstimate(flops=2000000000, bytes_accessed=8000000, transcendentals=0),
    )(where, outs, *ins[0], *ins[1])


def ring_copies(value, axis):
    return [value] + [shift(value, axis, j) for j in range(1, lax.axis_size(axis))]


def shards(
    token_ids,
    fitness_ranks,
    embedding,
    mix_weights,
    factors_in,
    factors_out,
    decay_rates,
    norm_gain,
    reward_dir,
):
    members, seq_count, step_count = token_ids.shape
    vocab, width = embedding.shape
    full_width = mix_weights.shape[2]
    rank_count = factors_in.shape[2]
    pop_count = lax.axis_size(POP)
    members_all = members * pop_count
    coef = noise_scale * (full_width * rank_count) ** (-0.5)
    y, xl, z = (lax.axis_index(a) for a in POP)
    xh, c = (lax.axis_index(a) for a in MP)
    where = jnp.stack([z, xh, c, y, xl]).astype(jnp.int32)
    rows_all = members * seq_count * step_count

    order = token_ids.reshape(CHUNKS, -1, step_count).transpose(0, 2, 1).reshape(-1)
    onehot = (order[:, None] == jnp.arange(vocab, dtype=jnp.int32)[None, :]).astype(bf16)

    def own_sum(own, peer):
        pair = own.astype(f32) + swap(peer, "c").astype(f32)
        return pair[0], pair[1].astype(bf16)

    peer, own = table_partial(0, 0, where, embedding, mix_weights)
    onehot = after(onehot, peer)
    a_blocks = regroup(after(factors_in, peer), "regroup_in", 0)
    keep, cross = own_sum(own, peer)
    lows = mp_parts(low_kernel(onehot, embedding, a_blocks))
    table = (keep + swap(cross, "xh").astype(f32)).astype(bf16)
    first_tables = ring_copies(table, "z")

    peer, own = table_partial(1, 3, after(where, cross), embedding, mix_weights)
    keep, cross = own_sum(own, peer)
    table_next = (keep + swap(after(cross, table), "xh").astype(f32)).astype(bf16)
    table_next = after(table_next, table)
    second_tables = jnp.stack(ring_copies(table_next, "y"))

    b_blocks = regroup(after(factors_out, lows[0]), "regroup_out", 0)
    b_own = lax.dynamic_slice_in_dim(b_blocks, (xh * 2 + c) * 8, 8, 0)

    late_weights = after(mix_weights, table)
    weights_peer = [
        swap(
            lax.dynamic_slice(
                late_weights, (1, 0, ((xh ^ rel) * 2 + (1 - c)) * width), (1, width, width)
            )[0],
            "c",
        )
        for rel in range(2)
    ]

    decay = [decay_rates[l : l + 1] for l in range(2)]
    gain = [norm_gain[l : l + 1] for l in range(2)]
    lifted, stats, peers = [], [], []
    for k in range(CHUNKS):
        up, st = first_layer(
            k, where, coef, onehot, first_tables, lows, b_own, a_blocks, decay[0], gain[0]
        )
        lifted.append(up)
        peers.append(swap(up, "c"))
        stats.append(st)
    stats = mp_parts(jnp.concatenate(stats, axis=1))
    both = lifted + peers
    sent = []
    for n in range(4):
        half = product(where, 1, n, 1, both, mix_weights, weights_peer[1], bf16)
        sent.append(swap(half, "xh"))
    own_half = product(after(where, half), 0, 0, 4, both, mix_weights, weights_peer[0], f32)

    pair_in = jnp.stack([a_blocks, swap(a_blocks, "xl")])
    pair_in = after(pair_in, lifted[0])
    first, second = pair_in[:, :4], pair_in[:, 4:]
    first_z = jnp.stack(ring_copies(first, "z"))
    second_y = jnp.stack(ring_copies(second, "y"))
    first_zy = ring_copies(first_z, "y")
    second_yz = ring_copies(second_y, "z")
    half_rows = b_blocks.shape[1] // 2
    my_rows = lax.dynamic_slice_in_dim(b_blocks, c * half_rows, half_rows, 1)
    digits = jnp.stack([fitness_ranks // 32, fitness_ranks % 32]).astype(bf16)
    digits = jnp.pad(digits, ((0, 6), (0, 128 - members)))
    digits = jnp.broadcast_to(digits[None], (pop_count, 8, 128))
    packed = after(jnp.concatenate([my_rows, digits], axis=1), half)
    arrived = lax.all_to_all(packed, POP, 0, 0, tiled=True)
    mine = arrived[:, :half_rows]
    digits_all = arrived[:, half_rows : half_rows + 2, :members].astype(f32)
    ranks_every = (digits_all[:, 0] * 32.0 + digits_all[:, 1]).reshape(-1)
    theirs = swap(mine, "c")
    outs = jnp.where(
        c == 0, jnp.concatenate([mine, theirs], axis=1), jnp.concatenate([theirs, mine], axis=1)
    )
    shares_all = ranks_every / members_all
    rank_mean = jnp.mean(shares_all)
    rank_spread = jnp.mean((shares_all - rank_mean) * (shares_all - rank_mean)) + spread_eps
    shaped = (shares_all - rank_mean) * lax.rsqrt(rank_spread)
    shaped = shaped * (members_all * rank_count) ** (-0.5)
    shaped_rows = jnp.repeat(shaped.reshape(pop_count, members), 2 * rank_count, axis=1)
    outs = (outs.astype(f32) * shaped_rows[:, :, None]).astype(bf16)
    weight_step = step_kernel(where, [first_zy, second_yz], outs, width)

    st = jnp.zeros((8, rows_all), f32)
    hiddens, lasts = [], []
    for n in range(4):
        st, hidden, last = second_layer(
            n, where, coef, full_width, onehot, embedding, second_tables, lows, stats,
            lifted, own_half, sent[n], b_own, decay[1], gain[1], reward_dir[None], st,
        )
        hiddens.append(hidden)
        lasts.append(last)
    so_far = sum(mp_parts(st))
    norm = lax.rsqrt(so_far[0] / full_width + norm_eps)
    terms = (so_far[2] + norm * so_far[1]).reshape(CHUNKS, step_count, -1)
    tail = norm.reshape(CHUNKS, step_count, -1)[:, -1].reshape(-1)
    finals = jnp.concatenate(hiddens, axis=1) + jnp.concatenate(lasts, axis=1) * tail[:, None]
    final_features = finals.astype(bf16).reshape(members, seq_count, width)
    scores = jnp.mean(terms, axis=1).reshape(members, seq_count) * full_width ** (-0.5)
    return (final_features, scores, weight_step)


def solution(mesh):
    fine = Mesh(mesh.devices.reshape(4, 2, 4, 2, 2), POP + MP)
    return jax.shard_map(
        shards,
        mesh=fine,
        in_specs=(
            P(POP, None, None),
            P(POP),
            P(None, MP),
            P(None, MP, None),
            P(None, POP, None, MP),
            P(None, POP, None, None),
            P(None, MP),
            P(None, MP),
            P(MP),
        ),
        out_specs=(P(POP, None, MP), P(POP, None), P(None, MP, POP)),
        check_vma=False,
    )
```

```python
import jax
import jax.numpy as jnp
from jax import lax
from jax.experimental import pallas as pl
from jax.experimental.pallas import tpu as pltpu
from jax.sharding import Mesh
from jax.sharding import PartitionSpec as P

noise_scale = 0.25
norm_eps = 1e-06
spread_eps = 1e-05

POP = ("y", "xl", "z")
MP = ("xh", "c")
CHUNKS = 3
f32 = jnp.float32
bf16 = jnp.bfloat16
SMEM = pl.BlockSpec(memory_space=pltpu.SMEM)
VMEM = pl.BlockSpec(memory_space=pltpu.VMEM)
small_cost = pl.CostEstimate(flops=1000, bytes_accessed=1000, transcendentals=0)


def params(mib=24):
    return pltpu.CompilerParams(vmem_limit_bytes=mib * 1024 * 1024)


def swap(value, axis):
    return lax.ppermute(value, axis, [(0, 1), (1, 0)])


def after(value, *earlier):
    return lax.optimization_barrier((value, *earlier))[0]


def mp_parts(value):
    pair = value + swap(value, "c")
    return pair, swap(pair, "xh")


def dot(a, b, ca, cb, precision=None):
    return lax.dot_general(
        a, b, (((ca,), (cb,)), ((), ())), preferred_element_type=f32, precision=precision
    )


def regroup(factors, first, second):
    layers, members, ranks, width = factors.shape
    blocks = width // 128

    def kernel(in_ref, out_ref):
        for m in range(members):
            rows = jnp.concatenate(
                [in_ref[l, m].astype(f32) for l in range(layers)], axis=0
            ).astype(bf16)
            lo = m * layers * ranks
            for b in range(blocks):
                out_ref[b, lo : lo + layers * ranks, :] = rows[:, b * 128 : (b + 1) * 128]

    return pl.pallas_call(
        kernel,
        out_shape=jax.ShapeDtypeStruct((blocks, members * layers * ranks, 128), bf16),
        in_specs=[VMEM],
        out_specs=VMEM,
        compiler_params=params(),
        name=first,
        cost_estimate=small_cost,
    )(factors)


def product(layer, rel, flip, where, lefts, weights, first=0, count=4):
    rows, width = lefts[0].shape
    total = rows * len(lefts)
    flips = len(flip)

    def kernel(where_ref, w_ref, *refs):
        left_refs = refs[: len(lefts)]
        out_refs = refs[len(lefts) : len(lefts) + flips]
        block, sems = refs[len(lefts) + flips :]

        def fetch(n, f):
            owner = (where_ref[1] ^ rel) * 2 + (where_ref[2] ^ flip[f])
            at = pl.multiple_of(owner * width + (first + n) * 256, 256)
            return pltpu.make_async_copy(
                w_ref.at[layer, :, pl.ds(at, 256)], block.at[n * flips + f], sems.at[n * flips + f]
            )

        for n in range(count):
            for f in range(flips):
                fetch(n, f).start()

        def one(n, carry):
            for f in range(flips):
                fetch(n, f).wait()
                w = block[n * flips + f]
                for k, left in enumerate(left_refs):
                    out_refs[f][n, k * rows : (k + 1) * rows, :] = jnp.dot(
                        left[...], w, preferred_element_type=f32
                    ).astype(bf16)
            return carry

        lax.fori_loop(0, count, one, 0)

    return pl.pallas_call(
        kernel,
        out_shape=[jax.ShapeDtypeStruct((count, total, 256), bf16)] * len(flip),
        in_specs=[SMEM, pl.BlockSpec(memory_space=pltpu.HBM)] + [VMEM] * len(lefts),
        out_specs=[VMEM] * len(flip),
        scratch_shapes=[
            pltpu.VMEM((count * flips, width, 256), bf16),
            pltpu.SemaphoreType.DMA((count * flips,)),
        ],
        compiler_params=params(16),
        name="product",
        cost_estimate=small_cost,
    )(where, weights, *lefts)


def member_of(shape, per, dim):
    return lax.broadcasted_iota(jnp.int32, shape, dim) // per


def low_kernel(onehot, embedding, factors):
    rows = onehot.shape[0]
    per_chunk = rows // CHUNKS
    group = factors.shape[1] // CHUNKS

    def kernel(o_ref, e_ref, a_ref, out_ref):
        for k in range(CHUNKS):
            x = jnp.dot(
                o_ref[k * per_chunk : (k + 1) * per_chunk, :], e_ref[...], preferred_element_type=f32
            ).astype(bf16)
            total = jnp.zeros((group, per_chunk), f32)
            for b in range(factors.shape[0]):
                total += dot(
                    a_ref[b, k * group : (k + 1) * group, :], x[:, b * 128 : (b + 1) * 128], 1, 1
                )
            out_ref[:, k * per_chunk : (k + 1) * per_chunk] = diagonal(total)

    return pl.pallas_call(
        kernel,
        out_shape=jax.ShapeDtypeStruct((8, rows), f32),
        in_specs=[VMEM] * 3,
        out_specs=VMEM,
        compiler_params=params(),
        name="low",
        cost_estimate=small_cost,
    )(onehot, embedding, factors)


def diagonal(total):
    group, cols = total.shape
    row_member = member_of((group, cols), 8, 0)
    col_member = (lax.broadcasted_iota(jnp.int32, (group, cols), 1) % 16) // 4
    kept = jnp.where(row_member == col_member, total, 0.0)
    out = kept[0:8]
    for m in range(1, group // 8):
        out = out + kept[m * 8 : (m + 1) * 8]
    return out


def spread(low, layer, group):
    cols = low.shape[1]
    row = lax.broadcasted_iota(jnp.int32, (group, cols), 0)
    col_member = (lax.broadcasted_iota(jnp.int32, (group, cols), 1) % 16) // 4
    keep = (row // 8 == col_member) & ((row % 8) // 4 == layer)
    tiled = jnp.concatenate([low] * (group // 8), axis=0)
    return jnp.where(keep, tiled, 0.0).astype(bf16)


def first_layer(chunk, where, coef, onehot, table_parts, lows, out_factors, in_factors, decay, gain):
    rows = onehot.shape[0] // CHUNKS
    group = out_factors.shape[1] // CHUNKS
    width = decay.shape[1]
    steps = 16
    per = rows // steps

    def kernel(o_ref, t0, t1, t2, l0, l1, b_ref, a_ref, d_ref, g_ref, lifted_ref, stats_ref, square):
        at = slice(chunk * rows, (chunk + 1) * rows)
        mine = slice(chunk * group, (chunk + 1) * group)
        low = (l0[:, at] + l1[:, at]) * coef
        spread_low = spread(low, 0, group)
        total = jnp.zeros((group, rows), f32)
        for n in range(width // 256):
            cols = slice(n * 256, (n + 1) * 256)
            table = (t0[n].astype(f32) + t1[n].astype(f32) + t2[n].astype(f32)).astype(bf16)
            factor = jnp.concatenate([b_ref[2 * n, mine], b_ref[2 * n + 1, mine]], axis=1)
            u = jnp.dot(o_ref[at], table, preferred_element_type=f32) + dot(
                spread_low, factor, 0, 0
            )
            d = d_ref[:, cols]
            g = g_ref[:, cols]
            rest = 1.0 - d
            h = jnp.zeros((per, 256), f32)
            for t in range(steps):
                span = slice(t * per, (t + 1) * per)
                h = d * h + rest * u[span]
                lifted_ref[span, cols] = (h * g).astype(bf16)
                hh = h * h
                hh = hh[:, :128] + hh[:, 128:]
                if n == 0:
                    square[span] = hh
                else:
                    square[span] += hh
            factor_in = jnp.concatenate([a_ref[2 * n, mine], a_ref[2 * n + 1, mine]], axis=1)
            total += dot(factor_in, lifted_ref[:, cols], 1, 1)
        sums = dot(jnp.ones((8, 128), f32), square[...], 1, 1, lax.Precision.HIGHEST)
        low_next = diagonal(total)
        row = lax.broadcasted_iota(jnp.int32, (8, rows), 0)
        stats_ref[...] = jnp.where(row < 4, sums, low_next)

    return pl.pallas_call(
        kernel,
        out_shape=[
            jax.ShapeDtypeStruct((rows, width), bf16),
            jax.ShapeDtypeStruct((8, rows), f32),
        ],
        in_specs=[VMEM] * 10,
        out_specs=[VMEM, VMEM],
        scratch_shapes=[pltpu.VMEM((rows, 128), f32)],
        compiler_params=params(16),
        name="first_layer",
        cost_estimate=small_cost,
    )(onehot, *table_parts, *lows, out_factors, in_factors, decay, gain)


def next_hidden(full_width, onehot, embedding, stats, lifted):
    rows = lifted[0].shape[0]
    total, width = rows * CHUNKS, embedding.shape[1]

    def kernel(o_ref, e_ref, s0, s1, up0, up1, up2, out_ref):
        for k, up in enumerate((up0, up1, up2)):
            span = slice(k * rows, (k + 1) * rows)
            so_far = s0[:, span] + s1[:, span]
            norm = lax.rsqrt(so_far / full_width + norm_eps)
            norm_col = jnp.transpose(norm)[:, 0:1]
            x = jnp.dot(o_ref[span], e_ref[...], preferred_element_type=f32)
            out_ref[span] = (x + norm_col * up[...].astype(f32)).astype(bf16)

    return pl.pallas_call(
        kernel,
        out_shape=jax.ShapeDtypeStruct((total, width), bf16),
        in_specs=[VMEM] * 7,
        out_specs=VMEM,
        compiler_params=params(16),
        name="next_hidden",
        cost_estimate=small_cost,
    )(onehot, embedding, *stats, *lifted)


def second_layer(n, coef, full_width, hidden, lows, stats, halves, crossed, out_factors,
                 decay, gain, reward, before):
    rows = hidden.shape[0] // CHUNKS
    group = out_factors.shape[1] // CHUNKS
    steps = 16
    per = rows // steps
    cols = slice(n * 256, (n + 1) * 256)

    def kernel(x_ref, l0, l1, s0, s1, own_ref, peer_ref, other_ref, b_ref, d_ref, g_ref, r_ref,
               before_ref, stats_ref, last_ref, square, lr, xr):
        factor = jnp.concatenate([b_ref[2 * n], b_ref[2 * n + 1]], axis=1)
        d = d_ref[:, cols]
        g = g_ref[:, cols]
        r = r_ref[:, cols]
        rest = 1.0 - d
        gr = g * r
        for k in range(CHUNKS):
            span_k = slice(k * rows, (k + 1) * rows)
            so_far = s0[:, span_k] + s1[:, span_k]
            norm = lax.rsqrt(so_far[0:1] / full_width + norm_eps)
            low = (l0[:, span_k] + l1[:, span_k] + norm * so_far) * coef
            spread_low = spread(low, 1, group)
            u = dot(spread_low, factor[k * group : (k + 1) * group], 0, 0) + (
                own_ref[n, span_k].astype(f32)
                + peer_ref[n, span_k].astype(f32)
                + other_ref[0, span_k].astype(f32)
            )
            h = jnp.zeros((per, 256), f32)
            xrr = x_ref[span_k, cols].astype(f32) * r
            xr[span_k] = xrr[:, :128] + xrr[:, 128:]
            for t in range(steps):
                span = slice(k * rows + t * per, k * rows + (t + 1) * per)
                h = d * h + rest * u[t * per : (t + 1) * per]
                hr = h * gr
                hh = h * h
                square[span] = hh[:, :128] + hh[:, 128:]
                lr[span] = hr[:, :128] + hr[:, 128:]
            last_ref[k * per : (k + 1) * per] = h * g
        ones = jnp.ones((8, 128), f32)
        sums = [dot(ones, a[...], 1, 1, lax.Precision.HIGHEST) for a in (square, lr, xr)]
        row = lax.broadcasted_iota(jnp.int32, (8, rows * CHUNKS), 0)
        stats_ref[...] = before_ref[...] + jnp.where(
            row == 0, sums[0], jnp.where(row == 1, sums[1], sums[2])
        )

    total = rows * CHUNKS
    return pl.pallas_call(
        kernel,
        out_shape=[
            jax.ShapeDtypeStruct((8, total), f32),
            jax.ShapeDtypeStruct((per * CHUNKS, 256), f32),
        ],
        in_specs=[VMEM] * 13,
        out_specs=[VMEM] * 2,
        scratch_shapes=[pltpu.VMEM((total, 128), f32)] * 3,
        compiler_params=params(16),
        name="second_layer",
        cost_estimate=small_cost,
    )(hidden, *lows, *stats, *halves, crossed, out_factors, decay, gain, reward, before)


def step_kernel(where, ins, outs):
    pops, blocks, k, lanes = ins.shape
    width = blocks * lanes

    def kernel(where_ref, ins_ref, outs_ref, mine_ref, theirs_ref, paired):
        xl = where_ref[4]
        layer = (lax.broadcasted_iota(jnp.int32, (k, lanes), 0) % 8) // 4
        for p in range(pops):
            at = slice(p * k, (p + 1) * k)
            for rel in range(2):
                o = outs_ref[p, xl ^ rel]
                zero = jnp.zeros_like(o)
                for l in range(2):
                    lo = (rel * 2 + l) * lanes
                    paired[at, lo : lo + lanes] = jnp.where(layer == l, o, zero)
        right = paired[...]
        for b in range(0, blocks, 2):
            left = jnp.concatenate(
                [
                    jnp.concatenate([ins_ref[p, b], ins_ref[p, b + 1]], axis=1)
                    for p in range(pops)
                ],
                axis=0,
            )
            out = dot(left, right, 0, 0)
            rows = slice(b * lanes, (b + 2) * lanes)
            for l in range(2):
                mine_ref[l, rows, :] = out[:, l * lanes : (l + 1) * lanes]
                theirs_ref[l, rows, :] = out[:, (2 + l) * lanes : (3 + l) * lanes].astype(bf16)

    return pl.pallas_call(
        kernel,
        out_shape=[
            jax.ShapeDtypeStruct((2, width, lanes), f32),
            jax.ShapeDtypeStruct((2, width, lanes), bf16),
        ],
        in_specs=[SMEM, VMEM, VMEM],
        out_specs=[VMEM, VMEM],
        scratch_shapes=[pltpu.VMEM((pops * k, 4 * lanes), bf16)],
        compiler_params=params(24),
        name="weight_step",
        cost_estimate=small_cost,
    )(where, ins, outs)


def shards(
    token_ids,
    fitness_ranks,
    embedding,
    mix_weights,
    factors_in,
    factors_out,
    decay_rates,
    norm_gain,
    reward_dir,
):
    members, seq_count, step_count = token_ids.shape
    vocab, width = embedding.shape
    full_width = mix_weights.shape[2]
    rank_count = factors_in.shape[2]
    pop_count = lax.axis_size(POP)
    members_all = members * pop_count
    coef = noise_scale * (full_width * rank_count) ** (-0.5)
    y, xl, z = (lax.axis_index(a) for a in POP)
    xh, c = (lax.axis_index(a) for a in MP)
    where = jnp.stack([z, xh, c, y, xl]).astype(jnp.int32)
    rows_all = members * seq_count * step_count

    order = token_ids.reshape(CHUNKS, -1, step_count).transpose(0, 2, 1).reshape(-1)
    onehot = (order[:, None] == jnp.arange(vocab, dtype=jnp.int32)[None, :]).astype(bf16)

    a_blocks = regroup(factors_in, "regroup_in", 0)
    ins_all = lax.all_gather(a_blocks, ("y", "z"))

    def added(a, b):
        return (a.astype(f32) + b.astype(f32)).astype(bf16)

    def sums_to_send(layer, lefts, first=0, count=4, dep=()):
        at = after(where, *dep) if dep else where
        peer, own = product(layer, 1, (1, 0), at, lefts, mix_weights, first, count)
        return added(own, swap(peer, "c"))

    def sums_to_keep(layer, lefts, dep):
        peer, own = product(layer, 0, (1, 0), after(where, *dep), lefts, mix_weights)
        return own, swap(peer, "c")

    lows = mp_parts(low_kernel(onehot, embedding, a_blocks))
    cross = sums_to_send(0, [embedding], dep=(lows[0],))
    table_cross = swap(cross, "xh")
    peer, own = product(0, 0, (1, 0), after(where, cross), [embedding], mix_weights)
    keep = jnp.concatenate([swap(peer[:2], "c"), swap(peer[2:], "c")])
    first_table = [own, keep, table_cross]

    b_blocks = regroup(after(factors_out, cross), "regroup_out", 0)
    b_own = lax.dynamic_slice_in_dim(b_blocks, (xh * 2 + c) * 8, 8, 0)

    decay = [decay_rates[l : l + 1] for l in range(2)]
    gain = [norm_gain[l : l + 1] for l in range(2)]
    lifted, stats = [], []
    for k in range(CHUNKS):
        up, st = first_layer(
            k, where, coef, onehot, first_table, lows, b_own, a_blocks, decay[0], gain[0]
        )
        lifted.append(up)
        stats.append(st)
    stats = mp_parts(jnp.concatenate(stats, axis=1))
    hidden = next_hidden(full_width, onehot, embedding, stats, lifted)
    sent, parts = [], []
    for n in range(4):
        part = sums_to_send(1, [hidden], n, 1, parts[n - 2 : n - 1] if n > 1 else ())
        parts.append(part)
        sent.append(swap(part, "xh"))
    halves = sums_to_keep(1, [hidden], (part,))

    half_rows = b_blocks.shape[1] // 2
    my_rows = lax.dynamic_slice_in_dim(b_blocks, c * half_rows, half_rows, 1)
    digits = jnp.stack([fitness_ranks // 32, fitness_ranks % 32]).astype(bf16)
    digits = jnp.pad(digits, ((0, 6), (0, 128 - members)))
    digits = jnp.broadcast_to(digits[None], (pop_count, 8, 128))
    packed = jnp.concatenate([my_rows, digits], axis=1)
    packed = packed.reshape(4, 2, 4, -1, 128).transpose(0, 2, 1, 3, 4).reshape(16, 2, -1, 128)
    arrived = lax.all_to_all(after(packed, part), ("y", "z"), 0, 0, tiled=True)
    mine = arrived[:, :, :half_rows]
    digits_all = arrived[:, 0, half_rows : half_rows + 2, :members].astype(f32)
    ranks_here = digits_all[:, 0] * 32.0 + digits_all[:, 1]
    ranks_there = swap(ranks_here, "xl")
    theirs = swap(mine, "c")
    outs = jnp.where(
        c == 0, jnp.concatenate([mine, theirs], axis=2), jnp.concatenate([theirs, mine], axis=2)
    )
    shares = ranks_here / members_all
    shares_there = ranks_there / members_all
    rank_mean = (jnp.sum(shares) + jnp.sum(shares_there)) / members_all
    spread_sum = jnp.sum((shares - rank_mean) ** 2) + jnp.sum((shares_there - rank_mean) ** 2)
    shaped = (shares - rank_mean) * lax.rsqrt(spread_sum / members_all + spread_eps)
    shaped = shaped * (members_all * rank_count) ** (-0.5)
    shaped_rows = jnp.repeat(shaped, 2 * rank_count, axis=1)
    outs = (outs.astype(f32) * shaped_rows[:, None, :, None]).astype(bf16)
    step_mine, step_theirs = step_kernel(where, ins_all, outs)

    st = jnp.zeros((8, rows_all), f32)
    lasts = []
    for n in range(4):
        st, last = second_layer(
            n, coef, full_width, hidden, lows, stats, halves, sent[n], b_own,
            decay[1], gain[1], reward_dir[None], st,
        )
        lasts.append(last)
    weight_step = step_mine + swap(after(step_theirs, sent[3]), "xl").astype(f32)
    so_far = sum(mp_parts(st))
    norm = lax.rsqrt(so_far[0] / full_width + norm_eps)
    terms = (so_far[2] + norm * so_far[1]).reshape(CHUNKS, step_count, -1)
    tail = norm.reshape(CHUNKS, step_count, -1)[:, -1].reshape(-1)
    last_hidden = hidden.reshape(CHUNKS, step_count, -1, width)[:, -1].reshape(-1, width)
    finals = last_hidden.astype(f32) + jnp.concatenate(lasts, axis=1) * tail[:, None]
    final_features = finals.astype(bf16).reshape(members, seq_count, width)
    scores = jnp.mean(terms, axis=1).reshape(members, seq_count) * full_width ** (-0.5)
    return (final_features, scores, weight_step)


def solution(mesh):
    fine = Mesh(mesh.devices.reshape(4, 2, 4, 2, 2), POP + MP)
    return jax.shard_map(
        shards,
        mesh=fine,
        in_specs=(
            P(POP, None, None),
            P(POP),
            P(None, MP),
            P(None, MP, None),
            P(None, POP, None, MP),
            P(None, POP, None, None),
            P(None, MP),
            P(None, MP),
            P(MP),
        ),
        out_specs=(P(POP, None, MP), P(POP, None), P(None, MP, POP)),
        check_vma=False,
    )
```

```python
import jax
import jax.numpy as jnp
from jax import lax
from jax.experimental import pallas as pl
from jax.experimental.pallas import tpu as pltpu
from jax.sharding import Mesh
from jax.sharding import PartitionSpec as P

noise_scale = 0.25
norm_eps = 1e-06
spread_eps = 1e-05

POP = ("y", "xl", "z")
MP = ("xh", "c")
CHUNKS = 3
f32 = jnp.float32
bf16 = jnp.bfloat16
SMEM = pl.BlockSpec(memory_space=pltpu.SMEM)
VMEM = pl.BlockSpec(memory_space=pltpu.VMEM)
small_cost = pl.CostEstimate(flops=1000, bytes_accessed=1000, transcendentals=0)


def params(mib=24):
    return pltpu.CompilerParams(vmem_limit_bytes=mib * 1024 * 1024)


def swap(value, axis):
    return lax.ppermute(value, axis, [(0, 1), (1, 0)])


def after(value, *earlier):
    return lax.optimization_barrier((value, *earlier))[0]


def mp_parts(value):
    pair = value + swap(value, "c")
    return pair, swap(pair, "xh")


def dot(a, b, ca, cb, precision=None):
    return lax.dot_general(
        a, b, (((ca,), (cb,)), ((), ())), preferred_element_type=f32, precision=precision
    )


def pack(where, digits, factors_in, factors_out, pops):
    layers, members, ranks, width = factors_in.shape
    k = members * layers * ranks
    half = members // 2
    blocks = width // 128
    part = k // 2 + 8
    rows = blocks * k + 2 * part

    def kernel(where_ref, digits_ref, in_ref, out_ref, a_ref, b_ref, packed_ref):
        own = pl.multiple_of((where_ref[1] * 2 + where_ref[2]) * width, width)
        c = where_ref[2]

        def member(ref, m, cols):
            return jnp.concatenate(
                [ref[l, m, :, cols].astype(f32) for l in range(layers)], axis=0
            ).astype(bf16)

        for m in range(members):
            a = member(in_ref, m, slice(None))
            b = member(out_ref, m, pl.ds(own, width))
            at = slice(m * 8, m * 8 + 8)
            for n in range(blocks):
                a_ref[n, at, :] = a[:, n * 128 : (n + 1) * 128]
                b_ref[n, at, :] = b[:, n * 128 : (n + 1) * 128]
        for m in range(half):
            b = member(out_ref, c * half + m, slice(None))
            for o in range(2 * pops):
                y, x, z = o // 8, (o // 4) % 2, o % 4
                lo = blocks * k + x * part + m * 8
                packed_ref[y * 4 + z, lo : lo + 8, :] = b[:, o * 128 : (o + 1) * 128]
        for p in range(pops):
            for n in range(blocks):
                packed_ref[p, n * k : (n + 1) * k, :] = a_ref[n]
            for x in range(2):
                lo = blocks * k + x * part + k // 2
                packed_ref[p, lo : lo + 8, :] = digits_ref[...]

    return pl.pallas_call(
        kernel,
        out_shape=[
            jax.ShapeDtypeStruct((blocks, k, 128), bf16),
            jax.ShapeDtypeStruct((blocks, k, 128), bf16),
            jax.ShapeDtypeStruct((pops, rows, 128), bf16),
        ],
        in_specs=[SMEM] + [VMEM] * 3,
        out_specs=[VMEM] * 3,
        compiler_params=params(16),
        name="pack",
        cost_estimate=small_cost,
    )(where, digits, factors_in, factors_out)


def product(layer, rel, where, left, weights, piece, first=0, count=1):
    rows, width = left.shape
    per_owner = width // piece

    def kernel(where_ref, left_ref, w0_ref, w1_ref, out0_ref, out1_ref):
        for w_ref, out_ref in ((w0_ref, out0_ref), (w1_ref, out1_ref)):
            out_ref[0] = jnp.dot(
                left_ref[...], w_ref[0], preferred_element_type=f32
            ).astype(bf16)

    def block(flip):
        def at(n, s):
            return (layer, 0, ((s[1] ^ rel) * 2 + (s[2] ^ flip)) * per_owner + first + n)

        return pl.BlockSpec((1, width, piece), at)

    return pl.pallas_call(
        kernel,
        grid_spec=pltpu.PrefetchScalarGridSpec(
            num_scalar_prefetch=1,
            grid=(count,),
            in_specs=[VMEM, block(1), block(0)],
            out_specs=[pl.BlockSpec((1, rows, piece), lambda n, s: (n, 0, 0))] * 2,
        ),
        out_shape=[jax.ShapeDtypeStruct((count, rows, piece), bf16)] * 2,
        compiler_params=params(48),
        name="product",
        cost_estimate=small_cost,
    )(where, left, weights, weights)


def member_of(shape, per, dim):
    return lax.broadcasted_iota(jnp.int32, shape, dim) // per


def low_kernel(onehot, embedding, factors):
    rows = onehot.shape[0]
    per_chunk = rows // CHUNKS
    group = factors.shape[1] // CHUNKS

    def kernel(o_ref, e_ref, a_ref, out_ref):
        for k in range(CHUNKS):
            x = jnp.dot(
                o_ref[k * per_chunk : (k + 1) * per_chunk, :], e_ref[...], preferred_element_type=f32
            ).astype(bf16)
            total = jnp.zeros((group, per_chunk), f32)
            for b in range(factors.shape[0]):
                total += dot(
                    a_ref[b, k * group : (k + 1) * group, :], x[:, b * 128 : (b + 1) * 128], 1, 1
                )
            out_ref[:, k * per_chunk : (k + 1) * per_chunk] = diagonal(total)

    return pl.pallas_call(
        kernel,
        out_shape=jax.ShapeDtypeStruct((8, rows), f32),
        in_specs=[VMEM] * 3,
        out_specs=VMEM,
        compiler_params=params(),
        name="low",
        cost_estimate=small_cost,
    )(onehot, embedding, factors)


def diagonal(total):
    group, cols = total.shape
    row_member = member_of((group, cols), 8, 0)
    col_member = (lax.broadcasted_iota(jnp.int32, (group, cols), 1) % 16) // 4
    kept = jnp.where(row_member == col_member, total, 0.0)
    out = kept[0:8]
    for m in range(1, group // 8):
        out = out + kept[m * 8 : (m + 1) * 8]
    return out


def spread(low, layer, group):
    cols = low.shape[1]
    row = lax.broadcasted_iota(jnp.int32, (group, cols), 0)
    col_member = (lax.broadcasted_iota(jnp.int32, (group, cols), 1) % 16) // 4
    keep = (row // 8 == col_member) & ((row % 8) // 4 == layer)
    tiled = jnp.concatenate([low] * (group // 8), axis=0)
    return jnp.where(keep, tiled, 0.0).astype(bf16)


def first_layer(chunk, where, coef, onehot, table_parts, lows, out_factors, in_factors, decay, gain):
    rows = onehot.shape[0] // CHUNKS
    group = out_factors.shape[1] // CHUNKS
    width = decay.shape[1]
    steps = 16
    per = rows // steps

    def kernel(o_ref, t0, t1, t2, l0, l1, b_ref, a_ref, d_ref, g_ref, lifted_ref, stats_ref, square):
        at = slice(chunk * rows, (chunk + 1) * rows)
        mine = slice(chunk * group, (chunk + 1) * group)
        low = (l0[:, at] + l1[:, at]) * coef
        spread_low = spread(low, 0, group)
        total = jnp.zeros((group, rows), f32)
        for n in range(width // 256):
            cols = slice(n * 256, (n + 1) * 256)
            in_half = slice(n % 2 * 256, n % 2 * 256 + 256)
            table = sum(t[n // 2, :, in_half].astype(f32) for t in (t0, t1, t2)).astype(bf16)
            factor = jnp.concatenate([b_ref[2 * n, mine], b_ref[2 * n + 1, mine]], axis=1)
            u = jnp.dot(o_ref[at], table, preferred_element_type=f32) + dot(
                spread_low, factor, 0, 0
            )
            d = d_ref[:, cols]
            g = g_ref[:, cols]
            rest = 1.0 - d
            h = jnp.zeros((per, 256), f32)
            for t in range(steps):
                span = slice(t * per, (t + 1) * per)
                h = d * h + rest * u[span]
                lifted_ref[span, cols] = (h * g).astype(bf16)
                hh = h * h
                hh = hh[:, :128] + hh[:, 128:]
                if n == 0:
                    square[span] = hh
                else:
                    square[span] += hh
            factor_in = jnp.concatenate([a_ref[2 * n, mine], a_ref[2 * n + 1, mine]], axis=1)
            total += dot(factor_in, lifted_ref[:, cols], 1, 1)
        sums = dot(jnp.ones((8, 128), f32), square[...], 1, 1, lax.Precision.HIGHEST)
        low_next = diagonal(total)
        row = lax.broadcasted_iota(jnp.int32, (8, rows), 0)
        stats_ref[...] = jnp.where(row < 4, sums, low_next)

    return pl.pallas_call(
        kernel,
        out_shape=[
            jax.ShapeDtypeStruct((rows, width), bf16),
            jax.ShapeDtypeStruct((8, rows), f32),
        ],
        in_specs=[VMEM] * 10,
        out_specs=[VMEM, VMEM],
        scratch_shapes=[pltpu.VMEM((rows, 128), f32)],
        compiler_params=params(16),
        name="first_layer",
        cost_estimate=small_cost,
    )(onehot, *table_parts, *lows, out_factors, in_factors, decay, gain)


def next_hidden(full_width, onehot, embedding, stats, lifted):
    rows = lifted[0].shape[0]
    total, width = rows * CHUNKS, embedding.shape[1]

    def kernel(o_ref, e_ref, s0, s1, up0, up1, up2, out_ref, last_ref):
        for k, up in enumerate((up0, up1, up2)):
            span = slice(k * rows, (k + 1) * rows)
            so_far = s0[:, span] + s1[:, span]
            norm = lax.rsqrt(so_far / full_width + norm_eps)
            norm_col = jnp.transpose(norm)[:, 0:1]
            x = jnp.dot(o_ref[span], e_ref[...], preferred_element_type=f32)
            x = (x + norm_col * up[...].astype(f32)).astype(bf16)
            out_ref[span] = x
            per = rows // 16
            last_ref[k * per : (k + 1) * per] = x[rows - per :].astype(f32)

    return pl.pallas_call(
        kernel,
        out_shape=[
            jax.ShapeDtypeStruct((total, width), bf16),
            jax.ShapeDtypeStruct((total // 16, width), f32),
        ],
        in_specs=[VMEM] * 7,
        out_specs=[VMEM] * 2,
        compiler_params=params(16),
        name="next_hidden",
        cost_estimate=small_cost,
    )(onehot, embedding, *stats, *lifted)


def second_layer(n, coef, full_width, hidden, lows, stats, halves, crossed, out_factors,
                 decay, gain, reward, before):
    rows = hidden.shape[0] // CHUNKS
    group = out_factors.shape[1] // CHUNKS
    steps = 16
    per = rows // steps
    cols = slice(n * 256, (n + 1) * 256)

    def kernel(x_ref, l0, l1, s0, s1, own_ref, peer_ref, other_ref, b_ref, d_ref, g_ref, r_ref,
               before_ref, stats_ref, last_ref, square, lr, xr):
        factor = jnp.concatenate([b_ref[2 * n], b_ref[2 * n + 1]], axis=1)
        d = d_ref[:, cols]
        g = g_ref[:, cols]
        r = r_ref[:, cols]
        rest = 1.0 - d
        gr = g * r
        for k in range(CHUNKS):
            span_k = slice(k * rows, (k + 1) * rows)
            so_far = s0[:, span_k] + s1[:, span_k]
            norm = lax.rsqrt(so_far[0:1] / full_width + norm_eps)
            low = (l0[:, span_k] + l1[:, span_k] + norm * so_far) * coef
            spread_low = spread(low, 1, group)
            u = dot(spread_low, factor[k * group : (k + 1) * group], 0, 0) + (
                own_ref[0, span_k].astype(f32)
                + peer_ref[0, span_k].astype(f32)
                + other_ref[0, span_k].astype(f32)
            )
            h = jnp.zeros((per, 256), f32)
            xrr = x_ref[span_k, cols].astype(f32) * r
            xr[span_k] = xrr[:, :128] + xrr[:, 128:]
            for t in range(steps):
                span = slice(k * rows + t * per, k * rows + (t + 1) * per)
                h = d * h + rest * u[t * per : (t + 1) * per]
                hr = h * gr
                hh = h * h
                square[span] = hh[:, :128] + hh[:, 128:]
                lr[span] = hr[:, :128] + hr[:, 128:]
            last_ref[k * per : (k + 1) * per] = h * g
        ones = jnp.ones((8, 128), f32)
        sums = [dot(ones, a[...], 1, 1, lax.Precision.HIGHEST) for a in (square, lr, xr)]
        row = lax.broadcasted_iota(jnp.int32, (8, rows * CHUNKS), 0)
        stats_ref[...] = before_ref[...] + jnp.where(
            row == 0, sums[0], jnp.where(row == 1, sums[1], sums[2])
        )

    total = rows * CHUNKS
    return pl.pallas_call(
        kernel,
        out_shape=[
            jax.ShapeDtypeStruct((8, total), f32),
            jax.ShapeDtypeStruct((per * CHUNKS, 256), f32),
        ],
        in_specs=[VMEM] * 13,
        out_specs=[VMEM] * 2,
        scratch_shapes=[pltpu.VMEM((total, 128), f32)] * 3,
        compiler_params=params(16),
        name="second_layer",
        cost_estimate=small_cost,
    )(hidden, *lows, *stats, *halves, crossed, out_factors, decay, gain, reward, before)


def step_kernel(where, arrived, arrived_peer, members, members_all, scale):
    pops, rows, lanes = arrived.shape
    k = members * 8
    part = k // 2 + 8
    blocks = (rows - 2 * part) // k
    width = blocks * lanes

    def kernel(where_ref, in_ref, peer_ref, mine_ref, theirs_ref, paired, digit_rows):
        xl, c = where_ref[4], where_ref[2]
        head = blocks * k
        for p in range(pops):
            digits = in_ref[p, head + k // 2 : head + k // 2 + 8, :].astype(f32)
            for i in range(4):
                digit_rows[i, p : p + 1, :] = digits[i : i + 1, :]
        lane = lax.broadcasted_iota(jnp.int32, (pops, lanes), 1)
        real = lane < members
        here = (digit_rows[0] * 32.0 + digit_rows[1]) / members_all
        there = (digit_rows[2] * 32.0 + digit_rows[3]) / members_all
        mean = (
            jnp.sum(jnp.where(real, here, 0.0), keepdims=True)
            + jnp.sum(jnp.where(real, there, 0.0), keepdims=True)
        ) / members_all
        here = jnp.where(real, here - mean, 0.0)
        there = jnp.where(real, there - mean, 0.0)
        var = (
            jnp.sum(here * here, keepdims=True) + jnp.sum(there * there, keepdims=True)
        ) / members_all
        shaped = here * (lax.rsqrt(var + spread_eps) * scale)
        pick = lax.broadcasted_iota(jnp.int32, (k, lanes), 0) // 8 == lax.broadcasted_iota(
            jnp.int32, (k, lanes), 1
        )
        by_row = dot(pick.astype(f32), shaped, 1, 1, lax.Precision.HIGHEST)
        layer = (lax.broadcasted_iota(jnp.int32, (k, lanes), 0) % 8) // 4
        for p in range(pops):
            at = slice(p * k, (p + 1) * k)
            for rel in range(2):
                lo = pl.multiple_of((xl ^ rel) * part, 8)
                mine = in_ref[p, pl.ds(head + lo, k // 2), :].astype(f32)
                theirs = peer_ref[p, pl.ds(lo, k // 2), :].astype(f32)
                o = jnp.concatenate(
                    [jnp.where(c == 0, mine, theirs), jnp.where(c == 0, theirs, mine)], axis=0
                )
                o = o * by_row[:, p : p + 1]
                for l in range(2):
                    col = (rel * 2 + l) * lanes
                    paired[at, col : col + lanes] = jnp.where(layer == l, o, 0.0).astype(bf16)
        right = paired[...]
        for b in range(0, blocks, 2):
            left = jnp.concatenate(
                [
                    jnp.concatenate(
                        [in_ref[p, b * k : (b + 1) * k, :], in_ref[p, (b + 1) * k : (b + 2) * k, :]],
                        axis=1,
                    )
                    for p in range(pops)
                ],
                axis=0,
            )
            out = dot(left, right, 0, 0)
            span = slice(b * lanes, (b + 2) * lanes)
            for l in range(2):
                mine_ref[l, span, :] = out[:, l * lanes : (l + 1) * lanes]
                theirs_ref[l, span, :] = out[:, (2 + l) * lanes : (3 + l) * lanes].astype(bf16)

    return pl.pallas_call(
        kernel,
        out_shape=[
            jax.ShapeDtypeStruct((2, width, lanes), f32),
            jax.ShapeDtypeStruct((2, width, lanes), bf16),
        ],
        in_specs=[SMEM, VMEM, VMEM],
        out_specs=[VMEM, VMEM],
        scratch_shapes=[
            pltpu.VMEM((pops * k, 4 * lanes), bf16),
            pltpu.VMEM((4, pops, lanes), f32),
        ],
        compiler_params=params(24),
        name="weight_step",
        cost_estimate=small_cost,
    )(where, arrived, arrived_peer)


def shards(
    token_ids,
    fitness_ranks,
    embedding,
    mix_weights,
    factors_in,
    factors_out,
    decay_rates,
    norm_gain,
    reward_dir,
):
    members, seq_count, step_count = token_ids.shape
    vocab, width = embedding.shape
    full_width = mix_weights.shape[2]
    rank_count = factors_in.shape[2]
    pop_count = lax.axis_size(POP)
    members_all = members * pop_count
    coef = noise_scale * (full_width * rank_count) ** (-0.5)
    y, xl, z = (lax.axis_index(a) for a in POP)
    xh, c = (lax.axis_index(a) for a in MP)
    where = jnp.stack([z, xh, c, y, xl]).astype(jnp.int32)
    rows_all = members * seq_count * step_count

    order = token_ids.reshape(CHUNKS, -1, step_count).transpose(0, 2, 1).reshape(-1)
    onehot = (order[:, None] == jnp.arange(vocab, dtype=jnp.int32)[None, :]).astype(bf16)

    def added(a, b):
        return (a.astype(f32) + b.astype(f32)).astype(bf16)

    peer, own = product(0, 1, where, embedding, mix_weights, 512, 0, 2)
    cross = added(own, swap(peer, "c"))
    table_cross = swap(cross, "xh")
    both = jnp.stack([fitness_ranks, swap(fitness_ranks, "xl")])
    digits = jnp.stack([both[0] // 32, both[0] % 32, both[1] // 32, both[1] % 32]).astype(bf16)
    digits = jnp.pad(digits, ((0, 4), (0, 128 - members)))
    pops = lax.axis_size("y") * lax.axis_size("z")
    a_blocks, b_own, packed = pack(
        after(where, peer), digits, factors_in, factors_out, pops
    )
    lows = mp_parts(low_kernel(after(onehot, peer), embedding, a_blocks))
    peer, own = product(0, 0, after(where, cross, lows[0]), embedding, mix_weights, 512, 0, 2)
    keep = jnp.concatenate([swap(peer[:1], "c"), swap(peer[1:], "c")])
    first_table = [own, keep, table_cross]
    arrived = lax.all_to_all(after(packed, own), ("y", "z"), 0, 0, tiled=True)

    decay = [decay_rates[l : l + 1] for l in range(2)]
    gain = [norm_gain[l : l + 1] for l in range(2)]
    lifted, stats = [], []
    for k in range(CHUNKS):
        up, st = first_layer(
            k, where, coef, onehot, first_table, lows, b_own, a_blocks, decay[0], gain[0]
        )
        lifted.append(up)
        stats.append(st)
    stats = mp_parts(jnp.concatenate(stats, axis=1))
    hidden, last_hidden = next_hidden(full_width, onehot, embedding, stats, lifted)
    sent, parts, halves = [], [], []
    for n in range(4):
        at = after(where, parts[n - 2]) if n > 1 else where
        peer, own = product(1, 1, at, hidden, mix_weights, 256, n)
        parts.append(added(own, swap(peer, "c")))
        sent.append(swap(parts[n], "xh"))
    for n in range(4):
        at = after(where, sent[n - 1]) if n > 0 else after(where, parts[3])
        peer, own = product(1, 0, at, hidden, mix_weights, 256, n)
        halves.append((own, swap(peer, "c")))

    outs_rows = 2 * (members * rank_count + 8)
    arrived = after(arrived, sent[2])
    arrived_peer = swap(arrived[:, -outs_rows:], "c")
    step_mine, step_theirs = step_kernel(
        where, arrived, arrived_peer, members, members_all, (members_all * rank_count) ** (-0.5)
    )

    st = jnp.zeros((8, rows_all), f32)
    lasts = []
    for n in range(4):
        if n == 3:
            st = after(st, step_theirs)
        st, last = second_layer(
            n, coef, full_width, hidden, lows, stats, halves[n], sent[n], b_own,
            decay[1], gain[1], reward_dir[None], st,
        )
        lasts.append(last)
    weight_step = step_mine + swap(after(step_theirs, sent[3]), "xl").astype(f32)
    so_far = sum(mp_parts(st))
    norm = lax.rsqrt(so_far[0] / full_width + norm_eps)
    terms = (so_far[2] + norm * so_far[1]).reshape(CHUNKS, step_count, -1)
    tail = norm.reshape(CHUNKS, step_count, -1)[:, -1].reshape(-1)
    finals = last_hidden + jnp.concatenate(lasts, axis=1) * tail[:, None]
    final_features = finals.astype(bf16).reshape(members, seq_count, width)
    scores = jnp.mean(terms, axis=1).reshape(members, seq_count) * full_width ** (-0.5)
    return (final_features, scores, weight_step)


def solution(mesh):
    fine = Mesh(mesh.devices.reshape(4, 2, 4, 2, 2), POP + MP)
    return jax.shard_map(
        shards,
        mesh=fine,
        in_specs=(
            P(POP, None, None),
            P(POP),
            P(None, MP),
            P(None, MP, None),
            P(None, POP, None, MP),
            P(None, POP, None, None),
            P(None, MP),
            P(None, MP),
            P(MP),
        ),
        out_specs=(P(POP, None, MP), P(POP, None), P(None, MP, POP)),
        check_vma=False,
    )
```

```python
import jax
import jax.numpy as jnp
from jax import lax
from jax.experimental import pallas as pl
from jax.experimental.pallas import tpu as pltpu
from jax.sharding import Mesh
from jax.sharding import PartitionSpec as P

noise_scale = 0.25
norm_eps = 1e-06
spread_eps = 1e-05

POP = ("y", "xl", "z")
MP = ("xh", "c")
CHUNKS = 3
f32 = jnp.float32
bf16 = jnp.bfloat16
SMEM = pl.BlockSpec(memory_space=pltpu.SMEM)
VMEM = pl.BlockSpec(memory_space=pltpu.VMEM)
small_cost = pl.CostEstimate(flops=1000, bytes_accessed=1000, transcendentals=0)


def params(mib=24):
    return pltpu.CompilerParams(vmem_limit_bytes=mib * 1024 * 1024)


def swap(value, axis):
    return lax.ppermute(value, axis, [(0, 1), (1, 0)])


def after(value, *earlier):
    return lax.optimization_barrier((value, *earlier))[0]


def mp_parts(value):
    pair = value + swap(value, "c")
    return pair, swap(pair, "xh")


def dot(a, b, ca, cb, precision=None):
    return lax.dot_general(
        a, b, (((ca,), (cb,)), ((), ())), preferred_element_type=f32, precision=precision
    )


def pack(where, digits, factors_in, factors_out, pops):
    layers, members, ranks, width = factors_in.shape
    k = members * layers * ranks
    half = members // 2
    blocks = width // 128
    part = k // 2 + 8
    rows = blocks * k + 2 * part

    def kernel(where_ref, digits_ref, in_ref, out_ref, a_ref, b_ref, packed_ref):
        own = pl.multiple_of((where_ref[1] * 2 + where_ref[2]) * width, width)
        c = where_ref[2]

        def member(ref, m, cols):
            return jnp.concatenate(
                [ref[l, m, :, cols].astype(f32) for l in range(layers)], axis=0
            ).astype(bf16)

        for m in range(members):
            a = member(in_ref, m, slice(None))
            b = member(out_ref, m, pl.ds(own, width))
            at = slice(m * 8, m * 8 + 8)
            for n in range(blocks):
                a_ref[n, at, :] = a[:, n * 128 : (n + 1) * 128]
                b_ref[n, at, :] = b[:, n * 128 : (n + 1) * 128]
        for m in range(half):
            b = member(out_ref, c * half + m, slice(None))
            for o in range(2 * pops):
                y, x, z = o // 8, (o // 4) % 2, o % 4
                lo = blocks * k + x * part + m * 8
                packed_ref[y * 4 + z, lo : lo + 8, :] = b[:, o * 128 : (o + 1) * 128]
        for p in range(pops):
            for n in range(blocks):
                packed_ref[p, n * k : (n + 1) * k, :] = a_ref[n]
            for x in range(2):
                lo = blocks * k + x * part + k // 2
                packed_ref[p, lo : lo + 8, :] = digits_ref[...]

    return pl.pallas_call(
        kernel,
        out_shape=[
            jax.ShapeDtypeStruct((blocks, k, 128), bf16),
            jax.ShapeDtypeStruct((blocks, k, 128), bf16),
            jax.ShapeDtypeStruct((pops, rows, 128), bf16),
        ],
        in_specs=[SMEM] + [VMEM] * 3,
        out_specs=[VMEM] * 3,
        compiler_params=params(16),
        name="pack",
        cost_estimate=small_cost,
    )(where, digits, factors_in, factors_out)


def product(layer, where, left, weights, piece):
    rows, width = left.shape
    per_owner = width // piece

    def kernel(where_ref, left_ref, w0_ref, w1_ref, out0_ref, out1_ref):
        for w_ref, out_ref in ((w0_ref, out0_ref), (w1_ref, out1_ref)):
            out_ref[0] = jnp.dot(
                left_ref[...], w_ref[0], preferred_element_type=f32
            ).astype(bf16)

    def block(flip):
        def at(i, s):
            half = s[1] ^ (1 - i // per_owner)
            return (layer, 0, (half * 2 + (s[2] ^ flip)) * per_owner + i % per_owner)

        return pl.BlockSpec((1, width, piece), at)

    count = 2 * per_owner
    return pl.pallas_call(
        kernel,
        grid_spec=pltpu.PrefetchScalarGridSpec(
            num_scalar_prefetch=1,
            grid=(count,),
            in_specs=[VMEM, block(1), block(0)],
            out_specs=[pl.BlockSpec((1, rows, piece), lambda i, s: (i, 0, 0))] * 2,
        ),
        out_shape=[jax.ShapeDtypeStruct((count, rows, piece), bf16)] * 2,
        compiler_params=params(48),
        name="product",
        cost_estimate=small_cost,
    )(where, left, weights, weights)


def stay(layer, weights):
    _, width, full = weights.shape
    cuts = 8
    rows = width // cuts

    def kernel(w_ref, out_ref, sems):
        def part(i):
            span = slice(i * rows, (i + 1) * rows)
            return pltpu.make_async_copy(w_ref.at[layer, span], out_ref.at[span], sems.at[i])

        for i in range(cuts):
            part(i).start()
        for i in range(cuts):
            part(i).wait()

    return pl.pallas_call(
        kernel,
        out_shape=jax.ShapeDtypeStruct((width, full), bf16),
        in_specs=[pl.BlockSpec(memory_space=pltpu.HBM)],
        out_specs=VMEM,
        scratch_shapes=[pltpu.SemaphoreType.DMA((cuts,))],
        compiler_params=params(40),
        name="stay",
        cost_estimate=small_cost,
    )(weights)


def dense(rel, where, left, weights, piece, first=0, count=1, earlier=()):
    rows, width = left.shape

    def kernel(where_ref, left_ref, w_ref, *refs):
        out0_ref, out1_ref = refs[len(earlier) :]
        for flip, out_ref in ((1, out0_ref), (0, out1_ref)):
            owner = (where_ref[1] ^ rel) * 2 + (where_ref[2] ^ flip)
            for n in range(count):
                at = pl.multiple_of(owner * width + (first + n) * piece, piece)
                out_ref[n] = jnp.dot(
                    left_ref[...], w_ref[:, pl.ds(at, piece)], preferred_element_type=f32
                ).astype(bf16)

    return pl.pallas_call(
        kernel,
        out_shape=[jax.ShapeDtypeStruct((count, rows, piece), bf16)] * 2,
        in_specs=[SMEM, VMEM, VMEM] + [pl.BlockSpec(memory_space=pl.ANY)] * len(earlier),
        out_specs=[VMEM] * 2,
        compiler_params=params(16),
        name="dense",
        cost_estimate=small_cost,
    )(where, left, weights, *earlier)


def member_of(shape, per, dim):
    return lax.broadcasted_iota(jnp.int32, shape, dim) // per


def low_kernel(onehot, embedding, factors):
    rows = onehot.shape[0]
    per_chunk = rows // CHUNKS
    group = factors.shape[1] // CHUNKS

    def kernel(o_ref, e_ref, a_ref, out_ref):
        for k in range(CHUNKS):
            x = jnp.dot(
                o_ref[k * per_chunk : (k + 1) * per_chunk, :], e_ref[...], preferred_element_type=f32
            ).astype(bf16)
            total = jnp.zeros((group, per_chunk), f32)
            for b in range(factors.shape[0]):
                total += dot(
                    a_ref[b, k * group : (k + 1) * group, :], x[:, b * 128 : (b + 1) * 128], 1, 1
                )
            out_ref[:, k * per_chunk : (k + 1) * per_chunk] = diagonal(total)

    return pl.pallas_call(
        kernel,
        out_shape=jax.ShapeDtypeStruct((8, rows), f32),
        in_specs=[VMEM] * 3,
        out_specs=VMEM,
        compiler_params=params(),
        name="low",
        cost_estimate=small_cost,
    )(onehot, embedding, factors)


def diagonal(total):
    group, cols = total.shape
    row_member = member_of((group, cols), 8, 0)
    col_member = (lax.broadcasted_iota(jnp.int32, (group, cols), 1) % 16) // 4
    kept = jnp.where(row_member == col_member, total, 0.0)
    out = kept[0:8]
    for m in range(1, group // 8):
        out = out + kept[m * 8 : (m + 1) * 8]
    return out


def spread(low, layer, group):
    cols = low.shape[1]
    row = lax.broadcasted_iota(jnp.int32, (group, cols), 0)
    col_member = (lax.broadcasted_iota(jnp.int32, (group, cols), 1) % 16) // 4
    keep = (row // 8 == col_member) & ((row % 8) // 4 == layer)
    tiled = jnp.concatenate([low] * (group // 8), axis=0)
    return jnp.where(keep, tiled, 0.0).astype(bf16)


def first_layer(chunk, where, coef, onehot, table_parts, lows, out_factors, in_factors, decay, gain):
    rows = onehot.shape[0] // CHUNKS
    group = out_factors.shape[1] // CHUNKS
    width = decay.shape[1]
    steps = 16
    per = rows // steps

    def kernel(o_ref, t0, t1, t2, l0, l1, b_ref, a_ref, d_ref, g_ref, lifted_ref, stats_ref, square):
        at = slice(chunk * rows, (chunk + 1) * rows)
        mine = slice(chunk * group, (chunk + 1) * group)
        low = (l0[:, at] + l1[:, at]) * coef
        spread_low = spread(low, 0, group)
        total = jnp.zeros((group, rows), f32)
        for n in range(width // 256):
            cols = slice(n * 256, (n + 1) * 256)
            in_half = slice(n % 2 * 256, n % 2 * 256 + 256)
            parts = (t0[2 + n // 2, :, in_half], t1[2 + n // 2, :, in_half], t2[n // 2, :, in_half])
            table = sum(p.astype(f32) for p in parts).astype(bf16)
            factor = jnp.concatenate([b_ref[2 * n, mine], b_ref[2 * n + 1, mine]], axis=1)
            u = jnp.dot(o_ref[at], table, preferred_element_type=f32) + dot(
                spread_low, factor, 0, 0
            )
            d = d_ref[:, cols]
            g = g_ref[:, cols]
            rest = 1.0 - d
            h = jnp.zeros((per, 256), f32)
            for t in range(steps):
                span = slice(t * per, (t + 1) * per)
                h = d * h + rest * u[span]
                lifted_ref[span, cols] = (h * g).astype(bf16)
                hh = h * h
                hh = hh[:, :128] + hh[:, 128:]
                if n == 0:
                    square[span] = hh
                else:
                    square[span] += hh
            factor_in = jnp.concatenate([a_ref[2 * n, mine], a_ref[2 * n + 1, mine]], axis=1)
            total += dot(factor_in, lifted_ref[:, cols], 1, 1)
        sums = dot(jnp.ones((8, 128), f32), square[...], 1, 1, lax.Precision.HIGHEST)
        low_next = diagonal(total)
        row = lax.broadcasted_iota(jnp.int32, (8, rows), 0)
        stats_ref[...] = jnp.where(row < 4, sums, low_next)

    return pl.pallas_call(
        kernel,
        out_shape=[
            jax.ShapeDtypeStruct((rows, width), bf16),
            jax.ShapeDtypeStruct((8, rows), f32),
        ],
        in_specs=[VMEM] * 10,
        out_specs=[VMEM, VMEM],
        scratch_shapes=[pltpu.VMEM((rows, 128), f32)],
        compiler_params=params(16),
        name="first_layer",
        cost_estimate=small_cost,
    )(onehot, *table_parts, *lows, out_factors, in_factors, decay, gain)


def next_hidden(full_width, onehot, embedding, stats, lifted):
    rows = lifted[0].shape[0]
    total, width = rows * CHUNKS, embedding.shape[1]

    def kernel(o_ref, e_ref, s0, s1, up0, up1, up2, out_ref, last_ref):
        for k, up in enumerate((up0, up1, up2)):
            span = slice(k * rows, (k + 1) * rows)
            so_far = s0[:, span] + s1[:, span]
            norm = lax.rsqrt(so_far / full_width + norm_eps)
            norm_col = jnp.transpose(norm)[:, 0:1]
            x = jnp.dot(o_ref[span], e_ref[...], preferred_element_type=f32)
            x = (x + norm_col * up[...].astype(f32)).astype(bf16)
            out_ref[span] = x
            per = rows // 16
            last_ref[k * per : (k + 1) * per] = x[rows - per :].astype(f32)

    return pl.pallas_call(
        kernel,
        out_shape=[
            jax.ShapeDtypeStruct((total, width), bf16),
            jax.ShapeDtypeStruct((total // 16, width), f32),
        ],
        in_specs=[VMEM] * 7,
        out_specs=[VMEM] * 2,
        compiler_params=params(16),
        name="next_hidden",
        cost_estimate=small_cost,
    )(onehot, embedding, *stats, *lifted)


def second_layer(n, coef, full_width, hidden, lows, stats, halves, crossed, out_factors,
                 decay, gain, reward, before):
    rows = hidden.shape[0] // CHUNKS
    group = out_factors.shape[1] // CHUNKS
    steps = 16
    per = rows // steps
    cols = slice(n * 256, (n + 1) * 256)

    def kernel(x_ref, l0, l1, s0, s1, own_ref, peer_ref, other_ref, b_ref, d_ref, g_ref, r_ref,
               before_ref, stats_ref, last_ref, square, lr, xr):
        factor = jnp.concatenate([b_ref[2 * n], b_ref[2 * n + 1]], axis=1)
        d = d_ref[:, cols]
        g = g_ref[:, cols]
        r = r_ref[:, cols]
        rest = 1.0 - d
        gr = g * r
        for k in range(CHUNKS):
            span_k = slice(k * rows, (k + 1) * rows)
            so_far = s0[:, span_k] + s1[:, span_k]
            norm = lax.rsqrt(so_far[0:1] / full_width + norm_eps)
            low = (l0[:, span_k] + l1[:, span_k] + norm * so_far) * coef
            spread_low = spread(low, 1, group)
            u = dot(spread_low, factor[k * group : (k + 1) * group], 0, 0) + (
                own_ref[0, span_k].astype(f32)
                + peer_ref[0, span_k].astype(f32)
                + other_ref[0, span_k].astype(f32)
            )
            h = jnp.zeros((per, 256), f32)
            xrr = x_ref[span_k, cols].astype(f32) * r
            xr[span_k] = xrr[:, :128] + xrr[:, 128:]
            for t in range(steps):
                span = slice(k * rows + t * per, k * rows + (t + 1) * per)
                h = d * h + rest * u[t * per : (t + 1) * per]
                hr = h * gr
                hh = h * h
                square[span] = hh[:, :128] + hh[:, 128:]
                lr[span] = hr[:, :128] + hr[:, 128:]
            last_ref[k * per : (k + 1) * per] = h * g
        ones = jnp.ones((8, 128), f32)
        sums = [dot(ones, a[...], 1, 1, lax.Precision.HIGHEST) for a in (square, lr, xr)]
        row = lax.broadcasted_iota(jnp.int32, (8, rows * CHUNKS), 0)
        stats_ref[...] = before_ref[...] + jnp.where(
            row == 0, sums[0], jnp.where(row == 1, sums[1], sums[2])
        )

    total = rows * CHUNKS
    return pl.pallas_call(
        kernel,
        out_shape=[
            jax.ShapeDtypeStruct((8, total), f32),
            jax.ShapeDtypeStruct((per * CHUNKS, 256), f32),
        ],
        in_specs=[VMEM] * 13,
        out_specs=[VMEM] * 2,
        scratch_shapes=[pltpu.VMEM((total, 128), f32)] * 3,
        compiler_params=params(16),
        name="second_layer",
        cost_estimate=small_cost,
    )(hidden, *lows, *stats, *halves, crossed, out_factors, decay, gain, reward, before)


def step_kernel(where, arrived, arrived_peer, members, members_all, scale, earlier):
    pops, rows, lanes = arrived.shape
    k = members * 8
    part = k // 2 + 8
    blocks = (rows - 2 * part) // k
    width = blocks * lanes

    def kernel(where_ref, in_ref, peer_ref, _, mine_ref, theirs_ref, paired, digit_rows):
        xl, c = where_ref[4], where_ref[2]
        head = blocks * k
        for p in range(pops):
            digits = in_ref[p, head + k // 2 : head + k // 2 + 8, :].astype(f32)
            for i in range(4):
                digit_rows[i, p : p + 1, :] = digits[i : i + 1, :]
        lane = lax.broadcasted_iota(jnp.int32, (pops, lanes), 1)
        real = lane < members
        here = (digit_rows[0] * 32.0 + digit_rows[1]) / members_all
        there = (digit_rows[2] * 32.0 + digit_rows[3]) / members_all
        mean = (
            jnp.sum(jnp.where(real, here, 0.0), keepdims=True)
            + jnp.sum(jnp.where(real, there, 0.0), keepdims=True)
        ) / members_all
        here = jnp.where(real, here - mean, 0.0)
        there = jnp.where(real, there - mean, 0.0)
        var = (
            jnp.sum(here * here, keepdims=True) + jnp.sum(there * there, keepdims=True)
        ) / members_all
        shaped = here * (lax.rsqrt(var + spread_eps) * scale)
        pick = lax.broadcasted_iota(jnp.int32, (k, lanes), 0) // 8 == lax.broadcasted_iota(
            jnp.int32, (k, lanes), 1
        )
        by_row = dot(pick.astype(f32), shaped, 1, 1, lax.Precision.HIGHEST)
        layer = (lax.broadcasted_iota(jnp.int32, (k, lanes), 0) % 8) // 4
        for p in range(pops):
            at = slice(p * k, (p + 1) * k)
            for rel in range(2):
                lo = pl.multiple_of((xl ^ rel) * part, 8)
                mine = in_ref[p, pl.ds(head + lo, k // 2), :].astype(f32)
                theirs = peer_ref[p, pl.ds(lo, k // 2), :].astype(f32)
                o = jnp.concatenate(
                    [jnp.where(c == 0, mine, theirs), jnp.where(c == 0, theirs, mine)], axis=0
                )
                o = o * by_row[:, p : p + 1]
                for l in range(2):
                    col = (rel * 2 + l) * lanes
                    paired[at, col : col + lanes] = jnp.where(layer == l, o, 0.0).astype(bf16)
        right = paired[...]
        for b in range(0, blocks, 2):
            left = jnp.concatenate(
                [
                    jnp.concatenate(
                        [in_ref[p, b * k : (b + 1) * k, :], in_ref[p, (b + 1) * k : (b + 2) * k, :]],
                        axis=1,
                    )
                    for p in range(pops)
                ],
                axis=0,
            )
            out = dot(left, right, 0, 0)
            span = slice(b * lanes, (b + 2) * lanes)
            for l in range(2):
                mine_ref[l, span, :] = out[:, l * lanes : (l + 1) * lanes]
                theirs_ref[l, span, :] = out[:, (2 + l) * lanes : (3 + l) * lanes].astype(bf16)

    return pl.pallas_call(
        kernel,
        out_shape=[
            jax.ShapeDtypeStruct((2, width, lanes), f32),
            jax.ShapeDtypeStruct((2, width, lanes), bf16),
        ],
        in_specs=[SMEM, VMEM, VMEM, pl.BlockSpec(memory_space=pl.ANY)],
        out_specs=[VMEM, VMEM],
        scratch_shapes=[
            pltpu.VMEM((pops * k, 4 * lanes), bf16),
            pltpu.VMEM((4, pops, lanes), f32),
        ],
        compiler_params=params(24),
        name="weight_step",
        cost_estimate=small_cost,
    )(where, arrived, arrived_peer, earlier)


def shards(
    token_ids,
    fitness_ranks,
    embedding,
    mix_weights,
    factors_in,
    factors_out,
    decay_rates,
    norm_gain,
    reward_dir,
):
    members, seq_count, step_count = token_ids.shape
    vocab, width = embedding.shape
    full_width = mix_weights.shape[2]
    rank_count = factors_in.shape[2]
    pop_count = lax.axis_size(POP)
    members_all = members * pop_count
    coef = noise_scale * (full_width * rank_count) ** (-0.5)
    y, xl, z = (lax.axis_index(a) for a in POP)
    xh, c = (lax.axis_index(a) for a in MP)
    where = jnp.stack([z, xh, c, y, xl]).astype(jnp.int32)
    rows_all = members * seq_count * step_count

    order = token_ids.reshape(CHUNKS, -1, step_count).transpose(0, 2, 1).reshape(-1)
    onehot = (order[:, None] == jnp.arange(vocab, dtype=jnp.int32)[None, :]).astype(bf16)

    def added(a, b):
        return (a.astype(f32) + b.astype(f32)).astype(bf16)

    peer, own = product(0, where, embedding, mix_weights, 512)
    theirs = swap(peer, "c")
    cross = added(own[:2], theirs[:2])
    first_table = [own, theirs, swap(cross, "xh")]
    both = jnp.stack([fitness_ranks, swap(after(fitness_ranks, peer), "xl")])
    digits = jnp.stack([both[0] // 32, both[0] % 32, both[1] // 32, both[1] % 32]).astype(bf16)
    digits = jnp.pad(digits, ((0, 4), (0, 128 - members)))
    pops = lax.axis_size("y") * lax.axis_size("z")
    a_blocks, b_own, packed = pack(
        after(where, peer), digits, factors_in, factors_out, pops
    )
    lows = mp_parts(low_kernel(after(onehot, peer), embedding, a_blocks))
    arrived = lax.all_to_all(after(packed, cross, lows[0]), ("y", "z"), 0, 0, tiled=True)

    decay = [decay_rates[l : l + 1] for l in range(2)]
    gain = [norm_gain[l : l + 1] for l in range(2)]
    lifted, stats = [], []
    for k in range(CHUNKS):
        up, st = first_layer(
            k, where, coef, onehot, first_table, lows, b_own, a_blocks, decay[0], gain[0]
        )
        lifted.append(up)
        stats.append(st)
    stats = mp_parts(jnp.concatenate(stats, axis=1))
    late_weights = stay(1, after(mix_weights, stats[0]))
    hidden, last_hidden = next_hidden(full_width, onehot, embedding, stats, lifted)
    sent, parts = [], []
    for n in range(4):
        earlier = parts[n - 2 : n - 1] if n > 1 else ()
        peer, own = dense(1, where, hidden, late_weights, 256, n, 1, earlier)
        parts.append(added(own, swap(peer, "c")))
        sent.append(swap(parts[n], "xh"))
    halves = []
    for n in range(4):
        peer, own = dense(0, where, hidden, late_weights, 256, n, 1, (sent[max(n - 1, 0)],))
        halves.append((own, swap(peer, "c")))

    st = jnp.zeros((8, rows_all), f32)
    lasts = []
    for n in range(4):
        if n == 1:
            outs_rows = 2 * (members * rank_count + 8)
            arrived_peer = swap(after(arrived, st)[:, -outs_rows:], "c")
        if n == 2:
            step_mine, step_theirs = step_kernel(
                where, arrived, arrived_peer, members, members_all,
                (members_all * rank_count) ** (-0.5), st,
            )
            st = after(st, step_theirs)
        st, last = second_layer(
            n, coef, full_width, hidden, lows, stats, halves[n], sent[n], b_own,
            decay[1], gain[1], reward_dir[None], st,
        )
        lasts.append(last)
    weight_step = step_mine + swap(after(step_theirs, sent[3]), "xl").astype(f32)
    so_far = sum(mp_parts(st))
    norm = lax.rsqrt(so_far[0] / full_width + norm_eps)
    terms = (so_far[2] + norm * so_far[1]).reshape(CHUNKS, step_count, -1)
    tail = norm.reshape(CHUNKS, step_count, -1)[:, -1].reshape(-1)
    finals = last_hidden + jnp.concatenate(lasts, axis=1) * tail[:, None]
    final_features = finals.astype(bf16).reshape(members, seq_count, width)
    scores = jnp.mean(terms, axis=1).reshape(members, seq_count) * full_width ** (-0.5)
    return (final_features, scores, weight_step)


def solution(mesh):
    fine = Mesh(mesh.devices.reshape(4, 2, 4, 2, 2), POP + MP)
    return jax.shard_map(
        shards,
        mesh=fine,
        in_specs=(
            P(POP, None, None),
            P(POP),
            P(None, MP),
            P(None, MP, None),
            P(None, POP, None, MP),
            P(None, POP, None, None),
            P(None, MP),
            P(None, MP),
            P(MP),
        ),
        out_specs=(P(POP, None, MP), P(POP, None), P(None, MP, POP)),
        check_vma=False,
    )
```

```python
import jax
import jax.numpy as jnp
from jax import lax
from jax.experimental import pallas as pl
from jax.experimental.pallas import tpu as pltpu
from jax.sharding import Mesh
from jax.sharding import PartitionSpec as P

noise_scale = 0.25
norm_eps = 1e-06
spread_eps = 1e-05

POP = ("y", "xl", "z")
MP = ("xh", "c")
CHUNKS = 3
f32 = jnp.float32
bf16 = jnp.bfloat16
SMEM = pl.BlockSpec(memory_space=pltpu.SMEM)
VMEM = pl.BlockSpec(memory_space=pltpu.VMEM)
small_cost = pl.CostEstimate(flops=1000, bytes_accessed=1000, transcendentals=0)


def params(mib=24):
    return pltpu.CompilerParams(vmem_limit_bytes=mib * 1024 * 1024)


def swap(value, axis):
    return lax.ppermute(value, axis, [(0, 1), (1, 0)])


def after(value, *earlier):
    return lax.optimization_barrier((value, *earlier))[0]


def mp_parts(value):
    pair = value + swap(value, "c")
    return pair, swap(pair, "xh")


def dot(a, b, ca, cb, precision=None):
    return lax.dot_general(
        a, b, (((ca,), (cb,)), ((), ())), preferred_element_type=f32, precision=precision
    )


def regroup(factors, start):
    layers, members, ranks, _ = factors.shape
    blocks, k = 8, members * layers * ranks

    def kernel(start_ref, in_ref, out_ref):
        cols = pl.ds(pl.multiple_of(start_ref[0], 1024), 1024)
        for m in range(members):
            rows = jnp.concatenate(
                [in_ref[l, m, :, cols].astype(f32) for l in range(layers)], axis=0
            ).astype(bf16)
            for n in range(blocks):
                out_ref[n, m * 8 : m * 8 + 8, :] = rows[:, n * 128 : (n + 1) * 128]

    return pl.pallas_call(
        kernel,
        out_shape=jax.ShapeDtypeStruct((blocks, k, 128), bf16),
        in_specs=[SMEM, VMEM],
        out_specs=VMEM,
        compiler_params=params(16),
        name="regroup",
        cost_estimate=small_cost,
    )(start, factors)


def pack(where, digits, a_blocks, factors_out, pops):
    layers, members, ranks, full = factors_out.shape
    blocks, k, _ = a_blocks.shape
    half = members // 2
    part = k // 2 + 8
    rows = blocks * k + 2 * part

    def kernel(where_ref, digits_ref, a_ref, out_ref, packed_ref):
        c = where_ref[2]
        for m in range(half):
            b = jnp.concatenate(
                [out_ref[l, c * half + m].astype(f32) for l in range(layers)], axis=0
            ).astype(bf16)
            for o in range(2 * pops):
                y, x, z = o // 8, (o // 4) % 2, o % 4
                lo = blocks * k + x * part + m * 8
                packed_ref[y * 4 + z, lo : lo + 8, :] = b[:, o * 128 : (o + 1) * 128]
        for p in range(pops):
            for n in range(blocks):
                packed_ref[p, n * k : (n + 1) * k, :] = a_ref[n]
            for x in range(2):
                lo = blocks * k + x * part + k // 2
                packed_ref[p, lo : lo + 8, :] = digits_ref[...]

    return pl.pallas_call(
        kernel,
        out_shape=jax.ShapeDtypeStruct((pops, rows, 128), bf16),
        in_specs=[SMEM] + [VMEM] * 3,
        out_specs=VMEM,
        compiler_params=params(16),
        name="pack",
        cost_estimate=small_cost,
    )(where, digits, a_blocks, factors_out)


def product(layer, where, left, weights, piece):
    rows, width = left.shape
    full = weights.shape[2]
    per_owner = width // piece
    cuts = 4
    depth = width // cuts
    count = 2 * per_owner

    def kernel(where_ref, left_ref, w_ref, out0_ref, out1_ref, total):
        k = pl.program_id(0)
        part = left_ref[:, pl.ds(pl.multiple_of(k * depth, depth), depth)]

        @pl.when(k == 0)
        def _():
            for n in range(full // piece):
                cols = slice(n * piece, (n + 1) * piece)
                total[:, cols] = jnp.dot(part, w_ref[0, :, cols], preferred_element_type=f32)

        @pl.when(k > 0)
        def _():
            for n in range(full // piece):
                cols = slice(n * piece, (n + 1) * piece)
                total[:, cols] += jnp.dot(part, w_ref[0, :, cols], preferred_element_type=f32)

        @pl.when(k == cuts - 1)
        def _():
            for flip, out_ref in ((1, out0_ref), (0, out1_ref)):
                for i in range(count):
                    half = where_ref[1] ^ (1 - i // per_owner)
                    owner = half * 2 + (where_ref[2] ^ flip)
                    at = pl.multiple_of(owner * width + i % per_owner * piece, piece)
                    out_ref[i] = total[:, pl.ds(at, piece)].astype(bf16)

    return pl.pallas_call(
        kernel,
        grid=(cuts,),
        in_specs=[
            SMEM,
            pl.BlockSpec((rows, width), lambda k: (0, 0)),
            pl.BlockSpec((1, depth, full), lambda k: (layer, k, 0)),
        ],
        out_specs=[pl.BlockSpec((count, rows, piece), lambda k: (0, 0, 0))] * 2,
        out_shape=[jax.ShapeDtypeStruct((count, rows, piece), bf16)] * 2,
        scratch_shapes=[pltpu.VMEM((rows, full), f32)],
        compiler_params=params(48),
        name="product",
        cost_estimate=small_cost,
    )(where, left, weights)


def stay(layer, weights):
    _, width, full = weights.shape
    cuts = 8
    rows = width // cuts

    def kernel(w_ref, out_ref, sems):
        def part(i):
            span = slice(i * rows, (i + 1) * rows)
            return pltpu.make_async_copy(w_ref.at[layer, span], out_ref.at[span], sems.at[i])

        for i in range(cuts):
            part(i).start()
        for i in range(cuts):
            part(i).wait()

    return pl.pallas_call(
        kernel,
        out_shape=jax.ShapeDtypeStruct((width, full), bf16),
        in_specs=[pl.BlockSpec(memory_space=pltpu.HBM)],
        out_specs=VMEM,
        scratch_shapes=[pltpu.SemaphoreType.DMA((cuts,))],
        compiler_params=params(40),
        name="stay",
        cost_estimate=small_cost,
    )(weights)


def dense(rel, where, left, weights, piece, first=0, count=1, earlier=()):
    rows, width = left.shape

    def kernel(where_ref, left_ref, w_ref, *refs):
        out0_ref, out1_ref = refs[len(earlier) :]
        for flip, out_ref in ((1, out0_ref), (0, out1_ref)):
            owner = (where_ref[1] ^ rel) * 2 + (where_ref[2] ^ flip)
            for n in range(count):
                at = pl.multiple_of(owner * width + (first + n) * piece, piece)
                out_ref[n] = jnp.dot(
                    left_ref[...], w_ref[:, pl.ds(at, piece)], preferred_element_type=f32
                ).astype(bf16)

    return pl.pallas_call(
        kernel,
        out_shape=[jax.ShapeDtypeStruct((count, rows, piece), bf16)] * 2,
        in_specs=[SMEM, VMEM, VMEM] + [pl.BlockSpec(memory_space=pl.ANY)] * len(earlier),
        out_specs=[VMEM] * 2,
        compiler_params=params(16),
        name="dense",
        cost_estimate=small_cost,
    )(where, left, weights, *earlier)


def member_of(shape, per, dim):
    return lax.broadcasted_iota(jnp.int32, shape, dim) // per


def low_kernel(onehot, embedding, factors):
    rows = onehot.shape[0]
    per_chunk = rows // CHUNKS
    group = factors.shape[1] // CHUNKS

    def kernel(o_ref, e_ref, a_ref, out_ref):
        for k in range(CHUNKS):
            x = jnp.dot(
                o_ref[k * per_chunk : (k + 1) * per_chunk, :], e_ref[...], preferred_element_type=f32
            ).astype(bf16)
            total = jnp.zeros((group, per_chunk), f32)
            for b in range(factors.shape[0]):
                total += dot(
                    a_ref[b, k * group : (k + 1) * group, :], x[:, b * 128 : (b + 1) * 128], 1, 1
                )
            out_ref[:, k * per_chunk : (k + 1) * per_chunk] = diagonal(total)

    return pl.pallas_call(
        kernel,
        out_shape=jax.ShapeDtypeStruct((8, rows), f32),
        in_specs=[VMEM] * 3,
        out_specs=VMEM,
        compiler_params=params(),
        name="low",
        cost_estimate=small_cost,
    )(onehot, embedding, factors)


def diagonal(total):
    group, cols = total.shape
    row_member = member_of((group, cols), 8, 0)
    col_member = (lax.broadcasted_iota(jnp.int32, (group, cols), 1) % 16) // 4
    kept = jnp.where(row_member == col_member, total, 0.0)
    out = kept[0:8]
    for m in range(1, group // 8):
        out = out + kept[m * 8 : (m + 1) * 8]
    return out


def spread(low, layer, group):
    cols = low.shape[1]
    row = lax.broadcasted_iota(jnp.int32, (group, cols), 0)
    col_member = (lax.broadcasted_iota(jnp.int32, (group, cols), 1) % 16) // 4
    keep = (row // 8 == col_member) & ((row % 8) // 4 == layer)
    tiled = jnp.concatenate([low] * (group // 8), axis=0)
    return jnp.where(keep, tiled, 0.0).astype(bf16)


def first_layer(chunk, where, coef, onehot, table_parts, lows, out_factors, in_factors, decay, gain):
    rows = onehot.shape[0] // CHUNKS
    group = out_factors.shape[1] // CHUNKS
    width = decay.shape[1]
    steps = 16
    per = rows // steps

    def kernel(o_ref, t0, t1, t2, l0, l1, b_ref, a_ref, d_ref, g_ref, lifted_ref, stats_ref, square):
        at = slice(chunk * rows, (chunk + 1) * rows)
        mine = slice(chunk * group, (chunk + 1) * group)
        low = (l0[:, at] + l1[:, at]) * coef
        spread_low = spread(low, 0, group)
        total = jnp.zeros((group, rows), f32)
        for n in range(width // 256):
            cols = slice(n * 256, (n + 1) * 256)
            in_half = slice(n % 2 * 256, n % 2 * 256 + 256)
            parts = (t0[2 + n // 2, :, in_half], t1[2 + n // 2, :, in_half], t2[n // 2, :, in_half])
            table = sum(p.astype(f32) for p in parts).astype(bf16)
            factor = jnp.concatenate([b_ref[2 * n, mine], b_ref[2 * n + 1, mine]], axis=1)
            u = jnp.dot(o_ref[at], table, preferred_element_type=f32) + dot(
                spread_low, factor, 0, 0
            )
            d = d_ref[:, cols]
            g = g_ref[:, cols]
            rest = 1.0 - d
            h = jnp.zeros((per, 256), f32)
            for t in range(steps):
                span = slice(t * per, (t + 1) * per)
                h = d * h + rest * u[span]
                lifted_ref[span, cols] = (h * g).astype(bf16)
                hh = h * h
                hh = hh[:, :128] + hh[:, 128:]
                if n == 0:
                    square[span] = hh
                else:
                    square[span] += hh
            factor_in = jnp.concatenate([a_ref[2 * n, mine], a_ref[2 * n + 1, mine]], axis=1)
            total += dot(factor_in, lifted_ref[:, cols], 1, 1)
        sums = dot(jnp.ones((8, 128), f32), square[...], 1, 1, lax.Precision.HIGHEST)
        low_next = diagonal(total)
        row = lax.broadcasted_iota(jnp.int32, (8, rows), 0)
        stats_ref[...] = jnp.where(row < 4, sums, low_next)

    return pl.pallas_call(
        kernel,
        out_shape=[
            jax.ShapeDtypeStruct((rows, width), bf16),
            jax.ShapeDtypeStruct((8, rows), f32),
        ],
        in_specs=[VMEM] * 10,
        out_specs=[VMEM, VMEM],
        scratch_shapes=[pltpu.VMEM((rows, 128), f32)],
        compiler_params=params(16),
        name="first_layer",
        cost_estimate=small_cost,
    )(onehot, *table_parts, *lows, out_factors, in_factors, decay, gain)


def next_hidden(full_width, onehot, embedding, stats, lifted):
    rows = lifted[0].shape[0]
    total, width = rows * CHUNKS, embedding.shape[1]

    def kernel(o_ref, e_ref, s0, s1, up0, up1, up2, out_ref, last_ref):
        for k, up in enumerate((up0, up1, up2)):
            span = slice(k * rows, (k + 1) * rows)
            so_far = s0[:, span] + s1[:, span]
            norm = lax.rsqrt(so_far / full_width + norm_eps)
            norm_col = jnp.transpose(norm)[:, 0:1]
            x = jnp.dot(o_ref[span], e_ref[...], preferred_element_type=f32)
            x = (x + norm_col * up[...].astype(f32)).astype(bf16)
            out_ref[span] = x
            per = rows // 16
            last_ref[k * per : (k + 1) * per] = x[rows - per :].astype(f32)

    return pl.pallas_call(
        kernel,
        out_shape=[
            jax.ShapeDtypeStruct((total, width), bf16),
            jax.ShapeDtypeStruct((total // 16, width), f32),
        ],
        in_specs=[VMEM] * 7,
        out_specs=[VMEM] * 2,
        compiler_params=params(16),
        name="next_hidden",
        cost_estimate=small_cost,
    )(onehot, embedding, *stats, *lifted)


def second_layer(n, coef, full_width, hidden, lows, stats, halves, crossed, slot, out_factors,
                 decay, gain, reward, before):
    rows = hidden.shape[0] // CHUNKS
    group = out_factors.shape[1] // CHUNKS
    steps = 16
    per = rows // steps
    cols = slice(n * 256, (n + 1) * 256)

    def kernel(x_ref, l0, l1, s0, s1, own_ref, peer_ref, other_ref, b_ref, d_ref, g_ref, r_ref,
               before_ref, stats_ref, last_ref, square, lr, xr):
        factor = jnp.concatenate([b_ref[2 * n], b_ref[2 * n + 1]], axis=1)
        d = d_ref[:, cols]
        g = g_ref[:, cols]
        r = r_ref[:, cols]
        rest = 1.0 - d
        gr = g * r
        for k in range(CHUNKS):
            span_k = slice(k * rows, (k + 1) * rows)
            so_far = s0[:, span_k] + s1[:, span_k]
            norm = lax.rsqrt(so_far[0:1] / full_width + norm_eps)
            low = (l0[:, span_k] + l1[:, span_k] + norm * so_far) * coef
            spread_low = spread(low, 1, group)
            u = dot(spread_low, factor[k * group : (k + 1) * group], 0, 0) + (
                own_ref[0, span_k].astype(f32)
                + peer_ref[0, span_k].astype(f32)
                + other_ref[slot, span_k].astype(f32)
            )
            h = jnp.zeros((per, 256), f32)
            xrr = x_ref[span_k, cols].astype(f32) * r
            xr[span_k] = xrr[:, :128] + xrr[:, 128:]
            for t in range(steps):
                span = slice(k * rows + t * per, k * rows + (t + 1) * per)
                h = d * h + rest * u[t * per : (t + 1) * per]
                hr = h * gr
                hh = h * h
                square[span] = hh[:, :128] + hh[:, 128:]
                lr[span] = hr[:, :128] + hr[:, 128:]
            last_ref[k * per : (k + 1) * per] = h * g
        ones = jnp.ones((8, 128), f32)
        sums = [dot(ones, a[...], 1, 1, lax.Precision.HIGHEST) for a in (square, lr, xr)]
        row = lax.broadcasted_iota(jnp.int32, (8, rows * CHUNKS), 0)
        stats_ref[...] = before_ref[...] + jnp.where(
            row == 0, sums[0], jnp.where(row == 1, sums[1], sums[2])
        )

    total = rows * CHUNKS
    return pl.pallas_call(
        kernel,
        out_shape=[
            jax.ShapeDtypeStruct((8, total), f32),
            jax.ShapeDtypeStruct((per * CHUNKS, 256), f32),
        ],
        in_specs=[VMEM] * 13,
        out_specs=[VMEM] * 2,
        scratch_shapes=[pltpu.VMEM((total, 128), f32)] * 3,
        compiler_params=params(16),
        name="second_layer",
        cost_estimate=small_cost,
    )(hidden, *lows, *stats, *halves, crossed, out_factors, decay, gain, reward, before)


def step_kernel(where, arrived, arrived_peer, digits_there, members, members_all, scale, earlier):
    pops, rows, lanes = arrived.shape
    k = members * 8
    part = k // 2 + 8
    blocks = (rows - 2 * part) // k
    width = blocks * lanes

    def kernel(where_ref, in_ref, peer_ref, there_ref, _, mine_ref, theirs_ref, paired, digit_rows):
        xl, c = where_ref[4], where_ref[2]
        head = blocks * k
        for p in range(pops):
            here = in_ref[p, head + k // 2 : head + k // 2 + 8, :].astype(f32)
            there = there_ref[p].astype(f32)
            for i in range(2):
                digit_rows[i, p : p + 1, :] = here[i : i + 1, :]
                digit_rows[2 + i, p : p + 1, :] = there[i : i + 1, :]
        lane = lax.broadcasted_iota(jnp.int32, (pops, lanes), 1)
        real = lane < members
        here = (digit_rows[0] * 32.0 + digit_rows[1]) / members_all
        there = (digit_rows[2] * 32.0 + digit_rows[3]) / members_all
        mean = (
            jnp.sum(jnp.where(real, here, 0.0), keepdims=True)
            + jnp.sum(jnp.where(real, there, 0.0), keepdims=True)
        ) / members_all
        here = jnp.where(real, here - mean, 0.0)
        there = jnp.where(real, there - mean, 0.0)
        var = (
            jnp.sum(here * here, keepdims=True) + jnp.sum(there * there, keepdims=True)
        ) / members_all
        shaped = here * (lax.rsqrt(var + spread_eps) * scale)
        pick = lax.broadcasted_iota(jnp.int32, (k, lanes), 0) // 8 == lax.broadcasted_iota(
            jnp.int32, (k, lanes), 1
        )
        by_row = dot(pick.astype(f32), shaped, 1, 1, lax.Precision.HIGHEST)
        layer = (lax.broadcasted_iota(jnp.int32, (k, lanes), 0) % 8) // 4
        for p in range(pops):
            at = slice(p * k, (p + 1) * k)
            for rel in range(2):
                lo = pl.multiple_of((xl ^ rel) * part, 8)
                mine = in_ref[p, pl.ds(head + lo, k // 2), :].astype(f32)
                theirs = peer_ref[p, pl.ds(lo, k // 2), :].astype(f32)
                o = jnp.concatenate(
                    [jnp.where(c == 0, mine, theirs), jnp.where(c == 0, theirs, mine)], axis=0
                )
                o = o * by_row[:, p : p + 1]
                for l in range(2):
                    col = (rel * 2 + l) * lanes
                    paired[at, col : col + lanes] = jnp.where(layer == l, o, 0.0).astype(bf16)
        right = paired[...]
        for b in range(0, blocks, 2):
            left = jnp.concatenate(
                [
                    jnp.concatenate(
                        [in_ref[p, b * k : (b + 1) * k, :], in_ref[p, (b + 1) * k : (b + 2) * k, :]],
                        axis=1,
                    )
                    for p in range(pops)
                ],
                axis=0,
            )
            out = dot(left, right, 0, 0)
            span = slice(b * lanes, (b + 2) * lanes)
            for l in range(2):
                mine_ref[l, span, :] = out[:, l * lanes : (l + 1) * lanes]
                theirs_ref[l, span, :] = out[:, (2 + l) * lanes : (3 + l) * lanes].astype(bf16)

    return pl.pallas_call(
        kernel,
        out_shape=[
            jax.ShapeDtypeStruct((2, width, lanes), f32),
            jax.ShapeDtypeStruct((2, width, lanes), bf16),
        ],
        in_specs=[SMEM, VMEM, VMEM, VMEM, pl.BlockSpec(memory_space=pl.ANY)],
        out_specs=[VMEM, VMEM],
        scratch_shapes=[
            pltpu.VMEM((pops * k, 4 * lanes), bf16),
            pltpu.VMEM((4, pops, lanes), f32),
        ],
        compiler_params=params(24),
        name="weight_step",
        cost_estimate=small_cost,
    )(where, arrived, arrived_peer, digits_there, earlier)


def shards(
    token_ids,
    fitness_ranks,
    embedding,
    mix_weights,
    factors_in,
    factors_out,
    decay_rates,
    norm_gain,
    reward_dir,
):
    members, seq_count, step_count = token_ids.shape
    vocab, width = embedding.shape
    full_width = mix_weights.shape[2]
    rank_count = factors_in.shape[2]
    pop_count = lax.axis_size(POP)
    members_all = members * pop_count
    coef = noise_scale * (full_width * rank_count) ** (-0.5)
    y, xl, z = (lax.axis_index(a) for a in POP)
    xh, c = (lax.axis_index(a) for a in MP)
    where = jnp.stack([z, xh, c, y, xl]).astype(jnp.int32)
    rows_all = members * seq_count * step_count

    order = token_ids.reshape(CHUNKS, -1, step_count).transpose(0, 2, 1).reshape(-1)
    onehot = (order[:, None] == jnp.arange(vocab, dtype=jnp.int32)[None, :]).astype(bf16)

    def added(a, b):
        return (a.astype(f32) + b.astype(f32)).astype(bf16)

    peer, own = product(0, where, embedding, mix_weights, 512)
    theirs = swap(peer, "c")
    cross = added(own[:2], theirs[:2])
    first_table = [own, theirs, swap(cross, "xh")]
    a_blocks = regroup(after(factors_in, peer), jnp.zeros((1,), jnp.int32))
    lows = mp_parts(low_kernel(after(onehot, peer), embedding, a_blocks))
    digits = jnp.stack([fitness_ranks // 32, fitness_ranks % 32]).astype(bf16)
    digits = jnp.pad(digits, ((0, 6), (0, 128 - members)))
    pops = lax.axis_size("y") * lax.axis_size("z")
    late_out = after(factors_out, cross)
    b_own = regroup(late_out, ((xh * 2 + c) * width).reshape(1).astype(jnp.int32))
    packed = pack(where, digits, a_blocks, late_out, pops)
    arrived = lax.all_to_all(after(packed, lows[0]), ("y", "z"), 0, 0, tiled=True)

    decay = [decay_rates[l : l + 1] for l in range(2)]
    gain = [norm_gain[l : l + 1] for l in range(2)]
    lifted, stats = [], []
    for k in range(CHUNKS):
        up, st = first_layer(
            k, where, coef, onehot, first_table, lows, b_own, a_blocks, decay[0], gain[0]
        )
        lifted.append(up)
        stats.append(st)
    stats = mp_parts(jnp.concatenate(stats, axis=1))
    late_weights = stay(1, after(mix_weights, stats[0]))
    hidden, last_hidden = next_hidden(full_width, onehot, embedding, stats, lifted)
    sent, parts, place = [], [], []
    for first, count in ((0, 3), (3, 1)):
        peer, own = dense(1, where, hidden, late_weights, 256, first, count, ())
        part = added(own, swap(peer, "c"))
        parts.append(part)
        sent.append(swap(part, "xh"))
        place += [(len(sent) - 1, n) for n in range(count)]
    halves = []
    for n in range(4):
        peer, own = dense(0, where, hidden, late_weights, 256, n, 1, (*parts, *(h[1] for h in halves)))
        halves.append((own, swap(peer, "c")))

    outs_rows = 2 * (members * rank_count + 8)
    tail_rows = after(arrived, halves[3][0])[:, -outs_rows:]
    arrived_peer = swap(tail_rows, "c")
    digits_there = swap(tail_rows[:, -8:], "xl")
    step_mine, step_theirs = step_kernel(
        where, arrived, arrived_peer, digits_there, members, members_all,
        (members_all * rank_count) ** (-0.5), halves[3][0],
    )
    st = after(jnp.zeros((8, rows_all), f32), step_theirs)
    lasts = []
    for n in range(4):
        st, last = second_layer(
            n, coef, full_width, hidden, lows, stats, halves[n], sent[place[n][0]], place[n][1], b_own,
            decay[1], gain[1], reward_dir[None], st,
        )
        lasts.append(last)
    weight_step = step_mine + swap(after(step_theirs, sent[-1]), "xl").astype(f32)
    so_far = sum(mp_parts(st))
    norm = lax.rsqrt(so_far[0] / full_width + norm_eps)
    terms = (so_far[2] + norm * so_far[1]).reshape(CHUNKS, step_count, -1)
    tail = norm.reshape(CHUNKS, step_count, -1)[:, -1].reshape(-1)
    finals = last_hidden + jnp.concatenate(lasts, axis=1) * tail[:, None]
    final_features = finals.astype(bf16).reshape(members, seq_count, width)
    scores = jnp.mean(terms, axis=1).reshape(members, seq_count) * full_width ** (-0.5)
    return (final_features, scores, weight_step)


def solution(mesh):
    fine = Mesh(mesh.devices.reshape(4, 2, 4, 2, 2), POP + MP)
    return jax.shard_map(
        shards,
        mesh=fine,
        in_specs=(
            P(POP, None, None),
            P(POP),
            P(None, MP),
            P(None, MP, None),
            P(None, POP, None, MP),
            P(None, POP, None, None),
            P(None, MP),
            P(None, MP),
            P(MP),
        ),
        out_specs=(P(POP, None, MP), P(POP, None), P(None, MP, POP)),
        check_vma=False,
    )
```

```python
import jax
import jax.numpy as jnp
from jax import lax
from jax.experimental import pallas as pl
from jax.experimental.pallas import tpu as pltpu
from jax.sharding import Mesh
from jax.sharding import PartitionSpec as P

noise_scale = 0.25
norm_eps = 1e-06
spread_eps = 1e-05

POP = ("y", "xl", "z")
MP = ("xh", "c")
CHUNKS = 3
f32 = jnp.float32
bf16 = jnp.bfloat16
SMEM = pl.BlockSpec(memory_space=pltpu.SMEM)
VMEM = pl.BlockSpec(memory_space=pltpu.VMEM)
small_cost = pl.CostEstimate(flops=1000, bytes_accessed=1000, transcendentals=0)


def params(mib=24):
    return pltpu.CompilerParams(vmem_limit_bytes=mib * 1024 * 1024)


def swap(value, axis):
    return lax.ppermute(value, axis, [(0, 1), (1, 0)])


def after(value, *earlier):
    return lax.optimization_barrier((value, *earlier))[0]


def mp_parts(value):
    pair = value + swap(value, "c")
    return pair, swap(pair, "xh")


def dot(a, b, ca, cb, precision=None):
    return lax.dot_general(
        a, b, (((ca,), (cb,)), ((), ())), preferred_element_type=f32, precision=precision
    )


def regroup(factors, start):
    layers, members, ranks, _ = factors.shape
    blocks, k = 8, members * layers * ranks

    def kernel(start_ref, in_ref, out_ref):
        cols = pl.ds(pl.multiple_of(start_ref[0], 1024), 1024)
        for m in range(members):
            rows = jnp.concatenate(
                [in_ref[l, m, :, cols].astype(f32) for l in range(layers)], axis=0
            ).astype(bf16)
            for n in range(blocks):
                out_ref[n, m * 8 : m * 8 + 8, :] = rows[:, n * 128 : (n + 1) * 128]

    return pl.pallas_call(
        kernel,
        out_shape=jax.ShapeDtypeStruct((blocks, k, 128), bf16),
        in_specs=[SMEM, VMEM],
        out_specs=VMEM,
        compiler_params=params(16),
        name="regroup",
        cost_estimate=small_cost,
    )(start, factors)


def pack(where, digits, a_blocks, factors_out, pops):
    layers, members, ranks, full = factors_out.shape
    blocks, k, _ = a_blocks.shape
    half = members // 2
    part = k // 2 + 8
    rows = blocks * k + 2 * part

    def kernel(where_ref, digits_ref, a_ref, out_ref, packed_ref):
        c = where_ref[2]
        for m in range(half):
            b = jnp.concatenate(
                [out_ref[l, c * half + m].astype(f32) for l in range(layers)], axis=0
            ).astype(bf16)
            for o in range(2 * pops):
                y, x, z = o // 8, (o // 4) % 2, o % 4
                lo = blocks * k + x * part + m * 8
                packed_ref[y * 4 + z, lo : lo + 8, :] = b[:, o * 128 : (o + 1) * 128]
        for p in range(pops):
            for n in range(blocks):
                packed_ref[p, n * k : (n + 1) * k, :] = a_ref[n]
            for x in range(2):
                lo = blocks * k + x * part + k // 2
                packed_ref[p, lo : lo + 8, :] = digits_ref[...]

    return pl.pallas_call(
        kernel,
        out_shape=jax.ShapeDtypeStruct((pops, rows, 128), bf16),
        in_specs=[SMEM] + [VMEM] * 3,
        out_specs=VMEM,
        compiler_params=params(16),
        name="pack",
        cost_estimate=small_cost,
    )(where, digits, a_blocks, factors_out)


def product(layer, where, left, weights, piece):
    rows, width = left.shape
    full = weights.shape[2]
    per_owner = width // piece
    cuts = 4
    depth = width // cuts
    count = 2 * per_owner

    def kernel(where_ref, left_ref, w_ref, out0_ref, out1_ref, total):
        k = pl.program_id(0)
        part = left_ref[:, pl.ds(pl.multiple_of(k * depth, depth), depth)]

        @pl.when(k == 0)
        def _():
            for n in range(full // piece):
                cols = slice(n * piece, (n + 1) * piece)
                total[:, cols] = jnp.dot(part, w_ref[0, :, cols], preferred_element_type=f32)

        @pl.when(k > 0)
        def _():
            for n in range(full // piece):
                cols = slice(n * piece, (n + 1) * piece)
                total[:, cols] += jnp.dot(part, w_ref[0, :, cols], preferred_element_type=f32)

        @pl.when(k == cuts - 1)
        def _():
            for flip, out_ref in ((1, out0_ref), (0, out1_ref)):
                for i in range(count):
                    half = where_ref[1] ^ (1 - i // per_owner)
                    owner = half * 2 + (where_ref[2] ^ flip)
                    at = pl.multiple_of(owner * width + i % per_owner * piece, piece)
                    out_ref[i] = total[:, pl.ds(at, piece)].astype(bf16)

    return pl.pallas_call(
        kernel,
        grid=(cuts,),
        in_specs=[
            SMEM,
            pl.BlockSpec((rows, width), lambda k: (0, 0)),
            pl.BlockSpec((1, depth, full), lambda k: (layer, k, 0)),
        ],
        out_specs=[pl.BlockSpec((count, rows, piece), lambda k: (0, 0, 0))] * 2,
        out_shape=[jax.ShapeDtypeStruct((count, rows, piece), bf16)] * 2,
        scratch_shapes=[pltpu.VMEM((rows, full), f32)],
        compiler_params=params(48),
        name="product",
        cost_estimate=small_cost,
    )(where, left, weights)


def stay(layer, weights):
    _, width, full = weights.shape
    cuts = 8
    rows = width // cuts

    def kernel(w_ref, out_ref, sems):
        def part(i):
            span = slice(i * rows, (i + 1) * rows)
            return pltpu.make_async_copy(w_ref.at[layer, span], out_ref.at[span], sems.at[i])

        for i in range(cuts):
            part(i).start()
        for i in range(cuts):
            part(i).wait()

    return pl.pallas_call(
        kernel,
        out_shape=jax.ShapeDtypeStruct((width, full), bf16),
        in_specs=[pl.BlockSpec(memory_space=pltpu.HBM)],
        out_specs=VMEM,
        scratch_shapes=[pltpu.SemaphoreType.DMA((cuts,))],
        compiler_params=params(40),
        name="stay",
        cost_estimate=small_cost,
    )(weights)


def dense(rel, where, left, weights, piece, first=0, count=1, earlier=()):
    rows, width = left.shape

    def kernel(where_ref, left_ref, w_ref, *refs):
        out0_ref, out1_ref = refs[len(earlier) :]
        for flip, out_ref in ((1, out0_ref), (0, out1_ref)):
            owner = (where_ref[1] ^ rel) * 2 + (where_ref[2] ^ flip)
            for n in range(count):
                at = pl.multiple_of(owner * width + (first + n) * piece, piece)
                out_ref[n] = jnp.dot(
                    left_ref[...], w_ref[:, pl.ds(at, piece)], preferred_element_type=f32
                ).astype(bf16)

    return pl.pallas_call(
        kernel,
        out_shape=[jax.ShapeDtypeStruct((count, rows, piece), bf16)] * 2,
        in_specs=[SMEM, VMEM, VMEM] + [pl.BlockSpec(memory_space=pl.ANY)] * len(earlier),
        out_specs=[VMEM] * 2,
        compiler_params=params(16),
        name="dense",
        cost_estimate=small_cost,
    )(where, left, weights, *earlier)


def member_of(shape, per, dim):
    return lax.broadcasted_iota(jnp.int32, shape, dim) // per


def low_kernel(onehot, embedding, factors):
    rows = onehot.shape[0]
    per_chunk = rows // CHUNKS
    group = factors.shape[1] // CHUNKS

    def kernel(o_ref, e_ref, a_ref, out_ref):
        for k in range(CHUNKS):
            x = jnp.dot(
                o_ref[k * per_chunk : (k + 1) * per_chunk, :], e_ref[...], preferred_element_type=f32
            ).astype(bf16)
            total = jnp.zeros((group, per_chunk), f32)
            for b in range(factors.shape[0]):
                total += dot(
                    a_ref[b, k * group : (k + 1) * group, :], x[:, b * 128 : (b + 1) * 128], 1, 1
                )
            out_ref[:, k * per_chunk : (k + 1) * per_chunk] = diagonal(total)

    return pl.pallas_call(
        kernel,
        out_shape=jax.ShapeDtypeStruct((8, rows), f32),
        in_specs=[VMEM] * 3,
        out_specs=VMEM,
        compiler_params=params(),
        name="low",
        cost_estimate=small_cost,
    )(onehot, embedding, factors)


def diagonal(total):
    group, cols = total.shape
    row_member = member_of((group, cols), 8, 0)
    col_member = (lax.broadcasted_iota(jnp.int32, (group, cols), 1) % 16) // 4
    kept = jnp.where(row_member == col_member, total, 0.0)
    out = kept[0:8]
    for m in range(1, group // 8):
        out = out + kept[m * 8 : (m + 1) * 8]
    return out


def spread(low, layer, group):
    cols = low.shape[1]
    row = lax.broadcasted_iota(jnp.int32, (group, cols), 0)
    col_member = (lax.broadcasted_iota(jnp.int32, (group, cols), 1) % 16) // 4
    keep = (row // 8 == col_member) & ((row % 8) // 4 == layer)
    tiled = jnp.concatenate([low] * (group // 8), axis=0)
    return jnp.where(keep, tiled, 0.0).astype(bf16)


def first_layer(chunk, where, coef, onehot, table_parts, lows, out_factors, in_factors, decay, gain):
    rows = onehot.shape[0] // CHUNKS
    group = out_factors.shape[1] // CHUNKS
    width = decay.shape[1]
    steps = 16
    per = rows // steps

    def kernel(o_ref, t0, t1, t2, l0, l1, b_ref, a_ref, d_ref, g_ref, lifted_ref, stats_ref, square):
        at = slice(chunk * rows, (chunk + 1) * rows)
        mine = slice(chunk * group, (chunk + 1) * group)
        low = (l0[:, at] + l1[:, at]) * coef
        spread_low = spread(low, 0, group)
        total = jnp.zeros((group, rows), f32)
        for n in range(width // 256):
            cols = slice(n * 256, (n + 1) * 256)
            in_half = slice(n % 2 * 256, n % 2 * 256 + 256)
            parts = (t0[2 + n // 2, :, in_half], t1[2 + n // 2, :, in_half], t2[n // 2, :, in_half])
            table = sum(p.astype(f32) for p in parts).astype(bf16)
            factor = jnp.concatenate([b_ref[2 * n, mine], b_ref[2 * n + 1, mine]], axis=1)
            u = jnp.dot(o_ref[at], table, preferred_element_type=f32) + dot(
                spread_low, factor, 0, 0
            )
            d = d_ref[:, cols]
            g = g_ref[:, cols]
            rest = 1.0 - d
            h = jnp.zeros((per, 256), f32)
            for t in range(steps):
                span = slice(t * per, (t + 1) * per)
                h = d * h + rest * u[span]
                lifted_ref[span, cols] = (h * g).astype(bf16)
                hh = h * h
                hh = hh[:, :128] + hh[:, 128:]
                if n == 0:
                    square[span] = hh
                else:
                    square[span] += hh
            factor_in = jnp.concatenate([a_ref[2 * n, mine], a_ref[2 * n + 1, mine]], axis=1)
            total += dot(factor_in, lifted_ref[:, cols], 1, 1)
        sums = dot(jnp.ones((8, 128), f32), square[...], 1, 1, lax.Precision.HIGHEST)
        low_next = diagonal(total)
        row = lax.broadcasted_iota(jnp.int32, (8, rows), 0)
        stats_ref[...] = jnp.where(row < 4, sums, low_next)

    return pl.pallas_call(
        kernel,
        out_shape=[
            jax.ShapeDtypeStruct((rows, width), bf16),
            jax.ShapeDtypeStruct((8, rows), f32),
        ],
        in_specs=[VMEM] * 10,
        out_specs=[VMEM, VMEM],
        scratch_shapes=[pltpu.VMEM((rows, 128), f32)],
        compiler_params=params(16),
        name="first_layer",
        cost_estimate=small_cost,
    )(onehot, *table_parts, *lows, out_factors, in_factors, decay, gain)


def next_hidden(full_width, onehot, embedding, stats, lifted):
    rows = lifted[0].shape[0]
    total, width = rows * CHUNKS, embedding.shape[1]

    def kernel(o_ref, e_ref, s0, s1, up0, up1, up2, out_ref, last_ref):
        for k, up in enumerate((up0, up1, up2)):
            span = slice(k * rows, (k + 1) * rows)
            so_far = s0[:, span] + s1[:, span]
            norm = lax.rsqrt(so_far / full_width + norm_eps)
            norm_col = jnp.transpose(norm)[:, 0:1]
            x = jnp.dot(o_ref[span], e_ref[...], preferred_element_type=f32)
            x = (x + norm_col * up[...].astype(f32)).astype(bf16)
            out_ref[span] = x
            per = rows // 16
            last_ref[k * per : (k + 1) * per] = x[rows - per :].astype(f32)

    return pl.pallas_call(
        kernel,
        out_shape=[
            jax.ShapeDtypeStruct((total, width), bf16),
            jax.ShapeDtypeStruct((total // 16, width), f32),
        ],
        in_specs=[VMEM] * 7,
        out_specs=[VMEM] * 2,
        compiler_params=params(16),
        name="next_hidden",
        cost_estimate=small_cost,
    )(onehot, embedding, *stats, *lifted)


def second_layer(n, coef, full_width, hidden, lows, stats, halves, crossed, slot, out_factors,
                 decay, gain, reward, before):
    rows = hidden.shape[0] // CHUNKS
    group = out_factors.shape[1] // CHUNKS
    steps = 16
    per = rows // steps
    cols = slice(n * 256, (n + 1) * 256)

    def kernel(x_ref, l0, l1, s0, s1, own_ref, peer_ref, other_ref, b_ref, d_ref, g_ref, r_ref,
               before_ref, stats_ref, last_ref, square, lr, xr):
        factor = jnp.concatenate([b_ref[2 * n], b_ref[2 * n + 1]], axis=1)
        d = d_ref[:, cols]
        g = g_ref[:, cols]
        r = r_ref[:, cols]
        rest = 1.0 - d
        gr = g * r
        for k in range(CHUNKS):
            span_k = slice(k * rows, (k + 1) * rows)
            so_far = s0[:, span_k] + s1[:, span_k]
            norm = lax.rsqrt(so_far[0:1] / full_width + norm_eps)
            low = (l0[:, span_k] + l1[:, span_k] + norm * so_far) * coef
            spread_low = spread(low, 1, group)
            u = dot(spread_low, factor[k * group : (k + 1) * group], 0, 0) + (
                own_ref[0, span_k].astype(f32)
                + peer_ref[0, span_k].astype(f32)
                + other_ref[slot, span_k].astype(f32)
            )
            h = jnp.zeros((per, 256), f32)
            xrr = x_ref[span_k, cols].astype(f32) * r
            xr[span_k] = xrr[:, :128] + xrr[:, 128:]
            for t in range(steps):
                span = slice(k * rows + t * per, k * rows + (t + 1) * per)
                h = d * h + rest * u[t * per : (t + 1) * per]
                hr = h * gr
                hh = h * h
                square[span] = hh[:, :128] + hh[:, 128:]
                lr[span] = hr[:, :128] + hr[:, 128:]
            last_ref[k * per : (k + 1) * per] = h * g
        ones = jnp.ones((8, 128), f32)
        sums = [dot(ones, a[...], 1, 1, lax.Precision.HIGHEST) for a in (square, lr, xr)]
        row = lax.broadcasted_iota(jnp.int32, (8, rows * CHUNKS), 0)
        stats_ref[...] = before_ref[...] + jnp.where(
            row == 0, sums[0], jnp.where(row == 1, sums[1], sums[2])
        )

    total = rows * CHUNKS
    return pl.pallas_call(
        kernel,
        out_shape=[
            jax.ShapeDtypeStruct((8, total), f32),
            jax.ShapeDtypeStruct((per * CHUNKS, 256), f32),
        ],
        in_specs=[VMEM] * 13,
        out_specs=[VMEM] * 2,
        scratch_shapes=[pltpu.VMEM((total, 128), f32)] * 3,
        compiler_params=params(16),
        name="second_layer",
        cost_estimate=small_cost,
    )(hidden, *lows, *stats, *halves, crossed, out_factors, decay, gain, reward, before)


def step_kernel(where, arrived, arrived_peer, members, members_all, scale, earlier):
    pops, rows, lanes = arrived.shape
    k = members * 8
    part = k // 2 + 8
    blocks = (rows - 2 * part) // k
    width = blocks * lanes

    def kernel(where_ref, in_ref, peer_ref, _, mine_ref, theirs_ref, paired, digit_rows):
        xl, c = where_ref[4], where_ref[2]
        head = blocks * k
        for p in range(pops):
            digits = in_ref[p, head + k // 2 : head + k // 2 + 8, :].astype(f32)
            for i in range(4):
                digit_rows[i, p : p + 1, :] = digits[i : i + 1, :]
        lane = lax.broadcasted_iota(jnp.int32, (pops, lanes), 1)
        real = lane < members
        here = (digit_rows[0] * 32.0 + digit_rows[1]) / members_all
        there = (digit_rows[2] * 32.0 + digit_rows[3]) / members_all
        mean = (
            jnp.sum(jnp.where(real, here, 0.0), keepdims=True)
            + jnp.sum(jnp.where(real, there, 0.0), keepdims=True)
        ) / members_all
        here = jnp.where(real, here - mean, 0.0)
        there = jnp.where(real, there - mean, 0.0)
        var = (
            jnp.sum(here * here, keepdims=True) + jnp.sum(there * there, keepdims=True)
        ) / members_all
        shaped = here * (lax.rsqrt(var + spread_eps) * scale)
        pick = lax.broadcasted_iota(jnp.int32, (k, lanes), 0) // 8 == lax.broadcasted_iota(
            jnp.int32, (k, lanes), 1
        )
        by_row = dot(pick.astype(f32), shaped, 1, 1, lax.Precision.HIGHEST)
        layer = (lax.broadcasted_iota(jnp.int32, (k, lanes), 0) % 8) // 4
        for p in range(pops):
            at = slice(p * k, (p + 1) * k)
            for rel in range(2):
                lo = pl.multiple_of((xl ^ rel) * part, 8)
                mine = in_ref[p, pl.ds(head + lo, k // 2), :].astype(f32)
                theirs = peer_ref[p, pl.ds(lo, k // 2), :].astype(f32)
                o = jnp.concatenate(
                    [jnp.where(c == 0, mine, theirs), jnp.where(c == 0, theirs, mine)], axis=0
                )
                o = o * by_row[:, p : p + 1]
                for l in range(2):
                    col = (rel * 2 + l) * lanes
                    paired[at, col : col + lanes] = jnp.where(layer == l, o, 0.0).astype(bf16)
        right = paired[...]
        for b in range(0, blocks, 2):
            left = jnp.concatenate(
                [
                    jnp.concatenate(
                        [in_ref[p, b * k : (b + 1) * k, :], in_ref[p, (b + 1) * k : (b + 2) * k, :]],
                        axis=1,
                    )
                    for p in range(pops)
                ],
                axis=0,
            )
            out = dot(left, right, 0, 0)
            span = slice(b * lanes, (b + 2) * lanes)
            for l in range(2):
                mine_ref[l, span, :] = out[:, l * lanes : (l + 1) * lanes]
                theirs_ref[l, span, :] = out[:, (2 + l) * lanes : (3 + l) * lanes].astype(bf16)

    return pl.pallas_call(
        kernel,
        out_shape=[
            jax.ShapeDtypeStruct((2, width, lanes), f32),
            jax.ShapeDtypeStruct((2, width, lanes), bf16),
        ],
        in_specs=[SMEM, VMEM, VMEM, pl.BlockSpec(memory_space=pl.ANY)],
        out_specs=[VMEM, VMEM],
        scratch_shapes=[
            pltpu.VMEM((pops * k, 4 * lanes), bf16),
            pltpu.VMEM((4, pops, lanes), f32),
        ],
        compiler_params=params(24),
        name="weight_step",
        cost_estimate=small_cost,
    )(where, arrived, arrived_peer, earlier)


def shards(
    token_ids,
    fitness_ranks,
    embedding,
    mix_weights,
    factors_in,
    factors_out,
    decay_rates,
    norm_gain,
    reward_dir,
):
    members, seq_count, step_count = token_ids.shape
    vocab, width = embedding.shape
    full_width = mix_weights.shape[2]
    rank_count = factors_in.shape[2]
    pop_count = lax.axis_size(POP)
    members_all = members * pop_count
    coef = noise_scale * (full_width * rank_count) ** (-0.5)
    y, xl, z = (lax.axis_index(a) for a in POP)
    xh, c = (lax.axis_index(a) for a in MP)
    where = jnp.stack([z, xh, c, y, xl]).astype(jnp.int32)
    rows_all = members * seq_count * step_count

    order = token_ids.reshape(CHUNKS, -1, step_count).transpose(0, 2, 1).reshape(-1)
    onehot = (order[:, None] == jnp.arange(vocab, dtype=jnp.int32)[None, :]).astype(bf16)

    def added(a, b):
        return (a.astype(f32) + b.astype(f32)).astype(bf16)

    peer, own = product(0, where, embedding, mix_weights, 512)
    theirs = swap(peer, "c")
    cross = added(own[:2], theirs[:2])
    first_table = [own, theirs, swap(cross, "xh")]
    a_blocks = regroup(after(factors_in, peer), jnp.zeros((1,), jnp.int32))
    lows = mp_parts(low_kernel(after(onehot, peer), embedding, a_blocks))
    both = jnp.stack([fitness_ranks, swap(after(fitness_ranks, peer), "xl")])
    digits = jnp.stack([both[0] // 32, both[0] % 32, both[1] // 32, both[1] % 32]).astype(bf16)
    digits = jnp.pad(digits, ((0, 4), (0, 128 - members)))
    pops = lax.axis_size("y") * lax.axis_size("z")
    late_out = after(factors_out, cross)
    b_own = regroup(late_out, ((xh * 2 + c) * width).reshape(1).astype(jnp.int32))
    packed = pack(where, digits, a_blocks, late_out, pops)
    arrived = lax.all_to_all(after(packed, lows[0]), ("y", "z"), 0, 0, tiled=True)

    decay = [decay_rates[l : l + 1] for l in range(2)]
    gain = [norm_gain[l : l + 1] for l in range(2)]
    lifted, stats = [], []
    for k in range(CHUNKS):
        up, st = first_layer(
            k, where, coef, onehot, first_table, lows, b_own, a_blocks, decay[0], gain[0]
        )
        lifted.append(up)
        stats.append(st)
    stats = mp_parts(jnp.concatenate(stats, axis=1))
    late_weights = stay(1, after(mix_weights, stats[0]))
    hidden, last_hidden = next_hidden(full_width, onehot, embedding, stats, lifted)
    sent, parts, place = [], [], []
    for first, count in ((0, 3), (3, 1)):
        peer, own = dense(1, where, hidden, late_weights, 256, first, count, ())
        part = added(own, swap(peer, "c"))
        parts.append(part)
        sent.append(swap(part, "xh"))
        place += [(len(sent) - 1, n) for n in range(count)]
    halves = []
    for n in range(4):
        peer, own = dense(0, where, hidden, late_weights, 256, n, 1, (*parts, *(h[1] for h in halves)))
        halves.append((own, swap(peer, "c")))

    outs_rows = 2 * (members * rank_count + 8)
    tail_rows = after(arrived, halves[3][0])[:, -outs_rows:]
    arrived_peer = swap(tail_rows, "c")
    step_mine, step_theirs = step_kernel(
        where, arrived, arrived_peer, members, members_all,
        (members_all * rank_count) ** (-0.5), halves[3][0],
    )
    st = after(jnp.zeros((8, rows_all), f32), step_theirs)
    lasts = []
    for n in range(4):
        st, last = second_layer(
            n, coef, full_width, hidden, lows, stats, halves[n], sent[place[n][0]], place[n][1], b_own,
            decay[1], gain[1], reward_dir[None], st,
        )
        lasts.append(last)
    weight_step = step_mine + swap(after(step_theirs, sent[-1]), "xl").astype(f32)
    so_far = sum(mp_parts(st))
    norm = lax.rsqrt(so_far[0] / full_width + norm_eps)
    terms = (so_far[2] + norm * so_far[1]).reshape(CHUNKS, step_count, -1)
    tail = norm.reshape(CHUNKS, step_count, -1)[:, -1].reshape(-1)
    finals = last_hidden + jnp.concatenate(lasts, axis=1) * tail[:, None]
    final_features = finals.astype(bf16).reshape(members, seq_count, width)
    scores = jnp.mean(terms, axis=1).reshape(members, seq_count) * full_width ** (-0.5)
    return (final_features, scores, weight_step)


def solution(mesh):
    fine = Mesh(mesh.devices.reshape(4, 2, 4, 2, 2), POP + MP)
    return jax.shard_map(
        shards,
        mesh=fine,
        in_specs=(
            P(POP, None, None),
            P(POP),
            P(None, MP),
            P(None, MP, None),
            P(None, POP, None, MP),
            P(None, POP, None, None),
            P(None, MP),
            P(None, MP),
            P(MP),
        ),
        out_specs=(P(POP, None, MP), P(POP, None), P(None, MP, POP)),
        check_vma=False,
    )
```

```python
import jax
import jax.numpy as jnp
from jax import lax
from jax.experimental import pallas as pl
from jax.experimental.pallas import tpu as pltpu
from jax.sharding import Mesh
from jax.sharding import PartitionSpec as P

noise_scale = 0.25
norm_eps = 1e-06
spread_eps = 1e-05

POP = ("y", "xl", "z")
MP = ("xh", "c")
CHUNKS = 3
f32 = jnp.float32
bf16 = jnp.bfloat16
SMEM = pl.BlockSpec(memory_space=pltpu.SMEM)
VMEM = pl.BlockSpec(memory_space=pltpu.VMEM)
small_cost = pl.CostEstimate(flops=1000, bytes_accessed=1000, transcendentals=0)


def params(mib=24):
    return pltpu.CompilerParams(vmem_limit_bytes=mib * 1024 * 1024)


def swap(value, axis):
    return lax.ppermute(value, axis, [(0, 1), (1, 0)])


def after(value, *earlier):
    return lax.optimization_barrier((value, *earlier))[0]


def mp_parts(value):
    pair = value + swap(value, "c")
    return pair, swap(pair, "xh")


def dot(a, b, ca, cb, precision=None):
    return lax.dot_general(
        a, b, (((ca,), (cb,)), ((), ())), preferred_element_type=f32, precision=precision
    )


def regroup(factors, start):
    layers, members, ranks, _ = factors.shape
    blocks, k = 8, members * layers * ranks

    def kernel(start_ref, in_ref, out_ref):
        cols = pl.ds(pl.multiple_of(start_ref[0], 1024), 1024)
        for m in range(members):
            rows = jnp.concatenate(
                [in_ref[l, m, :, cols].astype(f32) for l in range(layers)], axis=0
            ).astype(bf16)
            for n in range(blocks):
                out_ref[n, m * 8 : m * 8 + 8, :] = rows[:, n * 128 : (n + 1) * 128]

    return pl.pallas_call(
        kernel,
        out_shape=jax.ShapeDtypeStruct((blocks, k, 128), bf16),
        in_specs=[SMEM, VMEM],
        out_specs=VMEM,
        compiler_params=params(16),
        name="regroup",
        cost_estimate=small_cost,
    )(start, factors)


def pack(where, digits, a_blocks, factors_out, pops):
    layers, members, ranks, full = factors_out.shape
    blocks, k, _ = a_blocks.shape
    half = members // 2
    part = k // 2 + 8
    rows = blocks * k + 2 * part

    def kernel(where_ref, digits_ref, a_ref, out_ref, packed_ref):
        c = where_ref[2]
        for m in range(half):
            b = jnp.concatenate(
                [out_ref[l, c * half + m].astype(f32) for l in range(layers)], axis=0
            ).astype(bf16)
            for o in range(2 * pops):
                y, x, z = o // 8, (o // 4) % 2, o % 4
                lo = blocks * k + x * part + m * 8
                packed_ref[y * 4 + z, lo : lo + 8, :] = b[:, o * 128 : (o + 1) * 128]
        for p in range(pops):
            for n in range(blocks):
                packed_ref[p, n * k : (n + 1) * k, :] = a_ref[n]
            for x in range(2):
                lo = blocks * k + x * part + k // 2
                packed_ref[p, lo : lo + 8, :] = digits_ref[...]

    return pl.pallas_call(
        kernel,
        out_shape=jax.ShapeDtypeStruct((pops, rows, 128), bf16),
        in_specs=[SMEM] + [VMEM] * 3,
        out_specs=VMEM,
        compiler_params=params(16),
        name="pack",
        cost_estimate=small_cost,
    )(where, digits, a_blocks, factors_out)


def product(layer, where, left, weights, piece):
    rows, width = left.shape
    full = weights.shape[2]
    per_owner = width // piece
    cuts = 4
    depth = width // cuts
    count = 2 * per_owner

    def kernel(where_ref, left_ref, w_ref, out0_ref, out1_ref, total):
        k = pl.program_id(0)
        part = left_ref[:, pl.ds(pl.multiple_of(k * depth, depth), depth)]

        @pl.when(k == 0)
        def _():
            for n in range(full // piece):
                cols = slice(n * piece, (n + 1) * piece)
                total[:, cols] = jnp.dot(part, w_ref[0, :, cols], preferred_element_type=f32)

        @pl.when(k > 0)
        def _():
            for n in range(full // piece):
                cols = slice(n * piece, (n + 1) * piece)
                total[:, cols] += jnp.dot(part, w_ref[0, :, cols], preferred_element_type=f32)

        @pl.when(k == cuts - 1)
        def _():
            for flip, out_ref in ((1, out0_ref), (0, out1_ref)):
                for i in range(count):
                    half = where_ref[1] ^ (1 - i // per_owner)
                    owner = half * 2 + (where_ref[2] ^ flip)
                    at = pl.multiple_of(owner * width + i % per_owner * piece, piece)
                    out_ref[i] = total[:, pl.ds(at, piece)].astype(bf16)

    return pl.pallas_call(
        kernel,
        grid=(cuts,),
        in_specs=[
            SMEM,
            pl.BlockSpec((rows, width), lambda k: (0, 0)),
            pl.BlockSpec((1, depth, full), lambda k: (layer, k, 0)),
        ],
        out_specs=[pl.BlockSpec((count, rows, piece), lambda k: (0, 0, 0))] * 2,
        out_shape=[jax.ShapeDtypeStruct((count, rows, piece), bf16)] * 2,
        scratch_shapes=[pltpu.VMEM((rows, full), f32)],
        compiler_params=params(48),
        name="product",
        cost_estimate=small_cost,
    )(where, left, weights)


def stay(layer, weights):
    _, width, full = weights.shape
    cuts = 8
    rows = width // cuts

    def kernel(w_ref, out_ref, sems):
        def part(i):
            span = slice(i * rows, (i + 1) * rows)
            return pltpu.make_async_copy(w_ref.at[layer, span], out_ref.at[span], sems.at[i])

        for i in range(cuts):
            part(i).start()
        for i in range(cuts):
            part(i).wait()

    return pl.pallas_call(
        kernel,
        out_shape=jax.ShapeDtypeStruct((width, full), bf16),
        in_specs=[pl.BlockSpec(memory_space=pltpu.HBM)],
        out_specs=VMEM,
        scratch_shapes=[pltpu.SemaphoreType.DMA((cuts,))],
        compiler_params=params(40),
        name="stay",
        cost_estimate=small_cost,
    )(weights)


def dense(rel, where, left, weights, piece, first=0, count=1, earlier=()):
    rows, width = left.shape

    def kernel(where_ref, left_ref, w_ref, *refs):
        out0_ref, out1_ref = refs[len(earlier) :]
        for flip, out_ref in ((1, out0_ref), (0, out1_ref)):
            owner = (where_ref[1] ^ rel) * 2 + (where_ref[2] ^ flip)
            for n in range(count):
                at = pl.multiple_of(owner * width + (first + n) * piece, piece)
                out_ref[n] = jnp.dot(
                    left_ref[...], w_ref[:, pl.ds(at, piece)], preferred_element_type=f32
                ).astype(bf16)

    return pl.pallas_call(
        kernel,
        out_shape=[jax.ShapeDtypeStruct((count, rows, piece), bf16)] * 2,
        in_specs=[SMEM, VMEM, VMEM] + [pl.BlockSpec(memory_space=pl.ANY)] * len(earlier),
        out_specs=[VMEM] * 2,
        compiler_params=params(16),
        name="dense",
        cost_estimate=small_cost,
    )(where, left, weights, *earlier)


def member_of(shape, per, dim):
    return lax.broadcasted_iota(jnp.int32, shape, dim) // per


def low_kernel(onehot, embedding, factors):
    rows = onehot.shape[0]
    per_chunk = rows // CHUNKS
    group = factors.shape[1] // CHUNKS

    def kernel(o_ref, e_ref, a_ref, out_ref):
        for k in range(CHUNKS):
            x = jnp.dot(
                o_ref[k * per_chunk : (k + 1) * per_chunk, :], e_ref[...], preferred_element_type=f32
            ).astype(bf16)
            total = jnp.zeros((group, per_chunk), f32)
            for b in range(factors.shape[0]):
                total += dot(
                    a_ref[b, k * group : (k + 1) * group, :], x[:, b * 128 : (b + 1) * 128], 1, 1
                )
            out_ref[:, k * per_chunk : (k + 1) * per_chunk] = diagonal(total)

    return pl.pallas_call(
        kernel,
        out_shape=jax.ShapeDtypeStruct((8, rows), f32),
        in_specs=[VMEM] * 3,
        out_specs=VMEM,
        compiler_params=params(),
        name="low",
        cost_estimate=small_cost,
    )(onehot, embedding, factors)


def diagonal(total):
    group, cols = total.shape
    row_member = member_of((group, cols), 8, 0)
    col_member = (lax.broadcasted_iota(jnp.int32, (group, cols), 1) % 16) // 4
    kept = jnp.where(row_member == col_member, total, 0.0)
    out = kept[0:8]
    for m in range(1, group // 8):
        out = out + kept[m * 8 : (m + 1) * 8]
    return out


def spread(low, layer, group):
    cols = low.shape[1]
    row = lax.broadcasted_iota(jnp.int32, (group, cols), 0)
    col_member = (lax.broadcasted_iota(jnp.int32, (group, cols), 1) % 16) // 4
    keep = (row // 8 == col_member) & ((row % 8) // 4 == layer)
    tiled = jnp.concatenate([low] * (group // 8), axis=0)
    return jnp.where(keep, tiled, 0.0).astype(bf16)


def first_layer(chunk, where, coef, onehot, table, lows, out_factors, in_factors, decay, gain):
    rows = onehot.shape[0] // CHUNKS
    group = out_factors.shape[1] // CHUNKS
    width = decay.shape[1]
    steps = 16
    per = rows // steps

    def kernel(o_ref, t_ref, l0, l1, b_ref, a_ref, d_ref, g_ref, lifted_ref, stats_ref, square):
        at = slice(chunk * rows, (chunk + 1) * rows)
        mine = slice(chunk * group, (chunk + 1) * group)
        low = (l0[:, at] + l1[:, at]) * coef
        spread_low = spread(low, 0, group)
        total = jnp.zeros((group, rows), f32)
        for n in range(width // 256):
            cols = slice(n * 256, (n + 1) * 256)
            in_half = slice(n % 2 * 256, n % 2 * 256 + 256)
            table = t_ref[n // 2, :, in_half]
            factor = jnp.concatenate([b_ref[2 * n, mine], b_ref[2 * n + 1, mine]], axis=1)
            u = jnp.dot(o_ref[at], table, preferred_element_type=f32) + dot(
                spread_low, factor, 0, 0
            )
            d = d_ref[:, cols]
            g = g_ref[:, cols]
            rest = 1.0 - d
            h = jnp.zeros((per, 256), f32)
            for t in range(steps):
                span = slice(t * per, (t + 1) * per)
                h = d * h + rest * u[span]
                lifted_ref[span, cols] = (h * g).astype(bf16)
                hh = h * h
                hh = hh[:, :128] + hh[:, 128:]
                if n == 0:
                    square[span] = hh
                else:
                    square[span] += hh
            factor_in = jnp.concatenate([a_ref[2 * n, mine], a_ref[2 * n + 1, mine]], axis=1)
            total += dot(factor_in, lifted_ref[:, cols], 1, 1)
        sums = dot(jnp.ones((8, 128), f32), square[...], 1, 1, lax.Precision.HIGHEST)
        low_next = diagonal(total)
        row = lax.broadcasted_iota(jnp.int32, (8, rows), 0)
        stats_ref[...] = jnp.where(row < 4, sums, low_next)

    return pl.pallas_call(
        kernel,
        out_shape=[
            jax.ShapeDtypeStruct((rows, width), bf16),
            jax.ShapeDtypeStruct((8, rows), f32),
        ],
        in_specs=[VMEM] * 8,
        out_specs=[VMEM, VMEM],
        scratch_shapes=[pltpu.VMEM((rows, 128), f32)],
        compiler_params=params(16),
        name="first_layer",
        cost_estimate=small_cost,
    )(onehot, table, *lows, out_factors, in_factors, decay, gain)


def next_hidden(full_width, onehot, embedding, stats, lifted):
    rows = lifted[0].shape[0]
    total, width = rows * CHUNKS, embedding.shape[1]

    def kernel(o_ref, e_ref, s0, s1, up0, up1, up2, out_ref, last_ref):
        for k, up in enumerate((up0, up1, up2)):
            span = slice(k * rows, (k + 1) * rows)
            so_far = s0[:, span] + s1[:, span]
            norm = lax.rsqrt(so_far / full_width + norm_eps)
            norm_col = jnp.transpose(norm)[:, 0:1]
            x = jnp.dot(o_ref[span], e_ref[...], preferred_element_type=f32)
            x = (x + norm_col * up[...].astype(f32)).astype(bf16)
            out_ref[span] = x
            per = rows // 16
            last_ref[k * per : (k + 1) * per] = x[rows - per :].astype(f32)

    return pl.pallas_call(
        kernel,
        out_shape=[
            jax.ShapeDtypeStruct((total, width), bf16),
            jax.ShapeDtypeStruct((total // 16, width), f32),
        ],
        in_specs=[VMEM] * 7,
        out_specs=[VMEM] * 2,
        compiler_params=params(16),
        name="next_hidden",
        cost_estimate=small_cost,
    )(onehot, embedding, *stats, *lifted)


def second_layer(n, coef, full_width, hidden, lows, stats, halves, crossed, slot, out_factors,
                 decay, gain, reward, before):
    rows = hidden.shape[0] // CHUNKS
    group = out_factors.shape[1] // CHUNKS
    steps = 16
    per = rows // steps
    cols = slice(n * 256, (n + 1) * 256)

    def kernel(x_ref, l0, l1, s0, s1, own_ref, peer_ref, other_ref, b_ref, d_ref, g_ref, r_ref,
               before_ref, stats_ref, last_ref, square, lr, xr, other, sem):
        fetch = pltpu.make_async_copy(other_ref.at[slot], other, sem)
        fetch.start()
        factor = jnp.concatenate([b_ref[2 * n], b_ref[2 * n + 1]], axis=1)
        d = d_ref[:, cols]
        g = g_ref[:, cols]
        r = r_ref[:, cols]
        rest = 1.0 - d
        gr = g * r
        for k in range(CHUNKS):
            span_k = slice(k * rows, (k + 1) * rows)
            xrr = x_ref[span_k, cols].astype(f32) * r
            xr[span_k] = xrr[:, :128] + xrr[:, 128:]
        fetch.wait()
        for k in range(CHUNKS):
            span_k = slice(k * rows, (k + 1) * rows)
            so_far = s0[:, span_k] + s1[:, span_k]
            norm = lax.rsqrt(so_far[0:1] / full_width + norm_eps)
            low = (l0[:, span_k] + l1[:, span_k] + norm * so_far) * coef
            spread_low = spread(low, 1, group)
            u = dot(spread_low, factor[k * group : (k + 1) * group], 0, 0) + (
                own_ref[0, span_k].astype(f32)
                + peer_ref[0, span_k].astype(f32)
                + other[span_k].astype(f32)
            )
            h = jnp.zeros((per, 256), f32)
            for t in range(steps):
                span = slice(k * rows + t * per, k * rows + (t + 1) * per)
                h = d * h + rest * u[t * per : (t + 1) * per]
                hr = h * gr
                hh = h * h
                square[span] = hh[:, :128] + hh[:, 128:]
                lr[span] = hr[:, :128] + hr[:, 128:]
            last_ref[k * per : (k + 1) * per] = h * g
        ones = jnp.ones((8, 128), f32)
        sums = [dot(ones, a[...], 1, 1, lax.Precision.HIGHEST) for a in (square, lr, xr)]
        row = lax.broadcasted_iota(jnp.int32, (8, rows * CHUNKS), 0)
        stats_ref[...] = before_ref[...] + jnp.where(
            row == 0, sums[0], jnp.where(row == 1, sums[1], sums[2])
        )

    total = rows * CHUNKS
    return pl.pallas_call(
        kernel,
        out_shape=[
            jax.ShapeDtypeStruct((8, total), f32),
            jax.ShapeDtypeStruct((per * CHUNKS, 256), f32),
        ],
        in_specs=[VMEM] * 7 + [pl.BlockSpec(memory_space=pl.ANY)] + [VMEM] * 5,
        out_specs=[VMEM] * 2,
        scratch_shapes=[pltpu.VMEM((total, 128), f32)] * 3
        + [pltpu.VMEM((total, 256), bf16), pltpu.SemaphoreType.DMA],
        compiler_params=params(16),
        name="second_layer",
        cost_estimate=small_cost,
    )(hidden, *lows, *stats, *halves, crossed, out_factors, decay, gain, reward, before)


def step_kernel(where, arrived, arrived_peer, members, members_all, scale, earlier):
    pops, rows, lanes = arrived.shape
    k = members * 8
    part = k // 2 + 8
    blocks = (rows - 2 * part) // k
    width = blocks * lanes

    def kernel(where_ref, in_ref, peer_ref, _, mine_ref, theirs_ref, paired, digit_rows):
        xl, c = where_ref[4], where_ref[2]
        head = blocks * k
        for p in range(pops):
            digits = in_ref[p, head + k // 2 : head + k // 2 + 8, :].astype(f32)
            for i in range(4):
                digit_rows[i, p : p + 1, :] = digits[i : i + 1, :]
        lane = lax.broadcasted_iota(jnp.int32, (pops, lanes), 1)
        real = lane < members
        here = (digit_rows[0] * 32.0 + digit_rows[1]) / members_all
        there = (digit_rows[2] * 32.0 + digit_rows[3]) / members_all
        mean = (
            jnp.sum(jnp.where(real, here, 0.0), keepdims=True)
            + jnp.sum(jnp.where(real, there, 0.0), keepdims=True)
        ) / members_all
        here = jnp.where(real, here - mean, 0.0)
        there = jnp.where(real, there - mean, 0.0)
        var = (
            jnp.sum(here * here, keepdims=True) + jnp.sum(there * there, keepdims=True)
        ) / members_all
        shaped = here * (lax.rsqrt(var + spread_eps) * scale)
        pick = lax.broadcasted_iota(jnp.int32, (k, lanes), 0) // 8 == lax.broadcasted_iota(
            jnp.int32, (k, lanes), 1
        )
        by_row = dot(pick.astype(f32), shaped, 1, 1, lax.Precision.HIGHEST)
        layer = (lax.broadcasted_iota(jnp.int32, (k, lanes), 0) % 8) // 4
        for p in range(pops):
            at = slice(p * k, (p + 1) * k)
            for rel in range(2):
                lo = pl.multiple_of((xl ^ rel) * part, 8)
                mine = in_ref[p, pl.ds(head + lo, k // 2), :].astype(f32)
                theirs = peer_ref[p, pl.ds(lo, k // 2), :].astype(f32)
                o = jnp.concatenate(
                    [jnp.where(c == 0, mine, theirs), jnp.where(c == 0, theirs, mine)], axis=0
                )
                o = o * by_row[:, p : p + 1]
                for l in range(2):
                    col = (rel * 2 + l) * lanes
                    paired[at, col : col + lanes] = jnp.where(layer == l, o, 0.0).astype(bf16)
        right = paired[...]
        for b in range(0, blocks, 2):
            left = jnp.concatenate(
                [
                    jnp.concatenate(
                        [in_ref[p, b * k : (b + 1) * k, :], in_ref[p, (b + 1) * k : (b + 2) * k, :]],
                        axis=1,
                    )
                    for p in range(pops)
                ],
                axis=0,
            )
            out = dot(left, right, 0, 0)
            span = slice(b * lanes, (b + 2) * lanes)
            for l in range(2):
                mine_ref[l, span, :] = out[:, l * lanes : (l + 1) * lanes]
                theirs_ref[l, span, :] = out[:, (2 + l) * lanes : (3 + l) * lanes].astype(bf16)

    return pl.pallas_call(
        kernel,
        out_shape=[
            jax.ShapeDtypeStruct((2, width, lanes), f32),
            jax.ShapeDtypeStruct((2, width, lanes), bf16),
        ],
        in_specs=[SMEM, VMEM, VMEM, pl.BlockSpec(memory_space=pl.ANY)],
        out_specs=[VMEM, VMEM],
        scratch_shapes=[
            pltpu.VMEM((pops * k, 4 * lanes), bf16),
            pltpu.VMEM((4, pops, lanes), f32),
        ],
        compiler_params=params(24),
        name="weight_step",
        cost_estimate=small_cost,
    )(where, arrived, arrived_peer, earlier)


def shards(
    token_ids,
    fitness_ranks,
    embedding,
    mix_weights,
    factors_in,
    factors_out,
    decay_rates,
    norm_gain,
    reward_dir,
):
    members, seq_count, step_count = token_ids.shape
    vocab, width = embedding.shape
    full_width = mix_weights.shape[2]
    rank_count = factors_in.shape[2]
    pop_count = lax.axis_size(POP)
    members_all = members * pop_count
    coef = noise_scale * (full_width * rank_count) ** (-0.5)
    y, xl, z = (lax.axis_index(a) for a in POP)
    xh, c = (lax.axis_index(a) for a in MP)
    where = jnp.stack([z, xh, c, y, xl]).astype(jnp.int32)
    rows_all = members * seq_count * step_count

    order = token_ids.reshape(CHUNKS, -1, step_count).transpose(0, 2, 1).reshape(-1)
    onehot = (order[:, None] == jnp.arange(vocab, dtype=jnp.int32)[None, :]).astype(bf16)

    def added(a, b):
        return (a.astype(f32) + b.astype(f32)).astype(bf16)

    peer, own = product(0, where, embedding, mix_weights, 512)
    theirs = swap(peer, "c")
    cross = added(own[:2], theirs[:2])
    first_table = (
        own[2:].astype(f32) + theirs[2:].astype(f32) + swap(cross, "xh").astype(f32)
    ).astype(bf16)
    a_blocks = regroup(after(factors_in, peer), jnp.zeros((1,), jnp.int32))
    lows = mp_parts(low_kernel(after(onehot, peer), embedding, a_blocks))
    both = jnp.stack([fitness_ranks, swap(after(fitness_ranks, peer), "xl")])
    digits = jnp.stack([both[0] // 32, both[0] % 32, both[1] // 32, both[1] % 32]).astype(bf16)
    digits = jnp.pad(digits, ((0, 4), (0, 128 - members)))
    pops = lax.axis_size("y") * lax.axis_size("z")
    late_out = after(factors_out, cross)
    b_own = regroup(late_out, ((xh * 2 + c) * width).reshape(1).astype(jnp.int32))
    packed = pack(where, digits, a_blocks, late_out, pops)
    arrived = lax.all_to_all(after(packed, lows[0]), ("y", "z"), 0, 0, tiled=True)

    decay = [decay_rates[l : l + 1] for l in range(2)]
    gain = [norm_gain[l : l + 1] for l in range(2)]
    lifted, stats = [], []
    for k in range(CHUNKS):
        up, st = first_layer(
            k, where, coef, onehot, first_table, lows, b_own, a_blocks, decay[0], gain[0]
        )
        lifted.append(up)
        stats.append(st)
    stats = mp_parts(jnp.concatenate(stats, axis=1))
    late_weights = stay(1, after(mix_weights, stats[0]))
    hidden, last_hidden = next_hidden(full_width, onehot, embedding, stats, lifted)
    sent, parts, place = [], [], []
    for first, count in ((0, 3), (3, 1)):
        peer, own = dense(1, where, hidden, late_weights, 256, first, count, ())
        part = added(own, swap(peer, "c"))
        parts.append(part)
        sent.append(swap(part, "xh"))
        place += [(len(sent) - 1, n) for n in range(count)]
    halves = []
    for n in range(4):
        peer, own = dense(0, where, hidden, late_weights, 256, n, 1, (*parts, *(h[1] for h in halves)))
        halves.append((own, swap(peer, "c")))

    outs_rows = 2 * (members * rank_count + 8)
    tail_rows = after(arrived, halves[3][0])[:, -outs_rows:]
    arrived_peer = swap(tail_rows, "c")
    step_mine, step_theirs = step_kernel(
        where, arrived, arrived_peer, members, members_all,
        (members_all * rank_count) ** (-0.5), halves[3][0],
    )
    st = after(jnp.zeros((8, rows_all), f32), step_theirs)
    lasts = []
    for n in range(4):
        st, last = second_layer(
            n, coef, full_width, hidden, lows, stats, halves[n], sent[place[n][0]], place[n][1], b_own,
            decay[1], gain[1], reward_dir[None], st,
        )
        lasts.append(last)
    weight_step = step_mine + swap(after(step_theirs, sent[-1]), "xl").astype(f32)
    so_far = sum(mp_parts(st))
    norm = lax.rsqrt(so_far[0] / full_width + norm_eps)
    terms = (so_far[2] + norm * so_far[1]).reshape(CHUNKS, step_count, -1)
    tail = norm.reshape(CHUNKS, step_count, -1)[:, -1].reshape(-1)
    finals = last_hidden + jnp.concatenate(lasts, axis=1) * tail[:, None]
    final_features = finals.astype(bf16).reshape(members, seq_count, width)
    scores = jnp.mean(terms, axis=1).reshape(members, seq_count) * full_width ** (-0.5)
    return (final_features, scores, weight_step)


def solution(mesh):
    fine = Mesh(mesh.devices.reshape(4, 2, 4, 2, 2), POP + MP)
    return jax.shard_map(
        shards,
        mesh=fine,
        in_specs=(
            P(POP, None, None),
            P(POP),
            P(None, MP),
            P(None, MP, None),
            P(None, POP, None, MP),
            P(None, POP, None, None),
            P(None, MP),
            P(None, MP),
            P(MP),
        ),
        out_specs=(P(POP, None, MP), P(POP, None), P(None, MP, POP)),
        check_vma=False,
    )
```

```python
import jax
import jax.numpy as jnp
from jax import lax
from jax.experimental import pallas as pl
from jax.experimental.pallas import tpu as pltpu
from jax.sharding import Mesh
from jax.sharding import PartitionSpec as P

noise_scale = 0.25
norm_eps = 1e-06
spread_eps = 1e-05

POP = ("y", "xl", "z")
MP = ("xh", "c")
CHUNKS = 3
f32 = jnp.float32
bf16 = jnp.bfloat16
SMEM = pl.BlockSpec(memory_space=pltpu.SMEM)
VMEM = pl.BlockSpec(memory_space=pltpu.VMEM)
small_cost = pl.CostEstimate(flops=1000, bytes_accessed=1000, transcendentals=0)


def params(mib=24):
    return pltpu.CompilerParams(vmem_limit_bytes=mib * 1024 * 1024)


def swap(value, axis):
    return lax.ppermute(value, axis, [(0, 1), (1, 0)])


def after(value, *earlier):
    return lax.optimization_barrier((value, *earlier))[0]


def mp_parts(value):
    pair = value + swap(value, "c")
    return pair, swap(pair, "xh")


def dot(a, b, ca, cb, precision=None):
    return lax.dot_general(
        a, b, (((ca,), (cb,)), ((), ())), preferred_element_type=f32, precision=precision
    )


def regroup(factors, start):
    layers, members, ranks, _ = factors.shape
    blocks, k = 8, members * layers * ranks

    def kernel(start_ref, in_ref, out_ref):
        cols = pl.ds(pl.multiple_of(start_ref[0], 1024), 1024)
        for m in range(members):
            rows = jnp.concatenate(
                [in_ref[l, m, :, cols].astype(f32) for l in range(layers)], axis=0
            ).astype(bf16)
            for n in range(blocks):
                out_ref[n, m * 8 : m * 8 + 8, :] = rows[:, n * 128 : (n + 1) * 128]

    return pl.pallas_call(
        kernel,
        out_shape=jax.ShapeDtypeStruct((blocks, k, 128), bf16),
        in_specs=[SMEM, VMEM],
        out_specs=VMEM,
        compiler_params=params(16),
        name="regroup",
        cost_estimate=small_cost,
    )(start, factors)


def pack(where, digits, a_blocks, factors_out, pops):
    layers, members, ranks, full = factors_out.shape
    blocks, k, _ = a_blocks.shape
    half = members // 2
    part = k // 2 + 8
    rows = blocks * k + 2 * part

    def kernel(where_ref, digits_ref, a_ref, out_ref, packed_ref):
        c = where_ref[2]
        for m in range(half):
            b = jnp.concatenate(
                [out_ref[l, c * half + m].astype(f32) for l in range(layers)], axis=0
            ).astype(bf16)
            for o in range(2 * pops):
                y, x, z = o // 8, (o // 4) % 2, o % 4
                lo = blocks * k + x * part + m * 8
                packed_ref[y * 4 + z, lo : lo + 8, :] = b[:, o * 128 : (o + 1) * 128]
        for p in range(pops):
            for n in range(blocks):
                packed_ref[p, n * k : (n + 1) * k, :] = a_ref[n]
            for x in range(2):
                lo = blocks * k + x * part + k // 2
                packed_ref[p, lo : lo + 8, :] = digits_ref[...]

    return pl.pallas_call(
        kernel,
        out_shape=jax.ShapeDtypeStruct((pops, rows, 128), bf16),
        in_specs=[SMEM] + [VMEM] * 3,
        out_specs=VMEM,
        compiler_params=params(16),
        name="pack",
        cost_estimate=small_cost,
    )(where, digits, a_blocks, factors_out)


def product(layer, where, left, weights, piece):
    rows, width = left.shape
    full = weights.shape[2]
    per_owner = width // piece
    cuts = 4
    depth = width // cuts
    count = 2 * per_owner

    def kernel(where_ref, left_ref, w_ref, out0_ref, out1_ref, total):
        k = pl.program_id(0)
        part = left_ref[:, pl.ds(pl.multiple_of(k * depth, depth), depth)]

        @pl.when(k == 0)
        def _():
            for n in range(full // piece):
                cols = slice(n * piece, (n + 1) * piece)
                total[:, cols] = jnp.dot(part, w_ref[0, :, cols], preferred_element_type=f32)

        @pl.when(k > 0)
        def _():
            for n in range(full // piece):
                cols = slice(n * piece, (n + 1) * piece)
                total[:, cols] += jnp.dot(part, w_ref[0, :, cols], preferred_element_type=f32)

        @pl.when(k == cuts - 1)
        def _():
            for flip, out_ref in ((1, out0_ref), (0, out1_ref)):
                for i in range(count):
                    half = where_ref[1] ^ (1 - i // per_owner)
                    owner = half * 2 + (where_ref[2] ^ flip)
                    at = pl.multiple_of(owner * width + i % per_owner * piece, piece)
                    out_ref[i] = total[:, pl.ds(at, piece)].astype(bf16)

    return pl.pallas_call(
        kernel,
        grid=(cuts,),
        in_specs=[
            SMEM,
            pl.BlockSpec((rows, width), lambda k: (0, 0)),
            pl.BlockSpec((1, depth, full), lambda k: (layer, k, 0)),
        ],
        out_specs=[pl.BlockSpec((count, rows, piece), lambda k: (0, 0, 0))] * 2,
        out_shape=[jax.ShapeDtypeStruct((count, rows, piece), bf16)] * 2,
        scratch_shapes=[pltpu.VMEM((rows, full), f32)],
        compiler_params=params(48),
        name="product",
        cost_estimate=small_cost,
    )(where, left, weights)


def stay(layer, weights):
    _, width, full = weights.shape
    cuts = 8
    rows = width // cuts

    def kernel(w_ref, out_ref, sems):
        def part(i):
            span = slice(i * rows, (i + 1) * rows)
            return pltpu.make_async_copy(w_ref.at[layer, span], out_ref.at[span], sems.at[i])

        for i in range(cuts):
            part(i).start()
        for i in range(cuts):
            part(i).wait()

    return pl.pallas_call(
        kernel,
        out_shape=jax.ShapeDtypeStruct((width, full), bf16),
        in_specs=[pl.BlockSpec(memory_space=pltpu.HBM)],
        out_specs=VMEM,
        scratch_shapes=[pltpu.SemaphoreType.DMA((cuts,))],
        compiler_params=params(40),
        name="stay",
        cost_estimate=small_cost,
    )(weights)


def dense(rel, where, left, weights, piece, first=0, count=1, earlier=()):
    rows, width = left.shape

    def kernel(where_ref, left_ref, w_ref, *refs):
        out0_ref, out1_ref = refs[len(earlier) :]
        for flip, out_ref in ((1, out0_ref), (0, out1_ref)):
            owner = (where_ref[1] ^ rel) * 2 + (where_ref[2] ^ flip)
            for n in range(count):
                at = pl.multiple_of(owner * width + (first + n) * piece, piece)
                out_ref[n] = jnp.dot(
                    left_ref[...], w_ref[:, pl.ds(at, piece)], preferred_element_type=f32
                ).astype(bf16)

    return pl.pallas_call(
        kernel,
        out_shape=[jax.ShapeDtypeStruct((count, rows, piece), bf16)] * 2,
        in_specs=[SMEM, VMEM, VMEM] + [pl.BlockSpec(memory_space=pl.ANY)] * len(earlier),
        out_specs=[VMEM] * 2,
        compiler_params=params(16),
        name="dense",
        cost_estimate=small_cost,
    )(where, left, weights, *earlier)


def member_of(shape, per, dim):
    return lax.broadcasted_iota(jnp.int32, shape, dim) // per


def low_kernel(onehot, embedding, factors):
    rows = onehot.shape[0]
    per_chunk = rows // CHUNKS
    group = factors.shape[1] // CHUNKS

    def kernel(o_ref, e_ref, a_ref, out_ref):
        for k in range(CHUNKS):
            x = jnp.dot(
                o_ref[k * per_chunk : (k + 1) * per_chunk, :], e_ref[...], preferred_element_type=f32
            ).astype(bf16)
            total = jnp.zeros((group, per_chunk), f32)
            for b in range(factors.shape[0]):
                total += dot(
                    a_ref[b, k * group : (k + 1) * group, :], x[:, b * 128 : (b + 1) * 128], 1, 1
                )
            out_ref[:, k * per_chunk : (k + 1) * per_chunk] = diagonal(total)

    return pl.pallas_call(
        kernel,
        out_shape=jax.ShapeDtypeStruct((8, rows), f32),
        in_specs=[VMEM] * 3,
        out_specs=VMEM,
        compiler_params=params(),
        name="low",
        cost_estimate=small_cost,
    )(onehot, embedding, factors)


def diagonal(total):
    group, cols = total.shape
    row_member = member_of((group, cols), 8, 0)
    col_member = (lax.broadcasted_iota(jnp.int32, (group, cols), 1) % 16) // 4
    kept = jnp.where(row_member == col_member, total, 0.0)
    out = kept[0:8]
    for m in range(1, group // 8):
        out = out + kept[m * 8 : (m + 1) * 8]
    return out


def spread(low, layer, group):
    cols = low.shape[1]
    row = lax.broadcasted_iota(jnp.int32, (group, cols), 0)
    col_member = (lax.broadcasted_iota(jnp.int32, (group, cols), 1) % 16) // 4
    keep = (row // 8 == col_member) & ((row % 8) // 4 == layer)
    tiled = jnp.concatenate([low] * (group // 8), axis=0)
    return jnp.where(keep, tiled, 0.0).astype(bf16)


def first_layer(chunk, where, coef, onehot, table, lows, out_factors, in_factors, decay, gain):
    rows = onehot.shape[0] // CHUNKS
    group = out_factors.shape[1] // CHUNKS
    width = decay.shape[1]
    steps = 16
    per = rows // steps

    def kernel(o_ref, t_ref, l0, l1, b_ref, a_ref, d_ref, g_ref, lifted_ref, stats_ref, square):
        at = slice(chunk * rows, (chunk + 1) * rows)
        mine = slice(chunk * group, (chunk + 1) * group)
        low = (l0[:, at] + l1[:, at]) * coef
        spread_low = spread(low, 0, group)
        total = jnp.zeros((group, rows), f32)
        for n in range(width // 256):
            cols = slice(n * 256, (n + 1) * 256)
            in_half = slice(n % 2 * 256, n % 2 * 256 + 256)
            table = t_ref[n // 2, :, in_half]
            factor = jnp.concatenate([b_ref[2 * n, mine], b_ref[2 * n + 1, mine]], axis=1)
            u = jnp.dot(o_ref[at], table, preferred_element_type=f32) + dot(
                spread_low, factor, 0, 0
            )
            d = d_ref[:, cols]
            g = g_ref[:, cols]
            rest = 1.0 - d
            h = jnp.zeros((per, 256), f32)
            for t in range(steps):
                span = slice(t * per, (t + 1) * per)
                h = d * h + rest * u[span]
                lifted_ref[span, cols] = (h * g).astype(bf16)
                hh = h * h
                hh = hh[:, :128] + hh[:, 128:]
                if n == 0:
                    square[span] = hh
                else:
                    square[span] += hh
            factor_in = jnp.concatenate([a_ref[2 * n, mine], a_ref[2 * n + 1, mine]], axis=1)
            total += dot(factor_in, lifted_ref[:, cols], 1, 1)
        sums = dot(jnp.ones((8, 128), f32), square[...], 1, 1, lax.Precision.HIGHEST)
        low_next = diagonal(total)
        row = lax.broadcasted_iota(jnp.int32, (8, rows), 0)
        stats_ref[...] = jnp.where(row < 4, sums, low_next)

    return pl.pallas_call(
        kernel,
        out_shape=[
            jax.ShapeDtypeStruct((rows, width), bf16),
            jax.ShapeDtypeStruct((8, rows), f32),
        ],
        in_specs=[VMEM] * 8,
        out_specs=[VMEM, VMEM],
        scratch_shapes=[pltpu.VMEM((rows, 128), f32)],
        compiler_params=params(16),
        name="first_layer",
        cost_estimate=small_cost,
    )(onehot, table, *lows, out_factors, in_factors, decay, gain)


def next_hidden(full_width, onehot, embedding, stats, lifted):
    rows = lifted[0].shape[0]
    total, width = rows * CHUNKS, embedding.shape[1]

    def kernel(o_ref, e_ref, s0, s1, up0, up1, up2, out_ref, last_ref):
        for k, up in enumerate((up0, up1, up2)):
            span = slice(k * rows, (k + 1) * rows)
            so_far = s0[:, span] + s1[:, span]
            norm = lax.rsqrt(so_far / full_width + norm_eps)
            norm_col = jnp.transpose(norm)[:, 0:1]
            x = jnp.dot(o_ref[span], e_ref[...], preferred_element_type=f32)
            x = (x + norm_col * up[...].astype(f32)).astype(bf16)
            out_ref[span] = x
            per = rows // 16
            last_ref[k * per : (k + 1) * per] = x[rows - per :].astype(f32)

    return pl.pallas_call(
        kernel,
        out_shape=[
            jax.ShapeDtypeStruct((total, width), bf16),
            jax.ShapeDtypeStruct((total // 16, width), f32),
        ],
        in_specs=[VMEM] * 7,
        out_specs=[VMEM] * 2,
        compiler_params=params(16),
        name="next_hidden",
        cost_estimate=small_cost,
    )(onehot, embedding, *stats, *lifted)


def second_layer(n, coef, full_width, hidden, lows, stats, halves, crossed, slot, out_factors,
                 decay, gain, reward, before):
    rows = hidden.shape[0] // CHUNKS
    group = out_factors.shape[1] // CHUNKS
    steps = 16
    per = rows // steps
    cols = slice(n * 256, (n + 1) * 256)

    def kernel(x_ref, l0, l1, s0, s1, own_ref, peer_ref, other_ref, b_ref, d_ref, g_ref, r_ref,
               before_ref, stats_ref, last_ref, square, lr, xr, other, sem):
        fetch = pltpu.make_async_copy(other_ref.at[slot], other, sem)
        fetch.start()
        factor = jnp.concatenate([b_ref[2 * n], b_ref[2 * n + 1]], axis=1)
        d = d_ref[:, cols]
        g = g_ref[:, cols]
        r = r_ref[:, cols]
        rest = 1.0 - d
        gr = g * r
        for k in range(CHUNKS):
            span_k = slice(k * rows, (k + 1) * rows)
            xrr = x_ref[span_k, cols].astype(f32) * r
            xr[span_k] = xrr[:, :128] + xrr[:, 128:]
        fetch.wait()
        for k in range(CHUNKS):
            span_k = slice(k * rows, (k + 1) * rows)
            so_far = s0[:, span_k] + s1[:, span_k]
            norm = lax.rsqrt(so_far[0:1] / full_width + norm_eps)
            low = (l0[:, span_k] + l1[:, span_k] + norm * so_far) * coef
            spread_low = spread(low, 1, group)
            u = dot(spread_low, factor[k * group : (k + 1) * group], 0, 0) + (
                own_ref[0, span_k].astype(f32)
                + peer_ref[0, span_k].astype(f32)
                + other[span_k].astype(f32)
            )
            h = jnp.zeros((per, 256), f32)
            for t in range(steps):
                span = slice(k * rows + t * per, k * rows + (t + 1) * per)
                h = d * h + rest * u[t * per : (t + 1) * per]
                hr = h * gr
                hh = h * h
                square[span] = hh[:, :128] + hh[:, 128:]
                lr[span] = hr[:, :128] + hr[:, 128:]
            last_ref[k * per : (k + 1) * per] = h * g
        ones = jnp.ones((8, 128), f32)
        sums = [dot(ones, a[...], 1, 1, lax.Precision.HIGHEST) for a in (square, lr, xr)]
        row = lax.broadcasted_iota(jnp.int32, (8, rows * CHUNKS), 0)
        stats_ref[...] = before_ref[...] + jnp.where(
            row == 0, sums[0], jnp.where(row == 1, sums[1], sums[2])
        )

    total = rows * CHUNKS
    return pl.pallas_call(
        kernel,
        out_shape=[
            jax.ShapeDtypeStruct((8, total), f32),
            jax.ShapeDtypeStruct((per * CHUNKS, 256), f32),
        ],
        in_specs=[VMEM] * 7 + [pl.BlockSpec(memory_space=pl.ANY)] + [VMEM] * 5,
        out_specs=[VMEM] * 2,
        scratch_shapes=[pltpu.VMEM((total, 128), f32)] * 3
        + [pltpu.VMEM((total, 256), bf16), pltpu.SemaphoreType.DMA],
        compiler_params=params(16),
        name="second_layer",
        cost_estimate=small_cost,
    )(hidden, *lows, *stats, *halves, crossed, out_factors, decay, gain, reward, before)


def step_kernel(where, arrived, arrived_peer, members, members_all, scale, earlier):
    pops, rows, lanes = arrived.shape
    k = members * 8
    part = k // 2 + 8
    blocks = (rows - 2 * part) // k
    width = blocks * lanes

    def kernel(where_ref, in_ref, peer_ref, _, mine_ref, theirs_ref, paired, digit_rows):
        xl, c = where_ref[4], where_ref[2]
        head = blocks * k
        for p in range(pops):
            digits = in_ref[p, head + k // 2 : head + k // 2 + 8, :].astype(f32)
            for i in range(4):
                digit_rows[i, p : p + 1, :] = digits[i : i + 1, :]
        lane = lax.broadcasted_iota(jnp.int32, (pops, lanes), 1)
        real = lane < members
        here = (digit_rows[0] * 32.0 + digit_rows[1]) / members_all
        there = (digit_rows[2] * 32.0 + digit_rows[3]) / members_all
        mean = (
            jnp.sum(jnp.where(real, here, 0.0), keepdims=True)
            + jnp.sum(jnp.where(real, there, 0.0), keepdims=True)
        ) / members_all
        here = jnp.where(real, here - mean, 0.0)
        there = jnp.where(real, there - mean, 0.0)
        var = (
            jnp.sum(here * here, keepdims=True) + jnp.sum(there * there, keepdims=True)
        ) / members_all
        shaped = here * (lax.rsqrt(var + spread_eps) * scale)
        pick = lax.broadcasted_iota(jnp.int32, (k, lanes), 0) // 8 == lax.broadcasted_iota(
            jnp.int32, (k, lanes), 1
        )
        by_row = dot(pick.astype(f32), shaped, 1, 1, lax.Precision.HIGHEST)
        layer = (lax.broadcasted_iota(jnp.int32, (k, lanes), 0) % 8) // 4
        for p in range(pops):
            at = slice(p * k, (p + 1) * k)
            for rel in range(2):
                lo = pl.multiple_of((xl ^ rel) * part, 8)
                mine = in_ref[p, pl.ds(head + lo, k // 2), :].astype(f32)
                theirs = peer_ref[p, pl.ds(lo, k // 2), :].astype(f32)
                o = jnp.concatenate(
                    [jnp.where(c == 0, mine, theirs), jnp.where(c == 0, theirs, mine)], axis=0
                )
                o = o * by_row[:, p : p + 1]
                for l in range(2):
                    col = (rel * 2 + l) * lanes
                    paired[at, col : col + lanes] = jnp.where(layer == l, o, 0.0).astype(bf16)
        right = paired[...]
        for b in range(0, blocks, 2):
            left = jnp.concatenate(
                [
                    jnp.concatenate(
                        [in_ref[p, b * k : (b + 1) * k, :], in_ref[p, (b + 1) * k : (b + 2) * k, :]],
                        axis=1,
                    )
                    for p in range(pops)
                ],
                axis=0,
            )
            out = dot(left, right, 0, 0)
            span = slice(b * lanes, (b + 2) * lanes)
            for l in range(2):
                mine_ref[l, span, :] = out[:, l * lanes : (l + 1) * lanes]
                theirs_ref[l, span, :] = out[:, (2 + l) * lanes : (3 + l) * lanes].astype(bf16)

    return pl.pallas_call(
        kernel,
        out_shape=[
            jax.ShapeDtypeStruct((2, width, lanes), f32),
            jax.ShapeDtypeStruct((2, width, lanes), bf16),
        ],
        in_specs=[SMEM, VMEM, VMEM, pl.BlockSpec(memory_space=pl.ANY)],
        out_specs=[VMEM, VMEM],
        scratch_shapes=[
            pltpu.VMEM((pops * k, 4 * lanes), bf16),
            pltpu.VMEM((4, pops, lanes), f32),
        ],
        compiler_params=params(24),
        name="weight_step",
        cost_estimate=small_cost,
    )(where, arrived, arrived_peer, earlier)


def shards(
    token_ids,
    fitness_ranks,
    embedding,
    mix_weights,
    factors_in,
    factors_out,
    decay_rates,
    norm_gain,
    reward_dir,
):
    members, seq_count, step_count = token_ids.shape
    vocab, width = embedding.shape
    full_width = mix_weights.shape[2]
    rank_count = factors_in.shape[2]
    pop_count = lax.axis_size(POP)
    members_all = members * pop_count
    coef = noise_scale * (full_width * rank_count) ** (-0.5)
    y, xl, z = (lax.axis_index(a) for a in POP)
    xh, c = (lax.axis_index(a) for a in MP)
    where = jnp.stack([z, xh, c, y, xl]).astype(jnp.int32)
    rows_all = members * seq_count * step_count

    order = token_ids.reshape(CHUNKS, -1, step_count).transpose(0, 2, 1).reshape(-1)
    onehot = (order[:, None] == jnp.arange(vocab, dtype=jnp.int32)[None, :]).astype(bf16)

    def added(a, b):
        return (a.astype(f32) + b.astype(f32)).astype(bf16)

    peer, own = product(0, where, embedding, mix_weights, 512)
    theirs = swap(peer, "c")
    cross = added(own[:2], theirs[:2])
    first_table = (
        own[2:].astype(f32) + theirs[2:].astype(f32) + swap(cross, "xh").astype(f32)
    ).astype(bf16)
    a_blocks = regroup(after(factors_in, peer), jnp.zeros((1,), jnp.int32))
    lows = mp_parts(low_kernel(after(onehot, peer), embedding, a_blocks))
    both = jnp.stack([fitness_ranks, swap(after(fitness_ranks, peer), "xl")])
    digits = jnp.stack([both[0] // 32, both[0] % 32, both[1] // 32, both[1] % 32]).astype(bf16)
    digits = jnp.pad(digits, ((0, 4), (0, 128 - members)))
    pops = lax.axis_size("y") * lax.axis_size("z")
    late_out = after(factors_out, cross)
    b_own = regroup(late_out, ((xh * 2 + c) * width).reshape(1).astype(jnp.int32))
    packed = pack(where, digits, a_blocks, late_out, pops)
    arrived = lax.all_to_all(after(packed, lows[0]), ("y", "z"), 0, 0, tiled=True)

    decay = [decay_rates[l : l + 1] for l in range(2)]
    gain = [norm_gain[l : l + 1] for l in range(2)]
    lifted, stats = [], []
    for k in range(CHUNKS):
        up, st = first_layer(
            k, where, coef, onehot, first_table, lows, b_own, a_blocks, decay[0], gain[0]
        )
        lifted.append(up)
        stats.append(st)
    stats = mp_parts(jnp.concatenate(stats, axis=1))
    late_weights = stay(1, after(mix_weights, stats[0]))
    hidden, last_hidden = next_hidden(full_width, onehot, embedding, stats, lifted)
    sent, parts, place = [], [], []
    for first, count in ((0, 3), (3, 1)):
        peer, own = dense(1, where, hidden, late_weights, 256, first, count, ())
        part = added(own, swap(peer, "c"))
        parts.append(part)
        sent.append(swap(part, "xh"))
        place += [(len(sent) - 1, n) for n in range(count)]
    halves = []
    for n in range(4):
        peer, own = dense(0, where, hidden, late_weights, 256, n, 1, (*parts, *(h[1] for h in halves)))
        halves.append((own, swap(peer, "c")))

    outs_rows = 2 * (members * rank_count + 8)
    tail_rows = after(arrived, halves[3][0])[:, -outs_rows:]
    arrived_peer = swap(tail_rows, "c")
    step_mine, step_theirs = step_kernel(
        where, arrived, arrived_peer, members, members_all,
        (members_all * rank_count) ** (-0.5), halves[3][0],
    )
    st = after(jnp.zeros((8, rows_all), f32), step_theirs)
    lasts = []
    for n in range(4):
        st, last = second_layer(
            n, coef, full_width, hidden, lows, stats, halves[n], sent[place[n][0]], place[n][1], b_own,
            decay[1], gain[1], reward_dir[None], st,
        )
        lasts.append(last)
    weight_step = step_mine + swap(after(step_theirs, sent[-1]), "xl").astype(f32)
    pair, other_pair = mp_parts(st)
    so_far = after(pair + other_pair, weight_step)
    norm = lax.rsqrt(so_far[0] / full_width + norm_eps)
    terms = (so_far[2] + norm * so_far[1]).reshape(CHUNKS, step_count, -1)
    tail = norm.reshape(CHUNKS, step_count, -1)[:, -1].reshape(-1)
    finals = last_hidden + jnp.concatenate(lasts, axis=1) * tail[:, None]
    final_features = finals.astype(bf16).reshape(members, seq_count, width)
    scores = jnp.mean(terms, axis=1).reshape(members, seq_count) * full_width ** (-0.5)
    return (final_features, scores, weight_step)


def solution(mesh):
    fine = Mesh(mesh.devices.reshape(4, 2, 4, 2, 2), POP + MP)
    return jax.shard_map(
        shards,
        mesh=fine,
        in_specs=(
            P(POP, None, None),
            P(POP),
            P(None, MP),
            P(None, MP, None),
            P(None, POP, None, MP),
            P(None, POP, None, None),
            P(None, MP),
            P(None, MP),
            P(MP),
        ),
        out_specs=(P(POP, None, MP), P(POP, None), P(None, MP, POP)),
        check_vma=False,
    )
```
